32 devices in a mesh: dp: 16 (over z, y, core), tensor: 2 (over x).
Axes of the slice: x: 2, y: 2, z: 4, core: 2. Of those that a mesh axis runs over, the one named last changes fastest.
Arguments:
- tokens: bfloat16 [32768, 768], P(('dp', 'tensor')), may hold values from -6 to 6
- memory: bfloat16 [16, 1500, 768], P('dp'), may hold values from -6 to 6
- seg_ids: int32 [32768], P(('dp', 'tensor')), may hold values from 0 to 4, as said below
- positions: int32 [32768], P(('dp', 'tensor')), may hold values from 0 to 1535, as said below
- grad_output: bfloat16 [32768, 768], P(('dp', 'tensor')), may hold values from -6 to 6
- attn_in: bfloat16 [768, 3, 768], P('dp', None, 'tensor'), may hold values from -0.21875 to 0.21875
- attn_out: bfloat16 [768, 768], P('tensor', 'dp'), may hold values from -2.5 to 2.5
- cross_q: bfloat16 [768, 768], P('dp', 'tensor'), may hold values from -0.21875 to 0.21875
- cross_kv: bfloat16 [768, 2, 768], P('dp', None, 'tensor'), may hold values from -0.21875 to 0.21875
- cross_out: bfloat16 [768, 768], P('tensor', 'dp'), may hold values from -2.5 to 2.5
- mlp_in: bfloat16 [768, 3072], P('dp', 'tensor'), may hold values from -0.21875 to 0.21875
- mlp_out: bfloat16 [3072, 768], P('tensor', 'dp'), may hold values from -0.109375 to 0.109375
- norm_gain: float32 [3, 768], replicated, may hold values from 0.5 to 1.5
- norm_bias: float32 [3, 768], replicated, may hold values from -1 to 1
- proj_bias: float32 [6, 768], replicated, may hold values from -0.5 to 0.5
- mlp_bias: float32 [3072], replicated, may hold values from -1 to 1
- out_bias: float32 [768], replicated, may hold values from -2.5 to 2.5
Outputs:
- output: bfloat16 [32768, 768], P(('dp', 'tensor'))
- grad_tokens: float32 [32768, 768], P(('dp', 'tensor'))
- grad_attn_in: float32 [768, 3, 768], P('dp', None, 'tensor')
- grad_attn_out: float32 [768, 768], P('tensor', 'dp')
- grad_cross_q: float32 [768, 768], P('dp', 'tensor')
- grad_cross_kv: float32 [768, 2, 768], P('dp', None, 'tensor')
- grad_cross_out: float32 [768, 768], P('tensor', 'dp')
- grad_mlp_in: float32 [768, 3072], P('dp', 'tensor')
- grad_mlp_out: float32 [3072, 768], P('tensor', 'dp')
- grad_norm_gain: float32 [3, 768], replicated
- grad_norm_bias: float32 [3, 768], replicated
- grad_proj_bias: float32 [6, 768], replicated
- grad_mlp_bias: float32 [3072], replicated
- grad_out_bias: float32 [768], replicated
The draws below stay inside these ranges and needn't reach their ends.
Inputs may be any that keep to these rules, and one draw needn't show every extreme that they name: `seg_ids`: within each group of 2048 consecutive tokens, the first 1024 are 0 (the prompt); the rest are 4 runs numbered 1 to 4 in order, each of 1 to 512 tokens, one of exactly 512 tokens. Prompt tokens have positions 0, 1, ... in order; each continuation's tokens have positions 1024, 1025, ... in order.
All inputs are finite; a program needn't handle non-finite values.
Results may differ from the reference program's by a relative error of at most 0.029.
Values may be sent and summed in bfloat16 or wider, within the bound.
A program may use at most 256 MiB of HBM per device.

```python
import jax
import jax.numpy as jnp
from jax import lax

D = 768
HEADS = 12
HEAD = 64
FF = 3072
FRAMES = 1500
PROMPT = 1024
NCONT = 4
MOST_LEN = 512
CONT_TOK = 1024
GROUP_TOK = 2048
GROUPS = 16
TOKENS = 32768


def group_layout(key):
    group_keys = jax.random.split(jax.random.fold_in(key, 11), GROUPS)

    def one_group(sub_key):
        cut_key, order_key = jax.random.split(sub_key)
        remain = CONT_TOK - MOST_LEN
        cut_points = jnp.sort(jax.random.permutation(cut_key, remain - 1)[:NCONT - 2].astype(jnp.int32) + 1)
        bounds = jnp.concatenate([jnp.zeros((1,), jnp.int32), cut_points, jnp.full((1,), remain, jnp.int32)])
        lengths = jnp.concatenate([jnp.full((1,), MOST_LEN, jnp.int32), bounds[1:] - bounds[:-1]])
        lengths = lengths[jax.random.permutation(order_key, NCONT)]
        end_marks = jnp.cumsum(lengths).astype(jnp.int32)
        starts = end_marks - lengths
        places = jnp.arange(CONT_TOK, dtype=jnp.int32)
        segment_of = jnp.sum((places[:, None] >= end_marks[None, :]).astype(jnp.int32), axis=1)
        within = places - starts[segment_of]
        seg_rows = jnp.concatenate([jnp.zeros((PROMPT,), jnp.int32), segment_of + 1])
        pos_rows = jnp.concatenate([jnp.arange(PROMPT, dtype=jnp.int32), PROMPT + within])
        return (seg_rows, pos_rows)
    seg_all, pos_all = jax.vmap(one_group)(group_keys)
    return (seg_all.reshape(-1), pos_all.reshape(-1))


def draw_seg_ids(key, part):
    return group_layout(key)[0]


def draw_positions(key, part):
    return group_layout(key)[1]


def with_spikes(values, key, source, target, shards_of, factor):
    owner, partner = [(jnp.arange(values.shape[dim]) // (values.shape[dim] // shards_of)).reshape([-1 if axis == dim else 1 for axis in range(values.ndim)]) for dim in (source, target)]
    chosen = jax.random.permutation(key, shards_of)[partner]
    strong = (owner == chosen) | (owner == (partner + shards_of // 2) % shards_of)
    return jnp.where(strong, factor * values, values)


def shard_levels(key, shape, cuts, least, largest):
    gain = 1.0
    for axis_at, parts in cuts:
        heights = jax.random.uniform(jax.random.fold_in(jax.random.fold_in(key, 6), axis_at), (parts,), jnp.float32, least / len(cuts), largest / len(cuts))
        gain = gain * jnp.repeat(jnp.exp(heights), shape[axis_at] // parts).reshape((-1,) + (1,) * (len(shape) - 1 - axis_at))
    return gain


def gaussian(key, extent, scale, reach, cuts=(), held_as=jnp.bfloat16):
    array = jax.random.normal(key, extent, jnp.float32) * scale
    if len(cuts) > 0:
        array = shard_levels(key, extent, cuts, -0.22, 0.18) * array
    return jnp.clip(array, min=-reach, max=reach).astype(held_as)


def bell_draw_with(own_key, shape, scale, bound, cuts, heavy, held_as=jnp.bfloat16):
    values = scale * jax.random.normal(own_key, shape, jnp.float32)
    if cuts:
        values = values * shard_levels(own_key, shape, cuts, -0.22, 0.18)
    return jnp.clip(with_spikes(values, jax.random.fold_in(own_key, 3), *heavy), -bound, bound).astype(held_as)


def setup_inputs(seed: int = 0) -> dict:
    arg_keys = jax.random.split(jax.random.key(seed), 18)
    tokens = gaussian(arg_keys[0], (TOKENS, D), 1.0, 6.0, ((0, 32),))
    memory = gaussian(arg_keys[1], (GROUPS, FRAMES, D), 1.0, 6.0, ((0, 16),))
    seg_ids = draw_seg_ids(jax.random.fold_in(arg_keys[17], 71), 0)
    positions = draw_positions(jax.random.fold_in(arg_keys[17], 71), 0)
    grad_output = bell_draw_with(arg_keys[4], (TOKENS, D), 1.0, 6.0, ((0, 32),), (0, 1, 32, 2.75))
    attn_in = gaussian(arg_keys[5], (D, 3, D), D ** -0.5, 0.21875, ((0, 16), (2, 2)))
    attn_out = gaussian(arg_keys[6], (D, D), (D // 128) ** -0.5, 2.5, ((0, 2), (1, 16)))
    cross_q = gaussian(arg_keys[7], (D, D), D ** -0.5, 0.21875, ((0, 16), (1, 2)))
    cross_kv = gaussian(arg_keys[8], (D, 2, D), D ** -0.5, 0.21875, ((0, 16), (2, 2)))
    cross_out = gaussian(arg_keys[9], (D, D), (D // 128) ** -0.5, 2.5, ((0, 2), (1, 16)))
    mlp_in = gaussian(arg_keys[10], (D, FF), D ** -0.5, 0.21875, ((0, 16), (1, 2)))
    mlp_out = gaussian(arg_keys[11], (FF, D), FF ** -0.5, 0.109375, ((0, 2), (1, 16)))
    norm_gain = jnp.clip(1.0 + 0.1 * jax.random.normal(arg_keys[12], (3, D), jnp.float32), 0.5, 1.5)
    norm_bias = gaussian(arg_keys[13], (3, D), 0.2, 1.0, (), jnp.float32)
    proj_bias = gaussian(arg_keys[14], (6, D), 0.1, 0.5, (), jnp.float32)
    mlp_bias = gaussian(arg_keys[15], (FF,), 0.2, 1.0, (), jnp.float32)
    out_bias = gaussian(arg_keys[16], (D,), 0.5, 2.5, (), jnp.float32)
    return {"tokens": tokens, "memory": memory, "seg_ids": seg_ids, "positions": positions, "grad_output": grad_output, "attn_in": attn_in, "attn_out": attn_out, "cross_q": cross_q, "cross_kv": cross_kv, "cross_out": cross_out, "mlp_in": mlp_in, "mlp_out": mlp_out, "norm_gain": norm_gain, "norm_bias": norm_bias, "proj_bias": proj_bias, "mlp_bias": mlp_bias, "out_bias": out_bias}


@jax.custom_vjp
def low(v):
    return lax.optimization_barrier(v.astype(jnp.bfloat16)).astype(jnp.float32)

@jax.custom_vjp
def low_back(v):
    return v

def low_keep(v):
    return (low(v), None)

def low_pass(kept, grad):
    return (grad,)

def back_keep(v):
    return (v, None)

def back_low(kept, grad):
    return (low(grad),)
low.defvjp(low_keep, low_pass)
low_back.defvjp(back_keep, back_low)
EPSILON = 1e-05
NEG_LARGE = -1e+30
PRECISE = lax.Precision.HIGHEST

def matmul(left, right):
    return jnp.dot(left, right, precision=PRECISE)

def layer_norm(values, gain_row, offset_row):
    centre = values - lax.optimization_barrier(jnp.mean(values, -1, keepdims=True))
    spread = lax.optimization_barrier(jnp.mean(centre * centre, -1, keepdims=True))
    return centre * lax.rsqrt(spread + EPSILON) * gain_row + offset_row

def attend(queries, key_rows, values, allowed):
    scores = low_back(jnp.einsum('qhd,khd->hqk', queries, key_rows, precision=PRECISE))
    if allowed is not None:
        scores = jnp.where(allowed[None], scores, NEG_LARGE)
    row_peak = lax.optimization_barrier(jnp.max(scores, -1, keepdims=True))
    exp_scores = jnp.exp(scores - row_peak)
    attn_probs = low(exp_scores / lax.optimization_barrier(jnp.sum(exp_scores, -1, keepdims=True)))
    return jnp.einsum('hqk,khd->qhd', attn_probs, values, precision=PRECISE)

def group_layer(rows, mem_rows, seg_rows, pos_rows, weights):
    attn_in, attn_out, cross_q, cross_kv, cross_out, mlp_in, mlp_out, norm_gain, norm_bias, proj_bias, mlp_bias, out_bias = weights
    q_scale = HEAD ** (-0.5)
    group_rows = rows.shape[0]
    frame_rows = mem_rows.shape[0]
    norm_one = low(layer_norm(rows, norm_gain[0], norm_bias[0]))
    qkv_cols = matmul(norm_one, attn_in.reshape(D, 3 * D))
    q_self = low(low_back((qkv_cols[:, :D] + proj_bias[0]) * q_scale)).reshape(group_rows, HEADS, HEAD)
    k_self = low(low_back(qkv_cols[:, D:2 * D])).reshape(group_rows, HEADS, HEAD)
    v_self = low(low_back(qkv_cols[:, 2 * D:] + proj_bias[1])).reshape(group_rows, HEADS, HEAD)
    allowed = (pos_rows[None, :] <= pos_rows[:, None]) & ((seg_rows[None, :] == 0) | (seg_rows[None, :] == seg_rows[:, None]))
    attn_self = low(low_back(attend(q_self, k_self, v_self, allowed).reshape(group_rows, D)))
    resid_one = rows + low_back(matmul(attn_self, attn_out) + proj_bias[2])
    norm_two = low(layer_norm(resid_one, norm_gain[1], norm_bias[1]))
    q_cross = low(low_back((matmul(norm_two, cross_q) + proj_bias[3]) * q_scale)).reshape(group_rows, HEADS, HEAD)
    kv_cols = matmul(mem_rows, cross_kv.reshape(D, 2 * D))
    k_cross = low(low_back(kv_cols[:, :D])).reshape(frame_rows, HEADS, HEAD)
    v_cross = low(low_back(kv_cols[:, D:] + proj_bias[4])).reshape(frame_rows, HEADS, HEAD)
    attn_cross = low(low_back(attend(q_cross, k_cross, v_cross, None).reshape(group_rows, D)))
    resid_two = resid_one + low_back(matmul(attn_cross, cross_out) + proj_bias[5])
    norm_three = low(layer_norm(resid_two, norm_gain[2], norm_bias[2]))
    pre_act = low_back(matmul(norm_three, mlp_in) + mlp_bias)
    hidden = low(jax.nn.gelu(pre_act, approximate=False))
    return resid_two + low_back(matmul(hidden, mlp_out) + out_bias)

def reference(tokens, memory, seg_ids, positions, grad_output, attn_in, attn_out, cross_q, cross_kv, cross_out, mlp_in, mlp_out, norm_gain, norm_bias, proj_bias, mlp_bias, out_bias):
    weights = (attn_in.astype(jnp.float32), attn_out.astype(jnp.float32), cross_q.astype(jnp.float32), cross_kv.astype(jnp.float32), cross_out.astype(jnp.float32), mlp_in.astype(jnp.float32), mlp_out.astype(jnp.float32), norm_gain.astype(jnp.float32), norm_bias.astype(jnp.float32), proj_bias.astype(jnp.float32), mlp_bias.astype(jnp.float32), out_bias.astype(jnp.float32))
    mem_all = memory.astype(jnp.float32)
    seg_all = seg_ids.reshape(GROUPS, GROUP_TOK)
    pos_all = positions.reshape(GROUPS, GROUP_TOK)

    def forward(token_rows, weight_set):

        def one_group(pieces):
            return group_layer(pieces[0], pieces[1], pieces[2], pieces[3], weight_set)
        group_outs = lax.map(jax.checkpoint(one_group), (token_rows.reshape(GROUPS, GROUP_TOK, D), mem_all, seg_all, pos_all))
        return group_outs.reshape(GROUPS * GROUP_TOK, D)
    result, pull = jax.vjp(forward, tokens.astype(jnp.float32), weights)
    grad_tokens, grad_weights = pull(grad_output.astype(jnp.float32))
    return (result.astype(jnp.bfloat16), grad_tokens, grad_weights[0], grad_weights[1], grad_weights[2], grad_weights[3], grad_weights[4], grad_weights[5], grad_weights[6], grad_weights[7], grad_weights[8], grad_weights[9], grad_weights[10], grad_weights[11])
```

```python
import functools, jax, jax.numpy as jnp
from jax import lax
from jax.experimental import pallas as pl
from jax.experimental.pallas import tpu as pltpu
from jax.sharding import Mesh
from jax.sharding import PartitionSpec as P
HEAD=64
BLK=256
LANES=128
NEG=-1e30
LOG2E=1.4426950408889634
F32=jnp.float32; BF=jnp.bfloat16

def lane_ids(rows): return lax.broadcasted_iota(jnp.int32,(rows,LANES),1)

def nt(a,b): return lax.dot_general(a,b,(((1,),(1,)),((),())),preferred_element_type=F32)
def nn(a,b): return lax.dot_general(a,b,(((1,),(0,)),((),())),preferred_element_type=F32)
def tn(a,b): return lax.dot_general(a,b,(((0,),(0,)),((),())),preferred_element_type=F32)

def pick(head, lanes): return (lanes<64) if head==0 else (lanes>=64)

def self_fwd_kernel(q_ref,k_ref,v_ref,segq_ref,segk_ref,o_ref,lse_ref,vx_ref):
    rows=q_ref.shape[0]; half=rows//2; n=rows//BLK
    vx_ref[:,:LANES]=v_ref[...]
    vx_ref[:,LANES:]=jnp.ones((rows,LANES),BF)
    lanes=lane_ids(BLK)
    for i in range(n):
        r0=i*BLK; kn=r0+BLK
        q=q_ref[r0:kn,:]
        outs=[];lses=[]
        for h in range(2):
            qm=jnp.where(pick(h,lanes),q,jnp.zeros_like(q))
            s=nt(qm,k_ref[:kn,:])
            cut = half if i>=n//2 else r0
            a=s[:,:cut] if cut>0 else None
            b=s[:,cut:]
            w=kn-cut
            qi=lax.broadcasted_iota(jnp.int32,(BLK,w),0)+(r0-cut)
            kj=lax.broadcasted_iota(jnp.int32,(BLK,w),1)
            ok=kj<=qi
            if i>=n//2:
                ok=ok&(segk_ref[:,r0-half-(r0-cut):kn-half]==segq_ref[r0-half:kn-half,:])
            b=jnp.where(ok,b,NEG)
            m=jnp.max(b,-1,keepdims=True)
            if a is not None: m=jnp.maximum(m,jnp.max(a,-1,keepdims=True))
            pb=jnp.exp2(b-m).astype(BF)
            ox=nn(pb,vx_ref[cut:kn,:])
            if a is not None:
                pa=jnp.exp2(a-m).astype(BF)
                ox=ox+nn(pa,vx_ref[:cut,:])
            l=ox[:,LANES:]
            outs.append(ox[:,:LANES]/l); lses.append(m+jnp.log2(l))
        sel=lanes<64
        o_ref[r0:kn,:]=jnp.where(sel,outs[0],outs[1]).astype(BF)
        lse_ref[r0:kn,:]=jnp.where(sel,lses[0],lses[1])

def self_fwd(qkv,segq,segk,heads):
    rows=qkv.shape[0]; npair=heads//2
    return pl.pallas_call(self_fwd_kernel,
        grid=(npair,),
        in_specs=[pl.BlockSpec((rows,LANES),lambda p:(0,p)),
                  pl.BlockSpec((rows,LANES),lambda p:(0,npair+p)),
                  pl.BlockSpec((rows,LANES),lambda p:(0,2*npair+p)),
                  pl.BlockSpec(segq.shape,lambda p:(0,0)),pl.BlockSpec(segk.shape,lambda p:(0,0))],
        out_specs=[pl.BlockSpec((rows,LANES),lambda p:(0,p)),pl.BlockSpec((rows,LANES),lambda p:(0,p))],
        out_shape=[jax.ShapeDtypeStruct((rows,heads*64),BF),jax.ShapeDtypeStruct((rows,heads*64),F32)],
        scratch_shapes=[pltpu.VMEM((rows,2*LANES),BF)],
        compiler_params=pltpu.CompilerParams(vmem_limit_bytes=60*2**20),
        name="self_fwd",
    )(qkv,qkv,qkv,segq,segk)

def cross_fwd_kernel(frames,q_ref,k_ref,v_ref,o_ref,lse_ref,kx_ref,vx_ref):
    rows=q_ref.shape[0]; n=rows//BLK; kp=k_ref.shape[0]
    tail=frames//BLK*BLK
    kx_ref[...]=k_ref[...]
    vx_ref[:,:LANES]=v_ref[...]
    vx_ref[:,LANES:]=jnp.ones((kp,LANES),BF)
    if frames<kp:
        keep=lax.broadcasted_iota(jnp.int32,(kp-tail,LANES),0)+tail<frames
        kx_ref[tail:,:]=jnp.where(keep,k_ref[tail:,:],jnp.zeros((),BF))
        vx_ref[tail:,:LANES]=jnp.where(keep,v_ref[tail:,:],jnp.zeros((),BF))
    lanes=lane_ids(BLK)
    for i in range(n):
        r0=i*BLK
        q=q_ref[r0:r0+BLK,:]
        outs=[];lses=[]
        for h in range(2):
            qm=jnp.where(pick(h,lanes),q,jnp.zeros_like(q))
            s=nt(qm,kx_ref[...])
            if frames<kp:
                kj=lax.broadcasted_iota(jnp.int32,(BLK,kp-tail),1)+tail
                s=jnp.concatenate([s[:,:tail],jnp.where(kj<frames,s[:,tail:],NEG)],axis=1)
            m=jnp.max(s,-1,keepdims=True)
            p=jnp.exp2(s-m).astype(BF)
            ox=nn(p,vx_ref[...])
            l=ox[:,LANES:]
            outs.append(ox[:,:LANES]/l); lses.append(m+jnp.log2(l))
        sel=lanes<64
        o_ref[r0:r0+BLK,:]=jnp.where(sel,outs[0],outs[1]).astype(BF)
        lse_ref[r0:r0+BLK,:]=jnp.where(sel,lses[0],lses[1])

def cross_fwd(q,kv,heads):
    rows=q.shape[0]; npair=heads//2; frames=kv.shape[0]
    kp=(frames+BLK-1)//BLK*BLK
    return pl.pallas_call(functools.partial(cross_fwd_kernel,frames),
        grid=(npair,),
        in_specs=[pl.BlockSpec((rows,LANES),lambda p:(0,p)),
                  pl.BlockSpec((kp,LANES),lambda p:(0,p)),
                  pl.BlockSpec((kp,LANES),lambda p:(0,npair+p))],
        out_specs=[pl.BlockSpec((rows,LANES),lambda p:(0,p)),pl.BlockSpec((rows,LANES),lambda p:(0,p))],
        out_shape=[jax.ShapeDtypeStruct((rows,heads*64),BF),jax.ShapeDtypeStruct((rows,heads*64),F32)],
        scratch_shapes=[pltpu.VMEM((kp,LANES),BF),pltpu.VMEM((kp,2*LANES),BF)],
        compiler_params=pltpu.CompilerParams(vmem_limit_bytes=60*2**20),
        name="cross_fwd",
    )(q,kv,kv)

def split3(x):
    hi=x.astype(BF); r=x-hi.astype(F32); mid=r.astype(BF); lo=(r-mid.astype(F32)).astype(BF)
    return hi,mid,lo

def aug(value,head,lanes,one_lane):
    hi,mid,lo=split3(-value)
    z=jnp.zeros(lanes.shape,F32)
    b=64*head
    x=jnp.where(lanes==b,hi.astype(F32),jnp.where(lanes==b+1,mid.astype(F32),jnp.where(lanes==b+2,lo.astype(F32),z)))
    if one_lane: x=jnp.where(lanes==b+3,1.0,x)
    return x.astype(BF)

def build_q(q_ref,do_ref,o_ref,lse_ref,qx_ref,dox_ref,masked):
    rows=q_ref.shape[0]
    lanes=lane_ids(BLK)
    for r0 in range(0,rows,BLK):
        r1=r0+BLK
        q=q_ref[r0:r1,:]; do=do_ref[r0:r1,:]; lse=lse_ref[r0:r1,:]
        prod=do.astype(F32)*o_ref[r0:r1,:].astype(F32)
        for h in range(2):
            sel=pick(h,lanes)
            delta=jnp.sum(jnp.where(sel,prod,0.0),-1,keepdims=True)
            qx_ref[h,r0:r1,:LANES]=jnp.where(sel,q,jnp.zeros((),BF))
            qx_ref[h,r0:r1,LANES:]=aug(lse,h,lanes,masked)
            dox_ref[h,r0:r1,:LANES]=jnp.where(sel,do,jnp.zeros((),BF))
            dox_ref[h,r0:r1,LANES:]=aug(delta,h,lanes,False)

def build_k(k_ref,v_ref,kx_ref,km_ref,vx_ref,frames):
    rows=k_ref.shape[0]
    lanes=lane_ids(BLK)
    low=lanes%64
    for r0 in range(0,rows,BLK):
        r1=r0+BLK
        k=k_ref[r0:r1,:]; v=v_ref[r0:r1,:]
        ones=jnp.where(low<3,1.0,0.0)
        if frames is not None:
            kones=jnp.where(low==3,0.0,ones)
            if r1>frames:
                bad=lax.broadcasted_iota(jnp.int32,(BLK,LANES),0)+r0>=frames
                k=jnp.where(bad,jnp.zeros((),BF),k); v=jnp.where(bad,jnp.zeros((),BF),v)
                kones=jnp.where(bad&(low==3),NEG,ones)
        else: kones=ones
        kx_ref[r0:r1,:LANES]=k; kx_ref[r0:r1,LANES:]=kones.astype(BF)
        vx_ref[r0:r1,:LANES]=v; vx_ref[r0:r1,LANES:]=ones.astype(BF)
        for h in range(2): km_ref[h,r0:r1,:]=jnp.where(pick(h,lanes),k,jnp.zeros((),BF))

def block_back(kx,vx,km,qx,dox,mask):
    s=nt(kx,qx)
    if mask is not None: s=jnp.where(mask,s,NEG)
    p=jnp.exp2(s)
    dp=nt(vx,dox)
    ds=(p*dp).astype(BF)
    pb=p.astype(BF)
    dv=nn(pb,dox[:,:LANES])
    dk=nn(ds,qx[:,:LANES])
    dq=tn(ds,km)
    return dv,dk,dq

def self_bwd_kernel(q_ref,k_ref,v_ref,do_ref,o_ref,lse_ref,segq_ref,segk_ref,dq_ref,dk_ref,dv_ref,
                    qx_ref,dox_ref,kx_ref,km_ref,vx_ref,dqa_ref,dka_ref,dva_ref):
    rows=q_ref.shape[0]; n=rows//BLK; half=rows//2
    build_q(q_ref,do_ref,o_ref,lse_ref,qx_ref,dox_ref,False)
    build_k(k_ref,v_ref,kx_ref,km_ref,vx_ref,None)
    dqa_ref[...]=jnp.zeros_like(dqa_ref)
    tri=lax.broadcasted_iota(jnp.int32,(BLK,BLK),0)<=lax.broadcasted_iota(jnp.int32,(BLK,BLK),1)
    def pair(j,i,mask,first):
        kr=pl.ds(pl.multiple_of(j*BLK,BLK),BLK); qr=pl.ds(pl.multiple_of(i*BLK,BLK),BLK)
        r=[block_back(kx_ref[kr,:],vx_ref[kr,:],km_ref[h,kr,:],qx_ref[h,qr,:],dox_ref[h,qr,:],mask) for h in range(2)]
        dv=r[0][0]+r[1][0]; dk=r[0][1]+r[1][1]; dq=r[0][2]+r[1][2]
        if first: dva_ref[...]=dv; dka_ref[...]=dk
        else: dva_ref[...]+=dv; dka_ref[...]+=dk
        dqa_ref[qr,:]+=dq
    def flush(j):
        kr=pl.ds(pl.multiple_of(j*BLK,BLK),BLK)
        dk_ref[kr,:]=(dka_ref[...]*(1/LOG2E)).astype(BF)
        dv_ref[kr,:]=dva_ref[...].astype(BF)
    def outer_prompt(j,_):
        pair(j,j,tri,True)
        def inner(i,_): pair(j,i,None,False); return 0
        lax.fori_loop(j+1,n,inner,0)
        flush(j); return 0
    lax.fori_loop(0,n//2,outer_prompt,0)
    def segmask(j,i):
        sk=segk_ref[pl.ds(pl.multiple_of(j*BLK-half,BLK),BLK),:]
        sq=segq_ref[i-n//2]
        return sk==sq
    def outer_cont(j,_):
        pair(j,j,tri&segmask(j,j),True)
        def inner(i,_): pair(j,i,segmask(j,i),False); return 0
        lax.fori_loop(j+1,n,inner,0)
        flush(j); return 0
    lax.fori_loop(n//2,n,outer_cont,0)
    dq_ref[...]=(dqa_ref[...]*0.125).astype(BF)

def self_bwd(qkv,do,o,lse,segq,segk,heads):
    rows=qkv.shape[0]; npair=heads//2
    big=lambda f:pl.BlockSpec((rows,LANES),f)
    out=jax.ShapeDtypeStruct((rows,heads*64),BF)
    return pl.pallas_call(self_bwd_kernel,
        grid=(npair,),
        in_specs=[big(lambda p:(0,p)),big(lambda p:(0,npair+p)),big(lambda p:(0,2*npair+p)),big(lambda p:(0,p)),big(lambda p:(0,p)),big(lambda p:(0,p)),
                  pl.BlockSpec(segq.shape,lambda p:(0,0,0)),pl.BlockSpec(segk.shape,lambda p:(0,0))],
        out_specs=[big(lambda p:(0,p))]*3,
        out_shape=[out]*3,
        scratch_shapes=[pltpu.VMEM((2,rows,2*LANES),BF),pltpu.VMEM((2,rows,2*LANES),BF),pltpu.VMEM((rows,2*LANES),BF),
                        pltpu.VMEM((2,rows,LANES),BF),pltpu.VMEM((rows,2*LANES),BF),pltpu.VMEM((rows,LANES),F32),
                        pltpu.VMEM((BLK,LANES),F32),pltpu.VMEM((BLK,LANES),F32)],
        compiler_params=pltpu.CompilerParams(vmem_limit_bytes=60*2**20),
        name="self_bwd",
    )(qkv,qkv,qkv,do,o,lse,segq,segk)

def cross_bwd_kernel(frames,q_ref,k_ref,v_ref,do_ref,o_ref,lse_ref,dq_ref,dk_ref,dv_ref,
                     qx_ref,dox_ref,kx_ref,km_ref,vx_ref,dqa_ref,dka_ref,dva_ref):
    rows=q_ref.shape[0]; n=rows//BLK; kp=k_ref.shape[0]; nk=kp//BLK
    build_q(q_ref,do_ref,o_ref,lse_ref,qx_ref,dox_ref,True)
    build_k(k_ref,v_ref,kx_ref,km_ref,vx_ref,frames)
    dqa_ref[...]=jnp.zeros_like(dqa_ref)
    def outer(j,_):
        kr=pl.ds(pl.multiple_of(j*BLK,BLK),BLK)
        dva=None
        for i in range(n):
            qr=slice(i*BLK,(i+1)*BLK)
            r=[block_back(kx_ref[kr,:],vx_ref[kr,:],km_ref[h,kr,:],qx_ref[h,qr,:],dox_ref[h,qr,:],None) for h in range(2)]
            dv=r[0][0]+r[1][0]; dk=r[0][1]+r[1][1]; dq=r[0][2]+r[1][2]
            if i==0: dva_ref[...]=dv; dka_ref[...]=dk
            else: dva_ref[...]+=dv; dka_ref[...]+=dk
            dqa_ref[qr,:]+=dq
        dk_ref[kr,:]=(dka_ref[...]*(1/LOG2E)).astype(BF)
        dv_ref[kr,:]=dva_ref[...].astype(BF)
        return 0
    lax.fori_loop(0,nk,outer,0)
    dq_ref[...]=(dqa_ref[...]*0.125).astype(BF)

def cross_bwd(q,kv,do,o,lse,heads):
    rows=q.shape[0]; npair=heads//2; frames=kv.shape[0]
    kp=(frames+BLK-1)//BLK*BLK
    big=lambda f:pl.BlockSpec((rows,LANES),f)
    kb=lambda f:pl.BlockSpec((kp,LANES),f)
    return pl.pallas_call(functools.partial(cross_bwd_kernel,frames),
        grid=(npair,),
        in_specs=[big(lambda p:(0,p)),kb(lambda p:(0,p)),kb(lambda p:(0,npair+p)),big(lambda p:(0,p)),big(lambda p:(0,p)),big(lambda p:(0,p))],
        out_specs=[big(lambda p:(0,p)),kb(lambda p:(0,p)),kb(lambda p:(0,p))],
        out_shape=[jax.ShapeDtypeStruct((rows,heads*64),BF),jax.ShapeDtypeStruct((frames,heads*64),BF),jax.ShapeDtypeStruct((frames,heads*64),BF)],
        scratch_shapes=[pltpu.VMEM((2,rows,2*LANES),BF),pltpu.VMEM((2,rows,2*LANES),BF),pltpu.VMEM((kp,2*LANES),BF),
                        pltpu.VMEM((2,kp,LANES),BF),pltpu.VMEM((kp,2*LANES),BF),pltpu.VMEM((rows,LANES),F32),
                        pltpu.VMEM((BLK,LANES),F32),pltpu.VMEM((BLK,LANES),F32)],
        compiler_params=pltpu.CompilerParams(vmem_limit_bytes=60*2**20),
        name="cross_bwd",
    )(q,kv,kv,do,o,lse)


EPSILON = 1e-05


def layer_norm(values, gain_row, offset_row):
    centre = values - jnp.mean(values, -1, keepdims=True)
    spread = jnp.mean(centre * centre, -1, keepdims=True)
    return centre * lax.rsqrt(spread + EPSILON) * gain_row + offset_row


def exact_gelu(values):
    return jax.nn.gelu(values, approximate=False)


ALL = ("chip", "core", "tensor")


def fetch(shard):
    rows, cols = shard.shape
    full = lax.all_gather(shard, ALL, axis=0, tiled=False)
    return full.reshape(-1, 2, rows, cols).transpose(0, 2, 1, 3).reshape(-1, 2, cols)


def spread_sum(grad):
    rows, _, cols = grad.shape
    here = rows // (lax.axis_size("chip") * 2)
    blocks = grad.astype(BF).reshape(-1, here, 2, cols).transpose(0, 2, 1, 3).reshape(-1, cols)
    return lax.psum_scatter(blocks, ALL, scatter_dimension=0, tiled=True).astype(F32)


def on_device(tokens, memory, seg_ids, positions, grad_output, attn_in, attn_out, cross_q, cross_kv,
              cross_out, mlp_in, mlp_out, norm_gain, norm_bias, proj_bias, mlp_bias, out_bias):
    width = tokens.shape[1]
    part = attn_in.shape[2]
    units = mlp_in.shape[1]
    heads = width // HEAD
    core = lax.axis_index("core")
    tensor = lax.axis_index("tensor")
    swap = [(0, 0), (1, 2), (2, 1), (3, 3)]
    fix = lambda x: lax.ppermute(x, ("core", "tensor"), swap)
    other = lambda x: lax.ppermute(x, "core", [(0, 1), (1, 0)])

    def norm_back(resid_in, index_row, grad_norm):
        _, pull = jax.vjp(layer_norm, resid_in, norm_gain[index_row], norm_bias[index_row])
        return pull(grad_norm)

    rows_here = attn_in.shape[0]
    w_a = fetch(attn_in.reshape(rows_here, 3 * part))
    w_b = fetch(jnp.concatenate([attn_out.T, cross_q, cross_kv.reshape(rows_here, 2 * part), cross_out.T], 1))
    w_c = fetch(jnp.concatenate([mlp_in, mlp_out.T], 1))
    w_qkv = w_a.reshape(width, 2 * 3 * part)
    wt_attn_out = w_b[:, :, :part].reshape(width, width)
    w_cross_q = w_b[:, :, part:2 * part].reshape(width, width)
    w_cross_kv = w_b[:, :, 2 * part:4 * part].reshape(width, 2, 2, part).transpose(0, 2, 1, 3).reshape(width, 2 * width)
    wt_cross_out = w_b[:, :, 4 * part:].reshape(width, width)
    w_mlp_in = w_c[:, :, :units].reshape(width, 2 * units)
    wt_mlp_out = w_c[:, :, units:].reshape(width, 2 * units)

    rows = tokens.shape[0]
    moved = fix(tokens)
    grad_in = fix(grad_output)
    seg_mine = fix(seg_ids)
    seg_cont = jnp.where(core == 1, seg_mine, other(seg_mine))
    mem = memory[0]
    mem = jnp.where(core == tensor, mem, other(mem))

    resid_zero = moved.astype(F32)
    norm_one = layer_norm(resid_zero, norm_gain[0], norm_bias[0]).astype(BF)
    qkv = jnp.dot(norm_one, w_qkv, preferred_element_type=F32).reshape(rows, 2, 3, part)
    add = jnp.stack([proj_bias[0].reshape(2, part), jnp.zeros((2, part), F32), proj_bias[1].reshape(2, part)], 1)
    scale = jnp.array([HEAD ** -0.5 * LOG2E, 1.0, 1.0], F32)[None, :, None]
    qkv = ((qkv + add) * scale).astype(BF).reshape(rows, 2, 3 * part)

    def to_heads(x):
        kept = jnp.where(core == 0, x[:, 0], x[:, 1])
        come = other(jnp.where(core == 0, x[:, 1], x[:, 0]))
        return jnp.concatenate([jnp.where(core == 0, kept, come), jnp.where(core == 0, come, kept)], 0)

    def to_tokens(x):
        kept = jnp.where(core == 0, x[:rows], x[rows:])
        come = other(jnp.where(core == 0, x[rows:], x[:rows]))
        return jnp.stack([jnp.where(core == 0, kept, come), jnp.where(core == 0, come, kept)], 1)

    qkv_heads = to_heads(qkv)
    attn_heads, lse_self = self_fwd(qkv_heads, seg_cont[:, None], seg_cont[None, :], heads // 2)
    attn_self = to_tokens(attn_heads).reshape(rows, width)
    resid_one = resid_zero + nt(attn_self, wt_attn_out) + proj_bias[2]
    norm_two = layer_norm(resid_one, norm_gain[1], norm_bias[1]).astype(BF)
    q_cross = ((nn(norm_two, w_cross_q) + proj_bias[3]) * (HEAD ** -0.5 * LOG2E)).astype(BF)
    kv = (nn(mem, w_cross_kv) + jnp.concatenate([jnp.zeros((width,), F32), proj_bias[4]])).astype(BF)
    attn_cross, lse_cross = cross_fwd(q_cross, kv, heads)
    resid_two = resid_one + nt(attn_cross, wt_cross_out) + proj_bias[5]
    norm_three = layer_norm(resid_two, norm_gain[2], norm_bias[2]).astype(BF)
    pre_act = nn(norm_three, w_mlp_in) + mlp_bias
    hidden = exact_gelu(pre_act).astype(BF)
    resid_out = resid_two + nt(hidden, wt_mlp_out) + out_bias
    output = fix(resid_out.astype(BF))

    g_low = grad_in
    grad_resid = grad_in.astype(F32)
    gb_mlp_out = jnp.sum(grad_resid, 0)
    gw_mlp_out = tn(g_low, hidden)
    grad_hidden = nn(g_low, wt_mlp_out)
    _, gelu_pull = jax.vjp(exact_gelu, pre_act)
    grad_pre = gelu_pull(grad_hidden)[0].astype(BF)
    gw_mlp_in = tn(norm_three, grad_pre)
    gb_mlp_in = jnp.sum(grad_pre, 0, dtype=F32)
    g_c = spread_sum(jnp.concatenate([gw_mlp_in.reshape(width, 2, units), gw_mlp_out.reshape(width, 2, units)], 2))
    grad_input, gain_three, shift_three = norm_back(resid_two, 2, nt(grad_pre, w_mlp_in))
    grad_resid = grad_resid + grad_input
    g_low = grad_resid.astype(BF)
    gb_cross_out = jnp.sum(grad_resid, 0)
    gw_cross_out = tn(g_low, attn_cross)
    grad_attn = nn(g_low, wt_cross_out).astype(BF)
    dq, dk, dv = cross_bwd(q_cross, kv, grad_attn, attn_cross, lse_cross, heads)
    gw_cross_q = tn(norm_two, dq)
    gb_cross_q = jnp.sum(dq, 0, dtype=F32)
    gw_cross_k = tn(mem, dk)
    gw_cross_v = tn(mem, dv)
    gb_cross_v = jnp.sum(dv, 0, dtype=F32)
    grad_input, gain_two, shift_two = norm_back(resid_one, 1, nt(dq, w_cross_q))
    grad_resid = grad_resid + grad_input
    g_low = grad_resid.astype(BF)
    gb_attn_out = jnp.sum(grad_resid, 0)
    gw_attn_out = tn(g_low, attn_self)
    split = lambda x: x.reshape(width, 2, part)
    g_b = spread_sum(jnp.concatenate([split(gw_attn_out), split(gw_cross_q), split(gw_cross_k), split(gw_cross_v), split(gw_cross_out)], 2))
    grad_attn = nn(g_low, wt_attn_out).astype(BF)
    dq, dk, dv = self_bwd(qkv_heads, to_heads(grad_attn.reshape(rows, 2, part)), attn_heads, lse_self,
                          seg_cont.reshape(-1, 1, BLK), seg_cont[:, None], heads // 2)
    dqkv = to_tokens(jnp.concatenate([dq, dk, dv], 1))
    flat = dqkv.reshape(rows, 2 * 3 * part)
    g_a = spread_sum(tn(norm_one, flat).reshape(width, 2, 3 * part))
    gb_qkv = jnp.sum(flat, 0, dtype=F32).reshape(2, 3, part)
    grad_input, gain_one, shift_one = norm_back(resid_zero, 0, nt(flat, w_qkv))
    grad_tokens = fix((grad_resid + grad_input).astype(BF)).astype(F32)
    gain_grads = jnp.stack([gain_one, gain_two, gain_three])
    shift_grads = jnp.stack([shift_one, shift_two, shift_three])
    proj_grads = jnp.stack([gb_qkv[:, 0].reshape(-1), gb_qkv[:, 2].reshape(-1), gb_attn_out, gb_cross_q, gb_cross_v, gb_cross_out])
    g_gain, g_shift, g_proj, g_units, g_out_bias = lax.psum((gain_grads, shift_grads, proj_grads, gb_mlp_in, gb_mlp_out), ALL)
    cut = lambda i: g_b[:, i * part:(i + 1) * part]
    return (output, grad_tokens, g_a.reshape(rows_here, 3, part), cut(0).T, cut(1),
            g_b[:, 2 * part:4 * part].reshape(rows_here, 2, part), cut(4).T,
            g_c[:, :units], g_c[:, units:].T, g_gain, g_shift, g_proj, g_units, g_out_bias)


def solution(mesh):
    devices = mesh.devices.reshape(-1, 2, mesh.shape["tensor"])
    grid = Mesh(devices, ALL)
    dp = ("chip", "core")
    in_specs = (P(ALL, None), P(dp, None, None), P(ALL), P(ALL), P(ALL, None), P(dp, None, "tensor"), P("tensor", dp),
                P(dp, "tensor"), P(dp, None, "tensor"), P("tensor", dp), P(dp, "tensor"), P("tensor", dp),
                P(), P(), P(), P(), P())
    out_specs = (P(ALL, None), P(ALL, None), P(dp, None, "tensor"), P("tensor", dp), P(dp, "tensor"), P(dp, None, "tensor"),
                 P("tensor", dp), P(dp, "tensor"), P("tensor", dp), P(), P(), P(), P(), P())
    return jax.shard_map(on_device, mesh=grid, in_specs=in_specs, out_specs=out_specs, check_vma=False)
```

```python
import functools, jax, jax.numpy as jnp
from jax import lax
from jax.experimental import pallas as pl
from jax.experimental.pallas import tpu as pltpu
from jax.sharding import Mesh
from jax.sharding import PartitionSpec as P
BLK=256
HEAD=64
LANES=128
NEG=-1e30
LOG2E=1.4426950408889634
F32=jnp.float32; BF=jnp.bfloat16

def lane_ids(rows): return lax.broadcasted_iota(jnp.int32,(rows,LANES),1)

def nt(a,b): return lax.dot_general(a,b,(((1,),(1,)),((),())),preferred_element_type=F32)
def nn(a,b): return lax.dot_general(a,b,(((1,),(0,)),((),())),preferred_element_type=F32)
def tn(a,b): return lax.dot_general(a,b,(((0,),(0,)),((),())),preferred_element_type=F32)

def pick(head, lanes): return (lanes<64) if head==0 else (lanes>=64)

def places(core, half):
    return (core * half, (1 - core) * half)


def rows_at(base, offset, count):
    return pl.ds(pl.multiple_of(base + offset, BLK), count)


def self_fwd_kernel(core_ref,kept_ref,come_ref,segq_ref,segk_ref,own_ref,sent_ref,lse_ref,q_ref,k_ref,vx_ref,o_ref):
    half=kept_ref.shape[1]; rows=2*half; n=rows//BLK
    core=core_ref[0]
    for ref,base in zip((kept_ref,come_ref),places(core,half)):
        at=rows_at(base,0,half)
        q_ref[at,:]=ref[0]
        k_ref[at,:]=ref[1]
        vx_ref[at,:LANES]=ref[2]
    vx_ref[:,LANES:]=jnp.ones((rows,LANES),BF)
    lanes=lane_ids(BLK)
    for i in range(n):
        r0=i*BLK; kn=r0+BLK
        q=q_ref[r0:kn,:]
        outs=[];lses=[]
        for h in range(2):
            qm=jnp.where(pick(h,lanes),q,jnp.zeros_like(q))
            s=nt(qm,k_ref[:kn,:])
            cut = half if i>=n//2 else r0
            a=s[:,:cut] if cut>0 else None
            b=s[:,cut:]
            w=kn-cut
            qi=lax.broadcasted_iota(jnp.int32,(BLK,w),0)+(r0-cut)
            kj=lax.broadcasted_iota(jnp.int32,(BLK,w),1)
            ok=kj<=qi
            if i>=n//2:
                ok=ok&(segk_ref[:,:kn-half]==segq_ref[r0-half:kn-half,:])
            b=jnp.where(ok,b,NEG)
            m=jnp.max(b,-1,keepdims=True)
            if a is not None: m=jnp.maximum(m,jnp.max(a,-1,keepdims=True))
            pb=jnp.exp2(b-m).astype(BF)
            ox=nn(pb,vx_ref[cut:kn,:])
            if a is not None:
                pa=jnp.exp2(a-m).astype(BF)
                ox=ox+nn(pa,vx_ref[:cut,:])
            l=ox[:,LANES:]
            outs.append(ox[:,:LANES]/l); lses.append(m+jnp.log2(l))
        sel=lanes<64
        o_ref[r0:kn,:]=jnp.where(sel,outs[0],outs[1]).astype(BF)
        lse_ref[r0:kn,:]=jnp.where(sel,lses[0],lses[1])
    for ref,base in zip((own_ref,sent_ref),places(core,half)):
        ref[...]=o_ref[rows_at(base,0,half),:]


def scalar():
    return pl.BlockSpec(memory_space=pltpu.SMEM)


def pair_cost(pairs,passes,nbytes):
    return pl.CostEstimate(flops=int(pairs*passes*512),bytes_accessed=int(nbytes),transcendentals=int(pairs))


def self_fwd(core,kept,come,segq,segk):
    half,part=kept.shape[1:]; rows=2*half
    three=pl.BlockSpec((3,half,LANES),lambda p:(0,0,p))
    one=pl.BlockSpec((half,LANES),lambda p:(0,p))
    n=rows//BLK
    return pl.pallas_call(self_fwd_kernel,
        grid=(part//LANES,),
        in_specs=[scalar(),three,three,pl.BlockSpec(segq.shape,lambda p:(0,0)),pl.BlockSpec(segk.shape,lambda p:(0,0))],
        out_specs=[one,one,pl.BlockSpec((rows,LANES),lambda p:(0,p))],
        out_shape=[jax.ShapeDtypeStruct((half,part),BF),jax.ShapeDtypeStruct((half,part),BF),jax.ShapeDtypeStruct((rows,part),F32)],
        scratch_shapes=[pltpu.VMEM((rows,LANES),BF),pltpu.VMEM((rows,LANES),BF),pltpu.VMEM((rows,2*LANES),BF),pltpu.VMEM((rows,LANES),BF)],
        compiler_params=pltpu.CompilerParams(vmem_limit_bytes=60*2**20),
        cost_estimate=pair_cost(n*(n+1)//2*BLK*BLK*(part//HEAD),2,12*rows*part),
        name="self_fwd",
    )(core,kept,come,segq,segk)

def cross_fwd_kernel(frames,q_ref,k_ref,v_ref,o_ref,lse_ref,kx_ref,vx_ref):
    rows=q_ref.shape[0]; n=rows//BLK; kp=k_ref.shape[0]
    tail=frames//BLK*BLK
    kx_ref[...]=k_ref[...]
    vx_ref[:,:LANES]=v_ref[...]
    vx_ref[:,LANES:]=jnp.ones((kp,LANES),BF)
    if frames<kp:
        keep=lax.broadcasted_iota(jnp.int32,(kp-tail,LANES),0)+tail<frames
        kx_ref[tail:,:]=jnp.where(keep,k_ref[tail:,:],jnp.zeros((),BF))
        vx_ref[tail:,:LANES]=jnp.where(keep,v_ref[tail:,:],jnp.zeros((),BF))
    lanes=lane_ids(BLK)
    for i in range(n):
        r0=i*BLK
        q=q_ref[r0:r0+BLK,:]
        outs=[];lses=[]
        for h in range(2):
            qm=jnp.where(pick(h,lanes),q,jnp.zeros_like(q))
            s=nt(qm,kx_ref[...])
            if frames<kp:
                kj=lax.broadcasted_iota(jnp.int32,(BLK,kp-tail),1)+tail
                s=jnp.concatenate([s[:,:tail],jnp.where(kj<frames,s[:,tail:],NEG)],axis=1)
            m=jnp.max(s,-1,keepdims=True)
            p=jnp.exp2(s-m).astype(BF)
            ox=nn(p,vx_ref[...])
            l=ox[:,LANES:]
            outs.append(ox[:,:LANES]/l); lses.append(m+jnp.log2(l))
        sel=lanes<64
        o_ref[r0:r0+BLK,:]=jnp.where(sel,outs[0],outs[1]).astype(BF)
        lse_ref[r0:r0+BLK,:]=jnp.where(sel,lses[0],lses[1])

def cross_fwd(q,kv,frames,heads):
    rows=q.shape[0]; npair=heads//2; kp=kv.shape[0]
    return pl.pallas_call(functools.partial(cross_fwd_kernel,frames),
        grid=(npair,),
        in_specs=[pl.BlockSpec((rows,LANES),lambda p:(0,p)),
                  pl.BlockSpec((kp,LANES),lambda p:(0,p)),
                  pl.BlockSpec((kp,LANES),lambda p:(0,npair+p))],
        out_specs=[pl.BlockSpec((rows,LANES),lambda p:(0,p)),pl.BlockSpec((rows,LANES),lambda p:(0,p))],
        out_shape=[jax.ShapeDtypeStruct((rows,heads*64),BF),jax.ShapeDtypeStruct((rows,heads*64),F32)],
        scratch_shapes=[pltpu.VMEM((kp,LANES),BF),pltpu.VMEM((kp,2*LANES),BF)],
        compiler_params=pltpu.CompilerParams(vmem_limit_bytes=60*2**20),
        cost_estimate=pair_cost(rows*kp*heads,2,8*rows*heads*64+4*kp*heads*64),
        name="cross_fwd",
    )(q,kv,kv)

def split3(x):
    hi=x.astype(BF); r=x-hi.astype(F32); mid=r.astype(BF); lo=(r-mid.astype(F32)).astype(BF)
    return hi,mid,lo

def aug(value,head,lanes,one_lane):
    hi,mid,lo=split3(-value)
    z=jnp.zeros(lanes.shape,F32)
    b=64*head
    x=jnp.where(lanes==b,hi.astype(F32),jnp.where(lanes==b+1,mid.astype(F32),jnp.where(lanes==b+2,lo.astype(F32),z)))
    if one_lane: x=jnp.where(lanes==b+3,1.0,x)
    return x.astype(BF)

def build_q(q,do,o,lse,at,qx_ref,dox_ref,masked):
    lanes=lane_ids(BLK)
    prod=do.astype(F32)*o.astype(F32)
    for h in range(2):
        sel=pick(h,lanes)
        delta=jnp.sum(jnp.where(sel,prod,0.0),-1,keepdims=True)
        qx_ref[h,at,:LANES]=jnp.where(sel,q,jnp.zeros((),BF))
        qx_ref[h,at,LANES:]=aug(lse,h,lanes,masked)
        dox_ref[h,at,:LANES]=jnp.where(sel,do,jnp.zeros((),BF))
        dox_ref[h,at,LANES:]=aug(delta,h,lanes,False)

def build_k(k,v,r0,at,kx_ref,km_ref,vx_ref,frames):
    lanes=lane_ids(BLK)
    low=lanes%64
    ones=jnp.where(low<3,1.0,0.0)
    kones=ones
    if frames is not None and r0+BLK>frames:
        bad=lax.broadcasted_iota(jnp.int32,(BLK,LANES),0)+r0>=frames
        k=jnp.where(bad,jnp.zeros((),BF),k); v=jnp.where(bad,jnp.zeros((),BF),v)
        kones=jnp.where(bad&(low==3),NEG,ones)
    kx_ref[at,:LANES]=k; kx_ref[at,LANES:]=kones.astype(BF)
    vx_ref[at,:LANES]=v; vx_ref[at,LANES:]=ones.astype(BF)
    for h in range(2): km_ref[h,at,:]=jnp.where(pick(h,lanes),k,jnp.zeros((),BF))

def block_back(kx,vx,km,qx,dox,mask):
    s=nt(kx,qx)
    if mask is not None: s=jnp.where(mask,s,NEG)
    p=jnp.exp2(s)
    dp=nt(vx,dox)
    ds=(p*dp).astype(BF)
    pb=p.astype(BF)
    dv=nn(pb,dox[:,:LANES])
    dk=nn(ds,qx[:,:LANES])
    dq=tn(ds,km)
    return dv,dk,dq

def self_bwd_kernel(core_ref,kept_ref,come_ref,do_ref,do_come_ref,o_ref,o_sent_ref,lse_ref,segq_ref,segk_ref,own_ref,sent_ref,
                    qx_ref,dox_ref,kx_ref,km_ref,vx_ref,dqa_ref,dk_ref,dv_ref,dka_ref,dva_ref):
    half=kept_ref.shape[1]; rows=2*half; n=rows//BLK
    core=core_ref[0]
    for ref,d,o,base in zip((kept_ref,come_ref),(do_ref,do_come_ref),(o_ref,o_sent_ref),places(core,half)):
        for r0 in range(0,half,BLK):
            here=slice(r0,r0+BLK); at=rows_at(base,r0,BLK)
            build_q(ref[0,here,:],d[here,:],o[here,:],lse_ref[at,:],at,qx_ref,dox_ref,False)
            build_k(ref[1,here,:],ref[2,here,:],0,at,kx_ref,km_ref,vx_ref,None)
    dqa_ref[...]=jnp.zeros_like(dqa_ref)
    tri=lax.broadcasted_iota(jnp.int32,(BLK,BLK),0)<=lax.broadcasted_iota(jnp.int32,(BLK,BLK),1)
    def pair(j,i,mask,first):
        kr=pl.ds(pl.multiple_of(j*BLK,BLK),BLK); qr=pl.ds(pl.multiple_of(i*BLK,BLK),BLK)
        r=[block_back(kx_ref[kr,:],vx_ref[kr,:],km_ref[h,kr,:],qx_ref[h,qr,:],dox_ref[h,qr,:],mask) for h in range(2)]
        dv=r[0][0]+r[1][0]; dk=r[0][1]+r[1][1]; dq=r[0][2]+r[1][2]
        if first: dva_ref[...]=dv; dka_ref[...]=dk
        else: dva_ref[...]+=dv; dka_ref[...]+=dk
        dqa_ref[qr,:]+=dq
    def flush(j):
        kr=pl.ds(pl.multiple_of(j*BLK,BLK),BLK)
        dk_ref[kr,:]=(dka_ref[...]*(1/LOG2E)).astype(BF)
        dv_ref[kr,:]=dva_ref[...].astype(BF)
    def outer_prompt(j,_):
        pair(j,j,tri,True)
        def inner(i,_): pair(j,i,None,False); return 0
        lax.fori_loop(j+1,n,inner,0)
        flush(j); return 0
    lax.fori_loop(0,n//2,outer_prompt,0)
    def segmask(j,i):
        sk=segk_ref[pl.ds(pl.multiple_of(j*BLK-half,BLK),BLK),:]
        sq=segq_ref[i-n//2]
        return sk==sq
    def outer_cont(j,_):
        pair(j,j,tri&segmask(j,j),True)
        def inner(i,_): pair(j,i,segmask(j,i),False); return 0
        lax.fori_loop(j+1,n,inner,0)
        flush(j); return 0
    lax.fori_loop(n//2,n,outer_cont,0)
    for ref,base in zip((own_ref,sent_ref),places(core,half)):
        at=rows_at(base,0,half)
        ref[0]=(dqa_ref[at,:]*0.125).astype(BF)
        ref[1]=dk_ref[at,:]
        ref[2]=dv_ref[at,:]

def self_bwd(core,kept,come,do,do_come,o,o_sent,lse,segq,segk):
    half,part=kept.shape[1:]; rows=2*half
    three=pl.BlockSpec((3,half,LANES),lambda p:(0,0,p))
    one=pl.BlockSpec((half,LANES),lambda p:(0,p))
    out=jax.ShapeDtypeStruct((3,half,part),BF)
    n=rows//BLK
    return pl.pallas_call(self_bwd_kernel,
        grid=(part//LANES,),
        in_specs=[scalar(),three,three,one,one,one,one,pl.BlockSpec((rows,LANES),lambda p:(0,p)),
                  pl.BlockSpec(segq.shape,lambda p:(0,0,0)),pl.BlockSpec(segk.shape,lambda p:(0,0))],
        out_specs=[three,three],
        out_shape=[out,out],
        scratch_shapes=[pltpu.VMEM((2,rows,2*LANES),BF),pltpu.VMEM((2,rows,2*LANES),BF),pltpu.VMEM((rows,2*LANES),BF),
                        pltpu.VMEM((2,rows,LANES),BF),pltpu.VMEM((rows,2*LANES),BF),pltpu.VMEM((rows,LANES),F32),
                        pltpu.VMEM((rows,LANES),BF),pltpu.VMEM((rows,LANES),BF),
                        pltpu.VMEM((BLK,LANES),F32),pltpu.VMEM((BLK,LANES),F32)],
        compiler_params=pltpu.CompilerParams(vmem_limit_bytes=60*2**20),
        cost_estimate=pair_cost(n*(n+1)//2*BLK*BLK*(part//HEAD),5,20*rows*part),
        name="self_bwd",
    )(core,kept,come,do,do_come,o,o_sent,lse,segq,segk)

def cross_bwd_kernel(frames,q_ref,k_ref,v_ref,do_ref,o_ref,lse_ref,dq_ref,dk_ref,dv_ref,
                     qx_ref,dox_ref,kx_ref,km_ref,vx_ref,dqa_ref,dka_ref,dva_ref):
    rows=q_ref.shape[0]; n=rows//BLK; kp=k_ref.shape[0]; nk=kp//BLK
    for r0 in range(0,rows,BLK):
        at=slice(r0,r0+BLK)
        build_q(q_ref[at,:],do_ref[at,:],o_ref[at,:],lse_ref[at,:],at,qx_ref,dox_ref,True)
    for r0 in range(0,kp,BLK):
        at=slice(r0,r0+BLK)
        build_k(k_ref[at,:],v_ref[at,:],r0,at,kx_ref,km_ref,vx_ref,frames)
    dqa_ref[...]=jnp.zeros_like(dqa_ref)
    def outer(j,_):
        kr=pl.ds(pl.multiple_of(j*BLK,BLK),BLK)
        dva=None
        for i in range(n):
            qr=slice(i*BLK,(i+1)*BLK)
            r=[block_back(kx_ref[kr,:],vx_ref[kr,:],km_ref[h,kr,:],qx_ref[h,qr,:],dox_ref[h,qr,:],None) for h in range(2)]
            dv=r[0][0]+r[1][0]; dk=r[0][1]+r[1][1]; dq=r[0][2]+r[1][2]
            if i==0: dva_ref[...]=dv; dka_ref[...]=dk
            else: dva_ref[...]+=dv; dka_ref[...]+=dk
            dqa_ref[qr,:]+=dq
        dk_ref[kr,:]=(dka_ref[...]*(1/LOG2E)).astype(BF)
        dv_ref[kr,:]=dva_ref[...].astype(BF)
        return 0
    lax.fori_loop(0,nk,outer,0)
    dq_ref[...]=(dqa_ref[...]*0.125).astype(BF)

def cross_bwd(q,kv,frames,do,o,lse,heads):
    rows=q.shape[0]; npair=heads//2; kp=kv.shape[0]
    big=lambda f:pl.BlockSpec((rows,LANES),f)
    kb=lambda f:pl.BlockSpec((kp,LANES),f)
    return pl.pallas_call(functools.partial(cross_bwd_kernel,frames),
        grid=(npair,),
        in_specs=[big(lambda p:(0,p)),kb(lambda p:(0,p)),kb(lambda p:(0,npair+p)),big(lambda p:(0,p)),big(lambda p:(0,p)),big(lambda p:(0,p))],
        out_specs=[big(lambda p:(0,p)),kb(lambda p:(0,p)),kb(lambda p:(0,p))],
        out_shape=[jax.ShapeDtypeStruct((rows,heads*64),BF),jax.ShapeDtypeStruct((kp,heads*64),BF),jax.ShapeDtypeStruct((kp,heads*64),BF)],
        scratch_shapes=[pltpu.VMEM((2,rows,2*LANES),BF),pltpu.VMEM((2,rows,2*LANES),BF),pltpu.VMEM((kp,2*LANES),BF),
                        pltpu.VMEM((2,kp,LANES),BF),pltpu.VMEM((kp,2*LANES),BF),pltpu.VMEM((rows,LANES),F32),
                        pltpu.VMEM((BLK,LANES),F32),pltpu.VMEM((BLK,LANES),F32)],
        compiler_params=pltpu.CompilerParams(vmem_limit_bytes=60*2**20),
        cost_estimate=pair_cost(rows*kp*heads,5,12*rows*heads*64+8*kp*heads*64),
        name="cross_bwd",
    )(q,kv,kv,do,o,lse)


EPSILON = 1e-05
ROWS = 256
BIG = 60 * 2**20


def whole(shape):
    return pl.BlockSpec(shape, lambda *_: (0,) * len(shape), pipeline_mode=pl.Buffered(1))


def by_rows(*lead_and_cols):
    *lead, cols = lead_and_cols
    return pl.BlockSpec((*lead, ROWS, cols), lambda i: (0,) * len(lead) + (i, 0))


def shaped(shape, dtype):
    return jax.ShapeDtypeStruct(shape, dtype)


def cost(flops, nbytes, trans=0):
    return pl.CostEstimate(flops=int(flops), bytes_accessed=int(nbytes), transcendentals=int(trans))


def normalize(values):
    centre = values - jnp.mean(values, -1, keepdims=True)
    scale = lax.rsqrt(jnp.mean(centre * centre, -1, keepdims=True) + EPSILON)
    return centre * scale, scale


def norm_grad(normed, scale, gain, grad):
    weighted = grad * gain
    return scale * (weighted - jnp.mean(weighted, -1, keepdims=True)
                    - normed * jnp.mean(weighted * normed, -1, keepdims=True))


def accumulate(ref, value):
    @pl.when(pl.program_id(0) == 0)
    def _():
        ref[...] = value

    @pl.when(pl.program_id(0) > 0)
    def _():
        ref[...] += value


def column_sum(values):
    return jnp.sum(values, 0, keepdims=True)


def qkv_kernel(core_ref, x_ref, w_ref, gain_ref, shift_ref, bias_ref, norm_ref, kept_ref, sent_ref):
    part = kept_ref.shape[2]
    normed, _ = normalize(x_ref[...].astype(F32))
    low = (normed * gain_ref[0:1] + shift_ref[0:1]).astype(BF)
    norm_ref[...] = low
    core = core_ref[0]
    for out_ref, at in ((kept_ref, core), (sent_ref, 1 - core)):
        cols = nn(low, w_ref[at])
        out_ref[0] = ((cols[:, :part] + bias_ref[at, 0:1]) * (HEAD ** -0.5 * LOG2E)).astype(BF)
        out_ref[1] = cols[:, part:2 * part].astype(BF)
        out_ref[2] = (cols[:, 2 * part:] + bias_ref[at, 1:2]).astype(BF)


def qkv_project(core, x, w, gain, shift, bias):
    rows, width = x.shape
    part = width // 2
    out = shaped((3, rows, part), BF)
    return pl.pallas_call(
        qkv_kernel, grid=(rows // ROWS,),
        in_specs=[scalar(), by_rows(width), whole(w.shape), whole(gain.shape), whole(shift.shape), whole(bias.shape)],
        out_specs=[by_rows(width), by_rows(3, part), by_rows(3, part)],
        out_shape=[shaped((rows, width), BF), out, out],
        compiler_params=pltpu.CompilerParams(vmem_limit_bytes=BIG),
        cost_estimate=cost(6 * rows * width * width, 2 * (3 * width * width + 6 * rows * width)), name="qkv_project",
    )(core, x, w, gain, shift, bias)


def memory_kernel(frames, mine_ref, own_ref, come_ref, w_ref, bias_ref, kv_ref, mem_ref):
    width = own_ref.shape[1]
    part = width // 2
    mem = jnp.where(mine_ref[0] == 1, own_ref[...], come_ref[...])
    row = lax.broadcasted_iota(jnp.int32, mem.shape, 0) + pl.program_id(0) * ROWS
    mem = jnp.where(row < frames, mem, jnp.zeros((), BF))
    mem_ref[...] = mem
    for t in range(2):
        cols = nn(mem, w_ref[t])
        kv_ref[:, t * part:(t + 1) * part] = cols[:, :part].astype(BF)
        kv_ref[:, width + t * part:width + (t + 1) * part] = (cols[:, part:] + bias_ref[4:5, t * part:(t + 1) * part]).astype(BF)


def memory_project(mine, own, come, w_mid, bias):
    frames, width = own.shape
    steps = pl.cdiv(frames, ROWS)
    return pl.pallas_call(
        functools.partial(memory_kernel, frames), grid=(steps,),
        in_specs=[scalar(), by_rows(width), by_rows(width),
                  pl.BlockSpec((2, width, width), lambda i: (0, 0, 1), pipeline_mode=pl.Buffered(1)), whole(bias.shape)],
        out_specs=[by_rows(2 * width), by_rows(width)],
        out_shape=[shaped((steps * ROWS, 2 * width), BF), shaped((steps * ROWS, width), BF)],
        compiler_params=pltpu.CompilerParams(vmem_limit_bytes=BIG),
        cost_estimate=cost(4 * frames * width * width, 2 * (2 * width * width + 5 * frames * width)), name="memory_project",
    )(mine, own, come, w_mid, bias)


def middle_kernel(core_ref, x_ref, own_ref, come_ref, wo_ref, wq_ref, gain_ref, shift_ref, bias_ref,
                  resid_ref, norm_ref, q_ref):
    part = own_ref.shape[1]
    core = core_ref[0]
    resid = x_ref[...].astype(F32) + nt(own_ref[...], wo_ref[core]) + nt(come_ref[...], wo_ref[1 - core]) + bias_ref[2:3]
    resid_ref[...] = resid
    normed, _ = normalize(resid)
    low = (normed * gain_ref[1:2] + shift_ref[1:2]).astype(BF)
    norm_ref[...] = low
    for t in range(2):
        at = slice(t * part, (t + 1) * part)
        q_ref[:, at] = ((nn(low, wq_ref[t]) + bias_ref[3:4, at]) * (HEAD ** -0.5 * LOG2E)).astype(BF)


def middle(core, x, own, come, w_mid, gain, shift, bias):
    rows, width = x.shape
    part = width // 2
    w_at = lambda c: pl.BlockSpec((2, width, part), lambda i: (0, 0, c), pipeline_mode=pl.Buffered(1))
    return pl.pallas_call(
        middle_kernel, grid=(rows // ROWS,),
        in_specs=[scalar(), by_rows(width), by_rows(part), by_rows(part), w_at(0), w_at(1),
                  whole(gain.shape), whole(shift.shape), whole(bias.shape)],
        out_specs=[by_rows(width)] * 3,
        out_shape=[shaped((rows, width), F32), shaped((rows, width), BF), shaped((rows, width), BF)],
        compiler_params=pltpu.CompilerParams(vmem_limit_bytes=BIG),
        cost_estimate=cost(4 * rows * width * width, 4 * width * width + 12 * rows * width), name="middle",
    )(core, x, own, come, w_mid, w_mid, gain, shift, bias)


def gelu_parts(v):
    z = jnp.abs(v) * (0.5 ** 0.5)
    t = 1.0 / (1.0 + 0.3275911 * z)
    bell = jnp.exp2(v * v * (-0.5 * LOG2E))
    poly = ((((1.061405429 * t - 1.453152027) * t + 1.421413741) * t - 0.284496736) * t + 0.254829592) * t
    tail = (0.5 * poly) * bell
    phi = jnp.where(v >= 0, 1.0 - tail, tail)
    return phi, phi + v * bell * 0.3989422804014327


def feed_kernel(attn_ref, resid_ref, g_ref, wo_ref, wi_ref, wm_ref, gain_ref, shift_ref, bias_ref, unit_bias_ref, out_bias_ref,
                out_ref, norm_ref, hidden_ref, dpre_ref, g2_ref, dattn_ref,
                sum_g_ref, sum_dpre_ref, sum_g2_ref, sum_gain_ref, sum_shift_ref):
    part = wo_ref.shape[2]
    units = wi_ref.shape[2]
    resid = resid_ref[...] + bias_ref[5:6]
    for t in range(2):
        resid = resid + nt(attn_ref[:, t * part:(t + 1) * part], wo_ref[t])
    normed, scale = normalize(resid)
    low = (normed * gain_ref[2:3] + shift_ref[2:3]).astype(BF)
    norm_ref[...] = low
    g_low = g_ref[...]
    out = resid + out_bias_ref[...]
    back = jnp.zeros_like(resid)
    sums = []
    for t in range(2):
        at = slice(t * units, (t + 1) * units)
        pre = nn(low, wi_ref[t]) + unit_bias_ref[:, at]
        phi, slope = gelu_parts(pre)
        hidden = (pre * phi).astype(BF)
        hidden_ref[:, at] = hidden
        out = out + nt(hidden, wm_ref[t])
        dpre = nn(g_low, wm_ref[t]) * slope
        sums.append(column_sum(dpre))
        dpre = dpre.astype(BF)
        dpre_ref[:, at] = dpre
        back = back + nt(dpre, wi_ref[t])
    out_ref[...] = out.astype(BF)
    accumulate(sum_dpre_ref, jnp.concatenate(sums, 1))
    g = g_low.astype(F32)
    accumulate(sum_g_ref, column_sum(g))
    accumulate(sum_gain_ref, column_sum(back * normed))
    accumulate(sum_shift_ref, column_sum(back))
    g2 = g + norm_grad(normed, scale, gain_ref[2:3], back)
    accumulate(sum_g2_ref, column_sum(g2))
    g2_ref[...] = g2
    g2_low = g2.astype(BF)
    for t in range(2):
        dattn_ref[:, t * part:(t + 1) * part] = nn(g2_low, wo_ref[t]).astype(BF)


def feed(attn, resid, g, w_mid, w_ff, gain, shift, bias, unit_bias, out_bias):
    rows, width = resid.shape
    part = width // 2
    units = w_ff.shape[2] // 2
    w_at = lambda cols, c: pl.BlockSpec((2, width, cols), lambda i: (0, 0, c), pipeline_mode=pl.Buffered(1))
    line = lambda cols: (pl.BlockSpec((1, cols), lambda i: (0, 0)), shaped((1, cols), F32))
    lines = [line(width), line(2 * units), line(width), line(width), line(width)]
    return pl.pallas_call(
        feed_kernel, grid=(rows // ROWS,),
        in_specs=[by_rows(width), by_rows(width), by_rows(width), w_at(part, 4), w_at(units, 0), w_at(units, 1),
                  whole(gain.shape), whole(shift.shape), whole(bias.shape), whole(unit_bias.shape), whole(out_bias.shape)],
        out_specs=[by_rows(width), by_rows(width), by_rows(2 * units), by_rows(2 * units), by_rows(width), by_rows(width)] + [a for a, _ in lines],
        out_shape=[shaped((rows, width), BF), shaped((rows, width), BF), shaped((rows, 2 * units), BF), shaped((rows, 2 * units), BF),
                   shaped((rows, width), F32), shaped((rows, width), BF)] + [b for _, b in lines],
        compiler_params=pltpu.CompilerParams(vmem_limit_bytes=BIG),
        cost_estimate=cost(2 * rows * width * (2 * width + 8 * units), 2 * width * (width + 4 * units) + 2 * rows * (8 * width + 4 * units), 4 * rows * units),
        name="feed",
    )(attn, resid, g, w_mid, w_ff, w_ff, gain, shift, bias, unit_bias, out_bias)


def feed_weights_kernel(norm_ref, g_ref, dpre_ref, hidden_ref, out_ref):
    cols = dpre_ref.shape[1]
    out_ref[0, :, :cols] = tn(norm_ref[...], dpre_ref[...]).astype(BF)
    out_ref[0, :, cols:] = tn(g_ref[...], hidden_ref[...]).astype(BF)


def feed_weights(norm, g, dpre, hidden):
    rows, width = norm.shape
    units = dpre.shape[1] // 2
    cols = units // 2
    return pl.pallas_call(
        feed_weights_kernel, grid=(2, 2),
        in_specs=[whole(norm.shape), whole(g.shape), pl.BlockSpec((rows, cols), lambda t, c: (0, 2 * t + c)),
                  pl.BlockSpec((rows, cols), lambda t, c: (0, 2 * t + c))],
        out_specs=pl.BlockSpec((1, width, 2 * cols), lambda t, c: (t, 0, c)),
        out_shape=shaped((2, width, 2 * units), BF),
        compiler_params=pltpu.CompilerParams(vmem_limit_bytes=BIG),
        cost_estimate=cost(8 * rows * width * units, 2 * (4 * width * units + 4 * rows * units)), name="feed_weights",
    )(norm, g, dpre, hidden)


def middle_back_kernel(core_ref, dq_ref, resid_ref, g2_ref, wq_ref, wo_ref, gain_ref,
                       g1_ref, kept_ref, sent_ref, sum_dq_ref, sum_g1_ref, sum_gain_ref, sum_shift_ref):
    part = kept_ref.shape[1]
    core = core_ref[0]
    dq = dq_ref[...]
    back = nt(dq[:, :part], wq_ref[0]) + nt(dq[:, part:], wq_ref[1])
    accumulate(sum_dq_ref, column_sum(dq.astype(F32)))
    normed, scale = normalize(resid_ref[...])
    accumulate(sum_gain_ref, column_sum(back * normed))
    accumulate(sum_shift_ref, column_sum(back))
    g1 = g2_ref[...] + norm_grad(normed, scale, gain_ref[1:2], back)
    g1_ref[...] = g1
    accumulate(sum_g1_ref, column_sum(g1))
    low = g1.astype(BF)
    kept_ref[...] = nn(low, wo_ref[core]).astype(BF)
    sent_ref[...] = nn(low, wo_ref[1 - core]).astype(BF)


def middle_back(core, dq, resid, g2, w_mid, gain):
    rows, width = resid.shape
    part = width // 2
    w_at = lambda c: pl.BlockSpec((2, width, part), lambda i: (0, 0, c), pipeline_mode=pl.Buffered(1))
    line = pl.BlockSpec((1, width), lambda i: (0, 0))
    return pl.pallas_call(
        middle_back_kernel, grid=(rows // ROWS,),
        in_specs=[scalar(), by_rows(width), by_rows(width), by_rows(width), w_at(1), w_at(0), whole(gain.shape)],
        out_specs=[by_rows(width), by_rows(part), by_rows(part)] + [line] * 4,
        out_shape=[shaped((rows, width), F32), shaped((rows, part), BF), shaped((rows, part), BF)] + [shaped((1, width), F32)] * 4,
        compiler_params=pltpu.CompilerParams(vmem_limit_bytes=BIG),
        cost_estimate=cost(4 * rows * width * width, 4 * width * width + 18 * rows * width), name="middle_back",
    )(core, dq, resid, g2, w_mid, w_mid, gain)


def middle_weights_kernel(core_ref, g1_ref, own_ref, come_ref, norm_ref, dq_ref, mem_ref, dk_ref, dv_ref, g2_ref, attn_ref,
                          out_ref, sum_dv_ref):
    part = own_ref.shape[1]
    attn_self = jnp.where(pl.program_id(0) == core_ref[0], own_ref[...], come_ref[...])
    out_ref[0, :, :part] = tn(g1_ref[...].astype(BF), attn_self).astype(BF)
    out_ref[0, :, part:2 * part] = tn(norm_ref[...], dq_ref[...]).astype(BF)
    mem = mem_ref[...]
    out_ref[0, :, 2 * part:3 * part] = tn(mem, dk_ref[...]).astype(BF)
    out_ref[0, :, 3 * part:4 * part] = tn(mem, dv_ref[...]).astype(BF)
    out_ref[0, :, 4 * part:] = tn(g2_ref[...].astype(BF), attn_ref[...]).astype(BF)
    sum_dv_ref[...] = column_sum(dv_ref[...].astype(F32))


def middle_weights(core, g1, own, come, norm, dq, mem, dk, dv, g2, attn):
    rows, width = norm.shape
    frames = mem.shape[0]
    part = width // 2
    half = lambda n: pl.BlockSpec((n, part), lambda t: (0, t))
    return pl.pallas_call(
        middle_weights_kernel, grid=(2,),
        in_specs=[scalar(), whole(g1.shape), whole(own.shape), whole(come.shape), whole(norm.shape), half(rows), whole(mem.shape),
                  half(frames), half(frames), whole(g2.shape), half(rows)],
        out_specs=[pl.BlockSpec((1, width, 5 * part), lambda t: (t, 0, 0)), pl.BlockSpec((1, part), lambda t: (0, t))],
        out_shape=[shaped((2, width, 5 * part), BF), shaped((1, width), F32)],
        compiler_params=pltpu.CompilerParams(vmem_limit_bytes=BIG),
        cost_estimate=cost(2 * width * width * (3 * rows + 2 * frames), 10 * width * width + 2 * width * (10 * rows + 3 * frames)),
        name="middle_weights",
    )(core, g1, own, come, norm, dq, mem, dk, dv, g2, attn)


def qkv_back_kernel(core_ref, own_ref, come_ref, x_ref, g1_ref, w_ref, gain_ref, grad_ref, sum_gain_ref, sum_shift_ref):
    part = own_ref.shape[2]
    core = core_ref[0]
    back = jnp.zeros(x_ref.shape, F32)
    for ref, at in ((own_ref, core), (come_ref, 1 - core)):
        for j in range(3):
            back = back + nt(ref[j], w_ref[at, :, j * part:(j + 1) * part])
    normed, scale = normalize(x_ref[...].astype(F32))
    accumulate(sum_gain_ref, column_sum(back * normed))
    accumulate(sum_shift_ref, column_sum(back))
    grad_ref[...] = (g1_ref[...] + norm_grad(normed, scale, gain_ref[0:1], back)).astype(BF)


def qkv_back(core, own, come, x, g1, w, gain):
    rows, width = x.shape
    part = width // 2
    line = pl.BlockSpec((1, width), lambda i: (0, 0))
    return pl.pallas_call(
        qkv_back_kernel, grid=(rows // ROWS,),
        in_specs=[scalar(), by_rows(3, part), by_rows(3, part), by_rows(width), by_rows(width), whole(w.shape), whole(gain.shape)],
        out_specs=[by_rows(width), line, line],
        out_shape=[shaped((rows, width), BF), shaped((1, width), F32), shaped((1, width), F32)],
        compiler_params=pltpu.CompilerParams(vmem_limit_bytes=BIG),
        cost_estimate=cost(6 * rows * width * width, 2 * (3 * width * width + 7 * rows * width)), name="qkv_back",
    )(core, own, come, x, g1, w, gain)


def qkv_weights_kernel(core_ref, norm_ref, own_ref, come_ref, out_ref, sum_ref):
    part = own_ref.shape[2]
    mine = pl.program_id(0) == core_ref[0]
    norm = norm_ref[...]
    for j in range(3):
        grad = jnp.where(mine, own_ref[j], come_ref[j])
        out_ref[0, :, j * part:(j + 1) * part] = tn(norm, grad).astype(BF)
        sum_ref[0, :, j * part:(j + 1) * part] = column_sum(grad.astype(F32))


def qkv_weights(core, norm, own, come):
    rows, width = norm.shape
    part = width // 2
    return pl.pallas_call(
        qkv_weights_kernel, grid=(2,),
        in_specs=[scalar(), whole(norm.shape), whole(own.shape), whole(come.shape)],
        out_specs=[pl.BlockSpec((1, width, 3 * part), lambda t: (t, 0, 0)), pl.BlockSpec((1, 1, 3 * part), lambda t: (t, 0, 0))],
        out_shape=[shaped((2, width, 3 * part), BF), shaped((2, 1, 3 * part), F32)],
        compiler_params=pltpu.CompilerParams(vmem_limit_bytes=BIG),
        cost_estimate=cost(6 * rows * width * width, 2 * (3 * width * width + 4 * rows * width)), name="qkv_weights",
    )(core, norm, own, come)


ALL = ("tensor", "chip", "core")


def fetch(shard):
    full = lax.all_gather(shard, ALL, axis=0, tiled=True)
    return full.reshape(2, -1, shard.shape[1])


def spread_sum(grad):
    return lax.psum_scatter(grad.reshape(-1, grad.shape[2]), ALL, scatter_dimension=0, tiled=True).astype(F32)


def on_device(tokens, memory, seg_ids, positions, grad_output, attn_in, attn_out, cross_q, cross_kv,
              cross_out, mlp_in, mlp_out, norm_gain, norm_bias, proj_bias, mlp_bias, out_bias):
    width = tokens.shape[1]
    rows_here, _, part = attn_in.shape
    units = mlp_in.shape[1]
    heads = width // HEAD
    frames = memory.shape[1]
    core = lax.axis_index("core")
    tensor = lax.axis_index("tensor")
    core_at = core.astype(jnp.int32).reshape(1)
    swap = [(0, 0), (1, 2), (2, 1), (3, 3)]
    fix = lambda x: lax.ppermute(x, ("core", "tensor"), swap)
    other = lambda x: lax.ppermute(x, "core", [(0, 1), (1, 0)])

    w_qkv = fetch(attn_in.reshape(rows_here, 3 * part))
    moved = fix(tokens)
    w_mid = fetch(jnp.concatenate([attn_out.T, cross_q, cross_kv.reshape(rows_here, 2 * part), cross_out.T], 1))
    w_ff = fetch(jnp.concatenate([mlp_in, mlp_out.T], 1))
    grad_in = fix(grad_output)
    seg_mine = fix(seg_ids)
    seg_cont = jnp.where(core == 1, seg_mine, other(seg_mine))
    mem_come = other(memory[0])
    bias_halves = proj_bias[:2].reshape(2, 2, part).transpose(1, 0, 2)

    norm_one, kept, sent = qkv_project(core_at, moved, w_qkv, norm_gain, norm_bias, bias_halves)
    come = other(sent)
    kv, mem = memory_project((core == tensor).astype(jnp.int32).reshape(1), memory[0], mem_come, w_mid, proj_bias)
    o_kept, o_sent, lse_self = self_fwd(core_at, kept, come, seg_cont[:, None], seg_cont[None, :])
    o_come = other(o_sent)
    resid_one, norm_two, q_cross = middle(core_at, moved, o_kept, o_come, w_mid, norm_gain, norm_bias, proj_bias)
    attn_cross, lse_cross = cross_fwd(q_cross, kv, frames, heads)
    (out, norm_three, hidden, dpre, g_two, dattn, sum_g, sum_dpre, sum_g_two, gain_three, shift_three) = feed(
        attn_cross, resid_one, grad_in, w_mid, w_ff, norm_gain, norm_bias, proj_bias, mlp_bias[None], out_bias[None])
    output = fix(out)
    gw_ff = feed_weights(norm_three, grad_in, dpre, hidden)
    dattn, gw_ff = lax.optimization_barrier((dattn, gw_ff))
    g_ff = spread_sum(gw_ff)
    dq, dk, dv = cross_bwd(q_cross, kv, frames, dattn, attn_cross, lse_cross, heads)
    g_one, do_kept, do_sent, sum_dq, sum_g_one, gain_two, shift_two = middle_back(core_at, dq, resid_one, g_two, w_mid, norm_gain)
    do_come = other(do_sent)
    gw_mid, sum_dv = middle_weights(core_at, g_one, o_kept, o_come, norm_two, dq, mem, dk, dv, g_two, attn_cross)
    do_kept, gw_mid = lax.optimization_barrier((do_kept, gw_mid))
    g_mid = spread_sum(gw_mid)
    d_kept, d_sent = self_bwd(core_at, kept, come, do_kept, do_come, o_kept, o_sent, lse_self,
                              seg_cont.reshape(-1, 1, BLK), seg_cont[:, None])
    d_come = other(d_sent)
    gw_qkv, sum_qkv = qkv_weights(core_at, norm_one, d_kept, d_come)
    g_qkv = spread_sum(gw_qkv)
    grad_low, gain_one, shift_one = qkv_back(core_at, d_kept, d_come, moved, g_one, w_qkv, norm_gain)
    grad_tokens = fix(grad_low).astype(F32)

    sum_qkv = sum_qkv.reshape(2, 3, part)
    gain_grads = jnp.concatenate([gain_one, gain_two, gain_three])
    shift_grads = jnp.concatenate([shift_one, shift_two, shift_three])
    proj_grads = jnp.concatenate([sum_qkv[:, 0].reshape(1, -1), sum_qkv[:, 2].reshape(1, -1), sum_g_one, sum_dq, sum_dv, sum_g_two])
    g_gain, g_shift, g_proj, g_units, g_out_bias = lax.psum((gain_grads, shift_grads, proj_grads, sum_dpre[0], sum_g[0]), ALL)
    cut = lambda i: g_mid[:, i * part:(i + 1) * part]
    quarter = units // 2
    pieces = [g_ff[:, i * quarter:(i + 1) * quarter] for i in range(4)]
    return (output, grad_tokens, g_qkv.reshape(rows_here, 3, part), cut(0).T, cut(1),
            g_mid[:, 2 * part:4 * part].reshape(rows_here, 2, part), cut(4).T,
            jnp.concatenate([pieces[0], pieces[2]], 1), jnp.concatenate([pieces[1], pieces[3]], 1).T,
            g_gain, g_shift, g_proj, g_units, g_out_bias)


def solution(mesh):
    grid = Mesh(mesh.devices.reshape(-1, 2, mesh.shape["tensor"]), ("chip", "core", "tensor"))
    rows = ("chip", "core", "tensor")
    dp = ("chip", "core")
    in_specs = (P(rows, None), P(dp, None, None), P(rows), P(rows), P(rows, None), P(dp, None, "tensor"), P("tensor", dp),
                P(dp, "tensor"), P(dp, None, "tensor"), P("tensor", dp), P(dp, "tensor"), P("tensor", dp),
                P(), P(), P(), P(), P())
    out_specs = (P(rows, None), P(rows, None), P(dp, None, "tensor"), P("tensor", dp), P(dp, "tensor"), P(dp, None, "tensor"),
                 P("tensor", dp), P(dp, "tensor"), P("tensor", dp), P(), P(), P(), P(), P())
    return jax.shard_map(on_device, mesh=grid, in_specs=in_specs, out_specs=out_specs, check_vma=False)
```

```python
import functools, jax, jax.numpy as jnp
from jax import lax
from jax.experimental import pallas as pl
from jax.experimental.pallas import tpu as pltpu
from jax.sharding import Mesh
from jax.sharding import PartitionSpec as P
BLK=256
HEAD=64
LANES=128
NEG=-1e30
LOG2E=1.4426950408889634
F32=jnp.float32; BF=jnp.bfloat16

def lane_ids(rows): return lax.broadcasted_iota(jnp.int32,(rows,LANES),1)

def nt(a,b): return lax.dot_general(a,b,(((1,),(1,)),((),())),preferred_element_type=F32)
def nn(a,b): return lax.dot_general(a,b,(((1,),(0,)),((),())),preferred_element_type=F32)
def tn(a,b): return lax.dot_general(a,b,(((0,),(0,)),((),())),preferred_element_type=F32)

def pick(head, lanes): return (lanes<64) if head==0 else (lanes>=64)

def places(core, half):
    return (core * half, (1 - core) * half)


def rows_at(base, offset, count):
    return pl.ds(pl.multiple_of(base + offset, BLK), count)


def self_fwd_kernel(core_ref,kept_ref,come_ref,segq_ref,segk_ref,own_ref,sent_ref,lse_ref,q_ref,k_ref,vx_ref,o_ref):
    half=kept_ref.shape[1]; rows=2*half; n=rows//BLK
    core=core_ref[0]
    for ref,base in zip((kept_ref,come_ref),places(core,half)):
        at=rows_at(base,0,half)
        q_ref[at,:]=ref[0]
        k_ref[at,:]=ref[1]
        vx_ref[at,:LANES]=ref[2]
    vx_ref[:,LANES:]=jnp.ones((rows,LANES),BF)
    lanes=lane_ids(BLK)
    for i in range(n):
        r0=i*BLK; kn=r0+BLK
        q=q_ref[r0:kn,:]
        outs=[];lses=[]
        for h in range(2):
            qm=jnp.where(pick(h,lanes),q,jnp.zeros_like(q))
            s=nt(qm,k_ref[:kn,:])
            cut = half if i>=n//2 else r0
            a=s[:,:cut] if cut>0 else None
            b=s[:,cut:]
            w=kn-cut
            qi=lax.broadcasted_iota(jnp.int32,(BLK,w),0)+(r0-cut)
            kj=lax.broadcasted_iota(jnp.int32,(BLK,w),1)
            ok=kj<=qi
            if i>=n//2:
                ok=ok&(segk_ref[:,:kn-half]==segq_ref[r0-half:kn-half,:])
            b=jnp.where(ok,b,NEG)
            m=jnp.max(b,-1,keepdims=True)
            if a is not None: m=jnp.maximum(m,jnp.max(a,-1,keepdims=True))
            pb=jnp.exp2(b-m).astype(BF)
            ox=nn(pb,vx_ref[cut:kn,:])
            if a is not None:
                pa=jnp.exp2(a-m).astype(BF)
                ox=ox+nn(pa,vx_ref[:cut,:])
            l=ox[:,LANES:]
            outs.append(ox[:,:LANES]/l); lses.append(m+jnp.log2(l))
        sel=lanes<64
        o_ref[r0:kn,:]=jnp.where(sel,outs[0],outs[1]).astype(BF)
        lse_ref[r0:kn,:]=jnp.where(sel,lses[0],lses[1])
    for ref,base in zip((own_ref,sent_ref),places(core,half)):
        ref[...]=o_ref[rows_at(base,0,half),:]


def scalar():
    return pl.BlockSpec(memory_space=pltpu.SMEM)


def pair_cost(pairs,passes,nbytes):
    return pl.CostEstimate(flops=int(pairs*passes*512),bytes_accessed=int(nbytes),transcendentals=int(pairs))


def self_fwd(core,kept,come,segq,segk):
    half,part=kept.shape[1:]; rows=2*half
    three=pl.BlockSpec((3,half,LANES),lambda p:(0,0,p))
    one=pl.BlockSpec((half,LANES),lambda p:(0,p))
    n=rows//BLK
    return pl.pallas_call(self_fwd_kernel,
        grid=(part//LANES,),
        in_specs=[scalar(),three,three,pl.BlockSpec(segq.shape,lambda p:(0,0)),pl.BlockSpec(segk.shape,lambda p:(0,0))],
        out_specs=[one,one,pl.BlockSpec((rows,LANES),lambda p:(0,p))],
        out_shape=[jax.ShapeDtypeStruct((half,part),BF),jax.ShapeDtypeStruct((half,part),BF),jax.ShapeDtypeStruct((rows,part),F32)],
        scratch_shapes=[pltpu.VMEM((rows,LANES),BF),pltpu.VMEM((rows,LANES),BF),pltpu.VMEM((rows,2*LANES),BF),pltpu.VMEM((rows,LANES),BF)],
        compiler_params=pltpu.CompilerParams(vmem_limit_bytes=60*2**20),
        cost_estimate=pair_cost(n*(n+1)//2*BLK*BLK*(part//HEAD),2,12*rows*part),
        name="self_fwd",
    )(core,kept,come,segq,segk)

def cross_fwd_kernel(frames,q_ref,k_ref,v_ref,o_ref,lse_ref,kx_ref,vx_ref):
    rows=q_ref.shape[0]; n=rows//BLK; kp=k_ref.shape[0]
    tail=frames//BLK*BLK
    kx_ref[...]=k_ref[...]
    vx_ref[:,:LANES]=v_ref[...]
    vx_ref[:,LANES:]=jnp.ones((kp,LANES),BF)
    if frames<kp:
        keep=lax.broadcasted_iota(jnp.int32,(kp-tail,LANES),0)+tail<frames
        kx_ref[tail:,:]=jnp.where(keep,k_ref[tail:,:],jnp.zeros((),BF))
        vx_ref[tail:,:LANES]=jnp.where(keep,v_ref[tail:,:],jnp.zeros((),BF))
    lanes=lane_ids(BLK)
    for i in range(n):
        r0=i*BLK
        q=q_ref[r0:r0+BLK,:]
        outs=[];lses=[]
        for h in range(2):
            qm=jnp.where(pick(h,lanes),q,jnp.zeros_like(q))
            s=nt(qm,kx_ref[...])
            if frames<kp:
                kj=lax.broadcasted_iota(jnp.int32,(BLK,kp-tail),1)+tail
                s=jnp.concatenate([s[:,:tail],jnp.where(kj<frames,s[:,tail:],NEG)],axis=1)
            m=jnp.max(s,-1,keepdims=True)
            p=jnp.exp2(s-m).astype(BF)
            ox=nn(p,vx_ref[...])
            l=ox[:,LANES:]
            outs.append(ox[:,:LANES]/l); lses.append(m+jnp.log2(l))
        sel=lanes<64
        o_ref[r0:r0+BLK,:]=jnp.where(sel,outs[0],outs[1]).astype(BF)
        lse_ref[r0:r0+BLK,:]=jnp.where(sel,lses[0],lses[1])

def cross_fwd(q,kv,frames,heads):
    rows=q.shape[0]; npair=heads//2; kp=kv.shape[0]
    return pl.pallas_call(functools.partial(cross_fwd_kernel,frames),
        grid=(npair,),
        in_specs=[pl.BlockSpec((rows,LANES),lambda p:(0,p)),
                  pl.BlockSpec((kp,LANES),lambda p:(0,p)),
                  pl.BlockSpec((kp,LANES),lambda p:(0,npair+p))],
        out_specs=[pl.BlockSpec((rows,LANES),lambda p:(0,p)),pl.BlockSpec((rows,LANES),lambda p:(0,p))],
        out_shape=[jax.ShapeDtypeStruct((rows,heads*64),BF),jax.ShapeDtypeStruct((rows,heads*64),F32)],
        scratch_shapes=[pltpu.VMEM((kp,LANES),BF),pltpu.VMEM((kp,2*LANES),BF)],
        compiler_params=pltpu.CompilerParams(vmem_limit_bytes=60*2**20),
        cost_estimate=pair_cost(rows*kp*heads,2,8*rows*heads*64+4*kp*heads*64),
        name="cross_fwd",
    )(q,kv,kv)

def split3(x):
    hi=x.astype(BF); r=x-hi.astype(F32); mid=r.astype(BF); lo=(r-mid.astype(F32)).astype(BF)
    return hi,mid,lo

def aug(value,head,lanes,one_lane):
    hi,mid,lo=split3(-value)
    z=jnp.zeros(lanes.shape,F32)
    b=64*head
    x=jnp.where(lanes==b,hi.astype(F32),jnp.where(lanes==b+1,mid.astype(F32),jnp.where(lanes==b+2,lo.astype(F32),z)))
    if one_lane: x=jnp.where(lanes==b+3,1.0,x)
    return x.astype(BF)

def build_q(q,do,o,lse,at,qx_ref,dox_ref,masked):
    lanes=lane_ids(BLK)
    prod=do.astype(F32)*o.astype(F32)
    for h in range(2):
        sel=pick(h,lanes)
        delta=jnp.sum(jnp.where(sel,prod,0.0),-1,keepdims=True)
        qx_ref[h,at,:LANES]=jnp.where(sel,q,jnp.zeros((),BF))
        qx_ref[h,at,LANES:]=aug(lse,h,lanes,masked)
        dox_ref[h,at,:LANES]=jnp.where(sel,do,jnp.zeros((),BF))
        dox_ref[h,at,LANES:]=aug(delta,h,lanes,False)

def build_k(k,v,r0,at,kx_ref,km_ref,vx_ref,frames):
    lanes=lane_ids(BLK)
    low=lanes%64
    ones=jnp.where(low<3,1.0,0.0)
    kones=ones
    if frames is not None and r0+BLK>frames:
        bad=lax.broadcasted_iota(jnp.int32,(BLK,LANES),0)+r0>=frames
        k=jnp.where(bad,jnp.zeros((),BF),k); v=jnp.where(bad,jnp.zeros((),BF),v)
        kones=jnp.where(bad&(low==3),NEG,ones)
    kx_ref[at,:LANES]=k; kx_ref[at,LANES:]=kones.astype(BF)
    vx_ref[at,:LANES]=v; vx_ref[at,LANES:]=ones.astype(BF)
    for h in range(2): km_ref[h,at,:]=jnp.where(pick(h,lanes),k,jnp.zeros((),BF))

def block_back(kx,vx,km,qx,dox,mask):
    s=nt(kx,qx)
    if mask is not None: s=jnp.where(mask,s,NEG)
    p=jnp.exp2(s)
    dp=nt(vx,dox)
    ds=(p*dp).astype(BF)
    pb=p.astype(BF)
    dv=nn(pb,dox[:,:LANES])
    dk=nn(ds,qx[:,:LANES])
    dq=tn(ds,km)
    return dv,dk,dq

def self_bwd_kernel(core_ref,kept_ref,come_ref,do_ref,do_come_ref,o_ref,o_sent_ref,lse_ref,segq_ref,segk_ref,own_ref,sent_ref,
                    qx_ref,dox_ref,kx_ref,km_ref,vx_ref,dqa_ref,dk_ref,dv_ref,dka_ref,dva_ref):
    half=kept_ref.shape[1]; rows=2*half; n=rows//BLK
    core=core_ref[0]
    for ref,d,o,base in zip((kept_ref,come_ref),(do_ref,do_come_ref),(o_ref,o_sent_ref),places(core,half)):
        for r0 in range(0,half,BLK):
            here=slice(r0,r0+BLK); at=rows_at(base,r0,BLK)
            build_q(ref[0,here,:],d[here,:],o[here,:],lse_ref[at,:],at,qx_ref,dox_ref,False)
            build_k(ref[1,here,:],ref[2,here,:],0,at,kx_ref,km_ref,vx_ref,None)
    dqa_ref[...]=jnp.zeros_like(dqa_ref)
    tri=lax.broadcasted_iota(jnp.int32,(BLK,BLK),0)<=lax.broadcasted_iota(jnp.int32,(BLK,BLK),1)
    def pair(j,i,mask,first):
        kr=pl.ds(pl.multiple_of(j*BLK,BLK),BLK); qr=pl.ds(pl.multiple_of(i*BLK,BLK),BLK)
        r=[block_back(kx_ref[kr,:],vx_ref[kr,:],km_ref[h,kr,:],qx_ref[h,qr,:],dox_ref[h,qr,:],mask) for h in range(2)]
        dv=r[0][0]+r[1][0]; dk=r[0][1]+r[1][1]; dq=r[0][2]+r[1][2]
        if first: dva_ref[...]=dv; dka_ref[...]=dk
        else: dva_ref[...]+=dv; dka_ref[...]+=dk
        dqa_ref[qr,:]+=dq
    def flush(j):
        kr=pl.ds(pl.multiple_of(j*BLK,BLK),BLK)
        dk_ref[kr,:]=(dka_ref[...]*(1/LOG2E)).astype(BF)
        dv_ref[kr,:]=dva_ref[...].astype(BF)
    def outer_prompt(j,_):
        pair(j,j,tri,True)
        def inner(i,_): pair(j,i,None,False); return 0
        lax.fori_loop(j+1,n,inner,0)
        flush(j); return 0
    lax.fori_loop(0,n//2,outer_prompt,0)
    def segmask(j,i):
        sk=segk_ref[pl.ds(pl.multiple_of(j*BLK-half,BLK),BLK),:]
        sq=segq_ref[i-n//2]
        return sk==sq
    def outer_cont(j,_):
        pair(j,j,tri&segmask(j,j),True)
        def inner(i,_): pair(j,i,segmask(j,i),False); return 0
        lax.fori_loop(j+1,n,inner,0)
        flush(j); return 0
    lax.fori_loop(n//2,n,outer_cont,0)
    for ref,base in zip((own_ref,sent_ref),places(core,half)):
        at=rows_at(base,0,half)
        ref[0]=(dqa_ref[at,:]*0.125).astype(BF)
        ref[1]=dk_ref[at,:]
        ref[2]=dv_ref[at,:]

def self_bwd(core,kept,come,do,do_come,o,o_sent,lse,segq,segk):
    half,part=kept.shape[1:]; rows=2*half
    three=pl.BlockSpec((3,half,LANES),lambda p:(0,0,p))
    one=pl.BlockSpec((half,LANES),lambda p:(0,p))
    out=jax.ShapeDtypeStruct((3,half,part),BF)
    n=rows//BLK
    return pl.pallas_call(self_bwd_kernel,
        grid=(part//LANES,),
        in_specs=[scalar(),three,three,one,one,one,one,pl.BlockSpec((rows,LANES),lambda p:(0,p)),
                  pl.BlockSpec(segq.shape,lambda p:(0,0,0)),pl.BlockSpec(segk.shape,lambda p:(0,0))],
        out_specs=[three,three],
        out_shape=[out,out],
        scratch_shapes=[pltpu.VMEM((2,rows,2*LANES),BF),pltpu.VMEM((2,rows,2*LANES),BF),pltpu.VMEM((rows,2*LANES),BF),
                        pltpu.VMEM((2,rows,LANES),BF),pltpu.VMEM((rows,2*LANES),BF),pltpu.VMEM((rows,LANES),F32),
                        pltpu.VMEM((rows,LANES),BF),pltpu.VMEM((rows,LANES),BF),
                        pltpu.VMEM((BLK,LANES),F32),pltpu.VMEM((BLK,LANES),F32)],
        compiler_params=pltpu.CompilerParams(vmem_limit_bytes=60*2**20),
        cost_estimate=pair_cost(n*(n+1)//2*BLK*BLK*(part//HEAD),5,20*rows*part),
        name="self_bwd",
    )(core,kept,come,do,do_come,o,o_sent,lse,segq,segk)

def cross_bwd_kernel(frames,q_ref,k_ref,v_ref,do_ref,o_ref,lse_ref,dq_ref,dk_ref,dv_ref,
                     qx_ref,dox_ref,kx_ref,km_ref,vx_ref,dqa_ref,dka_ref,dva_ref):
    rows=q_ref.shape[0]; n=rows//BLK; kp=k_ref.shape[0]; nk=kp//BLK
    for r0 in range(0,rows,BLK):
        at=slice(r0,r0+BLK)
        build_q(q_ref[at,:],do_ref[at,:],o_ref[at,:],lse_ref[at,:],at,qx_ref,dox_ref,True)
    for r0 in range(0,kp,BLK):
        at=slice(r0,r0+BLK)
        build_k(k_ref[at,:],v_ref[at,:],r0,at,kx_ref,km_ref,vx_ref,frames)
    dqa_ref[...]=jnp.zeros_like(dqa_ref)
    def outer(j,_):
        kr=pl.ds(pl.multiple_of(j*BLK,BLK),BLK)
        dva=None
        for i in range(n):
            qr=slice(i*BLK,(i+1)*BLK)
            r=[block_back(kx_ref[kr,:],vx_ref[kr,:],km_ref[h,kr,:],qx_ref[h,qr,:],dox_ref[h,qr,:],None) for h in range(2)]
            dv=r[0][0]+r[1][0]; dk=r[0][1]+r[1][1]; dq=r[0][2]+r[1][2]
            if i==0: dva_ref[...]=dv; dka_ref[...]=dk
            else: dva_ref[...]+=dv; dka_ref[...]+=dk
            dqa_ref[qr,:]+=dq
        dk_ref[kr,:]=(dka_ref[...]*(1/LOG2E)).astype(BF)
        dv_ref[kr,:]=dva_ref[...].astype(BF)
        return 0
    lax.fori_loop(0,nk,outer,0)
    dq_ref[...]=(dqa_ref[...]*0.125).astype(BF)

def cross_bwd(q,kv,frames,do,o,lse,heads):
    rows=q.shape[0]; npair=heads//2; kp=kv.shape[0]
    big=lambda f:pl.BlockSpec((rows,LANES),f)
    kb=lambda f:pl.BlockSpec((kp,LANES),f)
    return pl.pallas_call(functools.partial(cross_bwd_kernel,frames),
        grid=(npair,),
        in_specs=[big(lambda p:(0,p)),kb(lambda p:(0,p)),kb(lambda p:(0,npair+p)),big(lambda p:(0,p)),big(lambda p:(0,p)),big(lambda p:(0,p))],
        out_specs=[big(lambda p:(0,p)),kb(lambda p:(0,p)),kb(lambda p:(0,p))],
        out_shape=[jax.ShapeDtypeStruct((rows,heads*64),BF),jax.ShapeDtypeStruct((kp,heads*64),BF),jax.ShapeDtypeStruct((kp,heads*64),BF)],
        scratch_shapes=[pltpu.VMEM((2,rows,2*LANES),BF),pltpu.VMEM((2,rows,2*LANES),BF),pltpu.VMEM((kp,2*LANES),BF),
                        pltpu.VMEM((2,kp,LANES),BF),pltpu.VMEM((kp,2*LANES),BF),pltpu.VMEM((rows,LANES),F32),
                        pltpu.VMEM((BLK,LANES),F32),pltpu.VMEM((BLK,LANES),F32)],
        compiler_params=pltpu.CompilerParams(vmem_limit_bytes=60*2**20),
        cost_estimate=pair_cost(rows*kp*heads,5,12*rows*heads*64+8*kp*heads*64),
        name="cross_bwd",
    )(q,kv,kv,do,o,lse)


EPSILON = 1e-05
ROWS = 256
BIG = 60 * 2**20


def whole(shape):
    return pl.BlockSpec(shape, lambda *_: (0,) * len(shape), pipeline_mode=pl.Buffered(1))


def by_rows(*lead_and_cols):
    *lead, cols = lead_and_cols
    return pl.BlockSpec((*lead, ROWS, cols), lambda i: (0,) * len(lead) + (i, 0))


def shaped(shape, dtype):
    return jax.ShapeDtypeStruct(shape, dtype)


def cost(flops, nbytes, trans=0):
    return pl.CostEstimate(flops=int(flops), bytes_accessed=int(nbytes), transcendentals=int(trans))


def normalize(values):
    centre = values - jnp.mean(values, -1, keepdims=True)
    scale = lax.rsqrt(jnp.mean(centre * centre, -1, keepdims=True) + EPSILON)
    return centre * scale, scale


def norm_grad(normed, scale, gain, grad):
    weighted = grad * gain
    return scale * (weighted - jnp.mean(weighted, -1, keepdims=True)
                    - normed * jnp.mean(weighted * normed, -1, keepdims=True))


def accumulate(ref, value):
    @pl.when(pl.program_id(0) == 0)
    def _():
        ref[...] = value

    @pl.when(pl.program_id(0) > 0)
    def _():
        ref[...] += value


def column_sum(values):
    return jnp.sum(values, 0, keepdims=True)


def qkv_kernel(core_ref, x_ref, w_ref, gain_ref, shift_ref, bias_ref, norm_ref, kept_ref, sent_ref):
    part = kept_ref.shape[2]
    normed, _ = normalize(x_ref[...].astype(F32))
    low = (normed * gain_ref[0:1] + shift_ref[0:1]).astype(BF)
    norm_ref[...] = low
    core = core_ref[0]
    for out_ref, at in ((kept_ref, core), (sent_ref, 1 - core)):
        cols = nn(low, w_ref[at])
        out_ref[0] = ((cols[:, :part] + bias_ref[at, 0:1]) * (HEAD ** -0.5 * LOG2E)).astype(BF)
        out_ref[1] = cols[:, part:2 * part].astype(BF)
        out_ref[2] = (cols[:, 2 * part:] + bias_ref[at, 1:2]).astype(BF)


def qkv_project(core, x, w, gain, shift, bias):
    rows, width = x.shape
    part = width // 2
    out = shaped((3, rows, part), BF)
    return pl.pallas_call(
        qkv_kernel, grid=(rows // ROWS,),
        in_specs=[scalar(), by_rows(width), whole(w.shape), whole(gain.shape), whole(shift.shape), whole(bias.shape)],
        out_specs=[by_rows(width), by_rows(3, part), by_rows(3, part)],
        out_shape=[shaped((rows, width), BF), out, out],
        compiler_params=pltpu.CompilerParams(vmem_limit_bytes=BIG),
        cost_estimate=cost(6 * rows * width * width, 2 * (3 * width * width + 6 * rows * width)), name="qkv_project",
    )(core, x, w, gain, shift, bias)


def memory_kernel(frames, mine_ref, own_ref, come_ref, w_ref, bias_ref, kv_ref, mem_ref):
    width = own_ref.shape[1]
    part = width // 2
    mem = jnp.where(mine_ref[0] == 1, own_ref[...], come_ref[...])
    row = lax.broadcasted_iota(jnp.int32, mem.shape, 0) + pl.program_id(0) * ROWS
    mem = jnp.where(row < frames, mem, jnp.zeros((), BF))
    mem_ref[...] = mem
    for t in range(2):
        cols = nn(mem, w_ref[t])
        kv_ref[:, t * part:(t + 1) * part] = cols[:, :part].astype(BF)
        kv_ref[:, width + t * part:width + (t + 1) * part] = (cols[:, part:] + bias_ref[4:5, t * part:(t + 1) * part]).astype(BF)


def memory_project(mine, own, come, w_mid, bias):
    frames, width = own.shape
    steps = pl.cdiv(frames, ROWS)
    return pl.pallas_call(
        functools.partial(memory_kernel, frames), grid=(steps,),
        in_specs=[scalar(), by_rows(width), by_rows(width),
                  pl.BlockSpec((2, width, width), lambda i: (0, 0, 1), pipeline_mode=pl.Buffered(1)), whole(bias.shape)],
        out_specs=[by_rows(2 * width), by_rows(width)],
        out_shape=[shaped((steps * ROWS, 2 * width), BF), shaped((steps * ROWS, width), BF)],
        compiler_params=pltpu.CompilerParams(vmem_limit_bytes=BIG),
        cost_estimate=cost(4 * frames * width * width, 2 * (2 * width * width + 5 * frames * width)), name="memory_project",
    )(mine, own, come, w_mid, bias)


def middle_kernel(core_ref, x_ref, own_ref, come_ref, wo_ref, wq_ref, gain_ref, shift_ref, bias_ref,
                  resid_ref, norm_ref, q_ref):
    part = own_ref.shape[1]
    core = core_ref[0]
    resid = x_ref[...].astype(F32) + nt(own_ref[...], wo_ref[core]) + nt(come_ref[...], wo_ref[1 - core]) + bias_ref[2:3]
    resid_ref[...] = resid
    normed, _ = normalize(resid)
    low = (normed * gain_ref[1:2] + shift_ref[1:2]).astype(BF)
    norm_ref[...] = low
    for t in range(2):
        at = slice(t * part, (t + 1) * part)
        q_ref[:, at] = ((nn(low, wq_ref[t]) + bias_ref[3:4, at]) * (HEAD ** -0.5 * LOG2E)).astype(BF)


def middle(core, x, own, come, w_mid, gain, shift, bias):
    rows, width = x.shape
    part = width // 2
    w_at = lambda c: pl.BlockSpec((2, width, part), lambda i: (0, 0, c), pipeline_mode=pl.Buffered(1))
    return pl.pallas_call(
        middle_kernel, grid=(rows // ROWS,),
        in_specs=[scalar(), by_rows(width), by_rows(part), by_rows(part), w_at(0), w_at(1),
                  whole(gain.shape), whole(shift.shape), whole(bias.shape)],
        out_specs=[by_rows(width)] * 3,
        out_shape=[shaped((rows, width), F32), shaped((rows, width), BF), shaped((rows, width), BF)],
        compiler_params=pltpu.CompilerParams(vmem_limit_bytes=BIG),
        cost_estimate=cost(4 * rows * width * width, 4 * width * width + 12 * rows * width), name="middle",
    )(core, x, own, come, w_mid, w_mid, gain, shift, bias)


def gelu_parts(v):
    z = jnp.abs(v) * (0.5 ** 0.5)
    t = 1.0 / (1.0 + 0.3275911 * z)
    bell = jnp.exp2(v * v * (-0.5 * LOG2E))
    poly = ((((1.061405429 * t - 1.453152027) * t + 1.421413741) * t - 0.284496736) * t + 0.254829592) * t
    tail = (0.5 * poly) * bell
    phi = jnp.where(v >= 0, 1.0 - tail, tail)
    return phi, phi + v * bell * 0.3989422804014327


def feed_kernel(attn_ref, resid_ref, g_ref, wo_ref, wi_ref, wm_ref, gain_ref, shift_ref, bias_ref, unit_bias_ref, out_bias_ref,
                out_ref, norm_ref, hidden_ref, dpre_ref, g2_ref, dattn_ref,
                sum_g_ref, sum_dpre_ref, sum_g2_ref, sum_gain_ref, sum_shift_ref):
    part = wo_ref.shape[2]
    units = wi_ref.shape[2]
    resid = resid_ref[...] + bias_ref[5:6]
    for t in range(2):
        resid = resid + nt(attn_ref[:, t * part:(t + 1) * part], wo_ref[t])
    normed, scale = normalize(resid)
    low = (normed * gain_ref[2:3] + shift_ref[2:3]).astype(BF)
    norm_ref[...] = low
    g_low = g_ref[...]
    out = resid + out_bias_ref[...]
    back = jnp.zeros_like(resid)
    sums = []
    for t in range(2):
        at = slice(t * units, (t + 1) * units)
        pre = nn(low, wi_ref[t]) + unit_bias_ref[:, at]
        phi, slope = gelu_parts(pre)
        hidden = (pre * phi).astype(BF)
        hidden_ref[:, at] = hidden
        out = out + nt(hidden, wm_ref[t])
        dpre = nn(g_low, wm_ref[t]) * slope
        sums.append(column_sum(dpre))
        dpre = dpre.astype(BF)
        dpre_ref[:, at] = dpre
        back = back + nt(dpre, wi_ref[t])
    out_ref[...] = out.astype(BF)
    sums = jnp.concatenate(sums, 1)
    wide = sum_dpre_ref.shape[1]
    accumulate(sum_dpre_ref, jnp.concatenate([sums[:, i * wide:(i + 1) * wide] for i in range(sum_dpre_ref.shape[0])], 0))
    g = g_low.astype(F32)
    accumulate(sum_g_ref, column_sum(g))
    accumulate(sum_gain_ref, column_sum(back * normed))
    accumulate(sum_shift_ref, column_sum(back))
    g2 = g + norm_grad(normed, scale, gain_ref[2:3], back)
    accumulate(sum_g2_ref, column_sum(g2))
    g2_ref[...] = g2
    g2_low = g2.astype(BF)
    for t in range(2):
        dattn_ref[:, t * part:(t + 1) * part] = nn(g2_low, wo_ref[t]).astype(BF)


def feed(attn, resid, g, w_mid, w_ff, gain, shift, bias, unit_bias, out_bias):
    rows, width = resid.shape
    part = width // 2
    units = w_ff.shape[2] // 2
    w_at = lambda cols, c: pl.BlockSpec((2, width, cols), lambda i: (0, 0, c), pipeline_mode=pl.Buffered(1))
    line = lambda count: (pl.BlockSpec((count, width), lambda i: (0, 0)), shaped((count, width), F32))
    lines = [line(1), line(2 * units // width), line(1), line(1), line(1)]
    return pl.pallas_call(
        feed_kernel, grid=(rows // ROWS,),
        in_specs=[by_rows(width), by_rows(width), by_rows(width), w_at(part, 4), w_at(units, 0), w_at(units, 1),
                  whole(gain.shape), whole(shift.shape), whole(bias.shape), whole(unit_bias.shape), whole(out_bias.shape)],
        out_specs=[by_rows(width), by_rows(width), by_rows(2 * units), by_rows(2 * units), by_rows(width), by_rows(width)] + [a for a, _ in lines],
        out_shape=[shaped((rows, width), BF), shaped((rows, width), BF), shaped((rows, 2 * units), BF), shaped((rows, 2 * units), BF),
                   shaped((rows, width), F32), shaped((rows, width), BF)] + [b for _, b in lines],
        compiler_params=pltpu.CompilerParams(vmem_limit_bytes=BIG),
        cost_estimate=cost(2 * rows * width * (2 * width + 8 * units), 2 * width * (width + 4 * units) + 2 * rows * (8 * width + 4 * units), 4 * rows * units),
        name="feed",
    )(attn, resid, g, w_mid, w_ff, w_ff, gain, shift, bias, unit_bias, out_bias)


def feed_weights_kernel(norm_ref, g_ref, dpre_ref, hidden_ref, out_ref):
    cols = dpre_ref.shape[1]
    out_ref[0, :, :cols] = tn(norm_ref[...], dpre_ref[...]).astype(BF)
    out_ref[0, :, cols:] = tn(g_ref[...], hidden_ref[...]).astype(BF)


def feed_weights(norm, g, dpre, hidden):
    rows, width = norm.shape
    units = dpre.shape[1] // 2
    cols = units // 2
    return pl.pallas_call(
        feed_weights_kernel, grid=(2, 2),
        in_specs=[whole(norm.shape), whole(g.shape), pl.BlockSpec((rows, cols), lambda t, c: (0, 2 * t + c)),
                  pl.BlockSpec((rows, cols), lambda t, c: (0, 2 * t + c))],
        out_specs=pl.BlockSpec((1, width, 2 * cols), lambda t, c: (t, 0, c)),
        out_shape=shaped((2, width, 2 * units), BF),
        compiler_params=pltpu.CompilerParams(vmem_limit_bytes=BIG),
        cost_estimate=cost(8 * rows * width * units, 2 * (4 * width * units + 4 * rows * units)), name="feed_weights",
    )(norm, g, dpre, hidden)


def middle_back_kernel(core_ref, dq_ref, resid_ref, g2_ref, wq_ref, wo_ref, gain_ref,
                       g1_ref, kept_ref, sent_ref, sum_dq_ref, sum_g1_ref, sum_gain_ref, sum_shift_ref):
    part = kept_ref.shape[1]
    core = core_ref[0]
    dq = dq_ref[...]
    back = nt(dq[:, :part], wq_ref[0]) + nt(dq[:, part:], wq_ref[1])
    accumulate(sum_dq_ref, column_sum(dq.astype(F32)))
    normed, scale = normalize(resid_ref[...])
    accumulate(sum_gain_ref, column_sum(back * normed))
    accumulate(sum_shift_ref, column_sum(back))
    g1 = g2_ref[...] + norm_grad(normed, scale, gain_ref[1:2], back)
    g1_ref[...] = g1
    accumulate(sum_g1_ref, column_sum(g1))
    low = g1.astype(BF)
    kept_ref[...] = nn(low, wo_ref[core]).astype(BF)
    sent_ref[...] = nn(low, wo_ref[1 - core]).astype(BF)


def middle_back(core, dq, resid, g2, w_mid, gain):
    rows, width = resid.shape
    part = width // 2
    w_at = lambda c: pl.BlockSpec((2, width, part), lambda i: (0, 0, c), pipeline_mode=pl.Buffered(1))
    line = pl.BlockSpec((1, width), lambda i: (0, 0))
    return pl.pallas_call(
        middle_back_kernel, grid=(rows // ROWS,),
        in_specs=[scalar(), by_rows(width), by_rows(width), by_rows(width), w_at(1), w_at(0), whole(gain.shape)],
        out_specs=[by_rows(width), by_rows(part), by_rows(part)] + [line] * 4,
        out_shape=[shaped((rows, width), F32), shaped((rows, part), BF), shaped((rows, part), BF)] + [shaped((1, width), F32)] * 4,
        compiler_params=pltpu.CompilerParams(vmem_limit_bytes=BIG),
        cost_estimate=cost(4 * rows * width * width, 4 * width * width + 18 * rows * width), name="middle_back",
    )(core, dq, resid, g2, w_mid, w_mid, gain)


def middle_weights_kernel(core_ref, g1_ref, own_ref, come_ref, norm_ref, dq_ref, mem_ref, dk_ref, dv_ref, g2_ref, attn_ref,
                          out_ref, sum_dv_ref):
    part = own_ref.shape[1]
    attn_self = jnp.where(pl.program_id(0) == core_ref[0], own_ref[...], come_ref[...])
    out_ref[0, :, :part] = tn(g1_ref[...].astype(BF), attn_self).astype(BF)
    out_ref[0, :, part:2 * part] = tn(norm_ref[...], dq_ref[...]).astype(BF)
    mem = mem_ref[...]
    out_ref[0, :, 2 * part:3 * part] = tn(mem, dk_ref[...]).astype(BF)
    out_ref[0, :, 3 * part:4 * part] = tn(mem, dv_ref[...]).astype(BF)
    out_ref[0, :, 4 * part:] = tn(g2_ref[...].astype(BF), attn_ref[...]).astype(BF)
    sum_dv_ref[...] = column_sum(dv_ref[...].astype(F32))


def middle_weights(core, g1, own, come, norm, dq, mem, dk, dv, g2, attn):
    rows, width = norm.shape
    frames = mem.shape[0]
    part = width // 2
    half = lambda n: pl.BlockSpec((n, part), lambda t: (0, t))
    return pl.pallas_call(
        middle_weights_kernel, grid=(2,),
        in_specs=[scalar(), whole(g1.shape), whole(own.shape), whole(come.shape), whole(norm.shape), half(rows), whole(mem.shape),
                  half(frames), half(frames), whole(g2.shape), half(rows)],
        out_specs=[pl.BlockSpec((1, width, 5 * part), lambda t: (t, 0, 0)), pl.BlockSpec((1, part), lambda t: (0, t))],
        out_shape=[shaped((2, width, 5 * part), BF), shaped((1, width), F32)],
        compiler_params=pltpu.CompilerParams(vmem_limit_bytes=BIG),
        cost_estimate=cost(2 * width * width * (3 * rows + 2 * frames), 10 * width * width + 2 * width * (10 * rows + 3 * frames)),
        name="middle_weights",
    )(core, g1, own, come, norm, dq, mem, dk, dv, g2, attn)


def qkv_back_kernel(core_ref, own_ref, come_ref, x_ref, g1_ref, w_ref, gain_ref, grad_ref, sum_gain_ref, sum_shift_ref):
    part = own_ref.shape[2]
    core = core_ref[0]
    back = jnp.zeros(x_ref.shape, F32)
    for ref, at in ((own_ref, core), (come_ref, 1 - core)):
        for j in range(3):
            back = back + nt(ref[j], w_ref[at, :, j * part:(j + 1) * part])
    normed, scale = normalize(x_ref[...].astype(F32))
    accumulate(sum_gain_ref, column_sum(back * normed))
    accumulate(sum_shift_ref, column_sum(back))
    grad_ref[...] = (g1_ref[...] + norm_grad(normed, scale, gain_ref[0:1], back)).astype(BF)


def qkv_back(core, own, come, x, g1, w, gain):
    rows, width = x.shape
    part = width // 2
    line = pl.BlockSpec((1, width), lambda i: (0, 0))
    return pl.pallas_call(
        qkv_back_kernel, grid=(rows // ROWS,),
        in_specs=[scalar(), by_rows(3, part), by_rows(3, part), by_rows(width), by_rows(width), whole(w.shape), whole(gain.shape)],
        out_specs=[by_rows(width), line, line],
        out_shape=[shaped((rows, width), BF), shaped((1, width), F32), shaped((1, width), F32)],
        compiler_params=pltpu.CompilerParams(vmem_limit_bytes=BIG),
        cost_estimate=cost(6 * rows * width * width, 2 * (3 * width * width + 7 * rows * width)), name="qkv_back",
    )(core, own, come, x, g1, w, gain)


def qkv_weights_kernel(core_ref, norm_ref, own_ref, come_ref, out_ref, sum_q_ref, sum_v_ref):
    part = own_ref.shape[2]
    mine = pl.program_id(0) == core_ref[0]
    norm = norm_ref[...]
    for j in range(3):
        grad = jnp.where(mine, own_ref[j], come_ref[j])
        out_ref[0, :, j * part:(j + 1) * part] = tn(norm, grad).astype(BF)
        if j != 1:
            (sum_q_ref if j == 0 else sum_v_ref)[...] = column_sum(grad.astype(F32))


def qkv_weights(core, norm, own, come):
    rows, width = norm.shape
    part = width // 2
    return pl.pallas_call(
        qkv_weights_kernel, grid=(2,),
        in_specs=[scalar(), whole(norm.shape), whole(own.shape), whole(come.shape)],
        out_specs=[pl.BlockSpec((1, width, 3 * part), lambda t: (t, 0, 0)), pl.BlockSpec((1, part), lambda t: (0, t)), pl.BlockSpec((1, part), lambda t: (0, t))],
        out_shape=[shaped((2, width, 3 * part), BF), shaped((1, width), F32), shaped((1, width), F32)],
        compiler_params=pltpu.CompilerParams(vmem_limit_bytes=BIG),
        cost_estimate=cost(6 * rows * width * width, 2 * (3 * width * width + 4 * rows * width)), name="qkv_weights",
    )(core, norm, own, come)


def bit_names(chips):
    return ["t"] + ["k%d" % b for b in reversed(range((chips - 1).bit_length()))] + ["core"]


def my_bit(name):
    if name == "t":
        return lax.axis_index("tensor")
    if name == "core":
        return lax.axis_index("core")
    return lax.axis_index("chip") // 2 ** int(name[1:]) % 2


def partner(name):
    bit = my_bit(name)
    if name == "t":
        return {"tensor": 1 - bit}
    if name == "core":
        return {"core": 1 - bit}
    return {"chip": lax.axis_index("chip") + 2 ** int(name[1:]) * (1 - 2 * bit)}


def greet(names):
    barrier = pltpu.get_barrier_semaphore()
    for name in names:
        pl.semaphore_signal(barrier, inc=1, device_id=partner(name), device_id_type=pl.DeviceIdType.MESH)
    pl.semaphore_wait(barrier, len(names))


def exchange_orders(names):
    low = [n for n in reversed(names) if n[0] == "k"]
    return [["core", "t"] + low, ["core"] + low + ["t"], ["core"] + low[1:] + ["t"] + low[:1]]


def stream_cols(cols, count):
    tiles = cols // LANES
    cuts = [tiles * i // count * LANES for i in range(count + 1)]
    return [slice(a, b) for a, b in zip(cuts, cuts[1:])]


def gather_kernel(names, orders, own_ref, out_ref, local_sem, send_sem, recv_sem):
    greet(names)
    lanes = stream_cols(own_ref.shape[1], len(orders))
    place = tuple(my_bit(n) for n in names)
    local = pltpu.make_async_copy(own_ref, out_ref.at[place], local_sem)
    local.start()
    known = [[] for _ in orders]
    sent = []
    flying = [None] * len(orders)

    def start(st, step):
        name = orders[st][step]
        at = tuple(slice(None) if n in known[st] else my_bit(n) for n in names)
        dst = out_ref.at[at + (slice(None), lanes[st])]
        src = dst if step else own_ref.at[:, lanes[st]]
        copy = pltpu.make_async_remote_copy(src, dst, send_sem.at[st, step], recv_sem.at[st, step],
                                            device_id=partner(name), device_id_type=pl.DeviceIdType.MESH)
        copy.start()
        known[st].append(name)
        sent.append(copy)
        flying[st] = copy

    for st in range(len(orders)):
        start(st, 0)
    local.wait()
    for step in range(len(names)):
        for st in range(len(orders)):
            flying[st].wait_recv()
            if step + 1 < len(names):
                start(st, step + 1)
    for copy in sent:
        copy.wait_send()


def gather_all(shard, chips):
    names = bit_names(chips)
    orders = [list(reversed(o)) for o in exchange_orders(names)]
    rows, cols = shard.shape
    dma = pltpu.SemaphoreType.DMA
    full = pl.pallas_call(
        functools.partial(gather_kernel, names, orders),
        in_specs=[pl.BlockSpec(memory_space=pl.ANY)], out_specs=pl.BlockSpec(memory_space=pl.ANY),
        out_shape=shaped((2,) * len(names) + (rows, cols), shard.dtype),
        scratch_shapes=[dma, dma((len(orders), len(names))), dma((len(orders), len(names)))],
        compiler_params=pltpu.CompilerParams(collective_id=0, has_side_effects=True, vmem_limit_bytes=BIG),
        cost_estimate=cost(0, 100e6), name="gather_all",
    )(shard)
    return full.reshape(2, -1, cols)


def sum_kernel(names, orders, parts, grad_ref, *refs):
    small_refs, (out_ref, small_out_ref), scratch = refs[:parts], refs[parts:parts + 2], refs[parts + 2:]
    greet(names)
    count, steps = len(orders), len(names)
    recv = [scratch[st * steps:(st + 1) * steps] for st in range(count)]
    held = [scratch[(count + st) * steps:(count + st + 1) * steps] for st in range(count)]
    small_recv, small_held, send_sem, recv_sem = scratch[2 * count * steps:]
    lanes = stream_cols(grad_ref.shape[-1], count)
    left = [list(names) for _ in orders]
    here = [grad_ref.at[(slice(None),) * (steps + 1) + (lanes[st],)] for st in range(count)]
    sent = []
    flying = [None] * (count + 1)

    def start(st, step):
        name = orders[st][step] if st < count else orders[0][step]
        if st < count:
            src = here[st].at[tuple(1 - my_bit(n) if n == name else slice(None) for n in left[st])]
            dst = recv[st][step]
        else:
            src = small_held.at[step]
            dst = small_recv.at[step]
        copy = pltpu.make_async_remote_copy(src, dst, send_sem.at[st, step], recv_sem.at[st, step],
                                            device_id=partner(name), device_id_type=pl.DeviceIdType.MESH)
        copy.start()
        sent.append(copy)
        flying[st] = copy

    for st in range(count):
        start(st, 0)
    row = 0
    for ref in small_refs:
        small_held[0, row:row + ref.shape[0]] = ref[...]
        row += ref.shape[0]
    small_held[0, row:] = jnp.zeros((small_held.shape[1] - row, small_held.shape[2]), F32)
    start(count, 0)
    for step in range(steps):
        for st in range(count):
            name = orders[st][step]
            flying[st].wait_recv()
            at = tuple(my_bit(n) if n == name else slice(None) for n in left[st])
            kept = here[st].at[at]
            total = kept[...].astype(F32) + recv[st][step][...].astype(F32)
            if step + 1 < steps:
                held[st][step][...] = total.astype(BF)
                here[st] = held[st][step]
                left[st].remove(name)
                start(st, step + 1)
            else:
                out_ref[:, lanes[st]] = total
        flying[count].wait_recv()
        total = small_held[step] + small_recv[step]
        if step + 1 < steps:
            small_held[step + 1] = total
            start(count, step + 1)
        else:
            small_out_ref[...] = total
    for copy in sent:
        copy.wait_send()


def sum_all(grad, small, chips):
    names = bit_names(chips)
    orders = exchange_orders(names)
    cols = grad.shape[2]
    rows = grad.shape[1] // (2 * chips)
    steps = len(names)
    bufs = [pltpu.VMEM((2,) * (steps - 1 - step) + (rows, lane.stop - lane.start), BF)
            for lane in stream_cols(cols, len(orders)) for step in range(steps)]
    small_rows = (sum(s.shape[0] for s in small) + 7) // 8 * 8
    small_shape = (small_rows, small[0].shape[1])
    dma = pltpu.SemaphoreType.DMA
    vmem = pl.BlockSpec(memory_space=pltpu.VMEM)
    return pl.pallas_call(
        functools.partial(sum_kernel, names, orders, len(small)),
        in_specs=[vmem] * (1 + len(small)), out_specs=[vmem, vmem],
        out_shape=[shaped((rows, cols), F32), shaped(small_shape, F32)],
        scratch_shapes=bufs + bufs + [pltpu.VMEM((steps,) + small_shape, F32), pltpu.VMEM((steps,) + small_shape, F32),
                                      dma((len(orders) + 1, steps)), dma((len(orders) + 1, steps))],
        compiler_params=pltpu.CompilerParams(collective_id=1, has_side_effects=True, vmem_limit_bytes=BIG),
        cost_estimate=cost(0, 100e6), name="sum_all",
    )(grad.reshape((2,) * steps + (rows, cols)), *small)


ALL = ("tensor", "chip", "core")


def fetch(shard):
    full = lax.all_gather(shard, ALL, axis=0, tiled=True)
    return full.reshape(2, -1, shard.shape[1])


def spread_sum(grad):
    return lax.psum_scatter(grad.reshape(-1, grad.shape[2]), ALL, scatter_dimension=0, tiled=True)


def on_device(tokens, memory, seg_ids, positions, grad_output, attn_in, attn_out, cross_q, cross_kv,
              cross_out, mlp_in, mlp_out, norm_gain, norm_bias, proj_bias, mlp_bias, out_bias):
    width = tokens.shape[1]
    rows_here, _, part = attn_in.shape
    units = mlp_in.shape[1]
    heads = width // HEAD
    frames = memory.shape[1]
    core = lax.axis_index("core")
    tensor = lax.axis_index("tensor")
    core_at = core.astype(jnp.int32).reshape(1)
    swap = [(0, 0), (1, 2), (2, 1), (3, 3)]
    fix = lambda x: lax.ppermute(x, ("core", "tensor"), swap)
    other = lambda x: lax.ppermute(x, "core", [(0, 1), (1, 0)])

    chips = lax.axis_size("chip")
    first, mid, last = lax.optimization_barrier((
        attn_in.reshape(rows_here, 3 * part),
        jnp.concatenate([attn_out.T, cross_q, cross_kv.reshape(rows_here, 2 * part), cross_out.T], 1),
        jnp.concatenate([mlp_in, mlp_out.T], 1)))
    moved = fix(tokens)
    w_mid = fetch(mid)
    w_ff = fetch(last)
    w_qkv = gather_all(first, chips)
    grad_in = fix(grad_output)
    seg_mine = fix(seg_ids)
    seg_cont = jnp.where(core == 1, seg_mine, other(seg_mine))
    mem_come = other(memory[0])
    bias_halves = proj_bias[:2].reshape(2, 2, part).transpose(1, 0, 2)

    norm_one, kept, sent = qkv_project(core_at, moved, w_qkv, norm_gain, norm_bias, bias_halves)
    come = other(sent)
    kv, mem = memory_project((core == tensor).astype(jnp.int32).reshape(1), memory[0], mem_come, w_mid, proj_bias)
    o_kept, o_sent, lse_self = self_fwd(core_at, kept, come, seg_cont[:, None], seg_cont[None, :])
    o_come = other(o_sent)
    resid_one, norm_two, q_cross = middle(core_at, moved, o_kept, o_come, w_mid, norm_gain, norm_bias, proj_bias)
    attn_cross, lse_cross = cross_fwd(q_cross, kv, frames, heads)
    (out, norm_three, hidden, dpre, g_two, dattn, sum_g, sum_dpre, sum_g_two, gain_three, shift_three) = feed(
        attn_cross, resid_one, grad_in, w_mid, w_ff, norm_gain, norm_bias, proj_bias, mlp_bias[None], out_bias[None])
    output = fix(out)
    gw_ff = feed_weights(norm_three, grad_in, dpre, hidden)
    dattn, gw_ff = lax.optimization_barrier((dattn, gw_ff))
    g_ff = spread_sum(gw_ff)
    dq, dk, dv = cross_bwd(q_cross, kv, frames, dattn, attn_cross, lse_cross, heads)
    g_one, do_kept, do_sent, sum_dq, sum_g_one, gain_two, shift_two = middle_back(core_at, dq, resid_one, g_two, w_mid, norm_gain)
    do_come = other(do_sent)
    gw_mid, sum_dv = middle_weights(core_at, g_one, o_kept, o_come, norm_two, dq, mem, dk, dv, g_two, attn_cross)
    do_kept, gw_mid = lax.optimization_barrier((do_kept, gw_mid))
    g_mid = spread_sum(gw_mid)
    d_kept, d_sent = self_bwd(core_at, kept, come, do_kept, do_come, o_kept, o_sent, lse_self,
                              seg_cont.reshape(-1, 1, BLK), seg_cont[:, None])
    d_kept, d_sent, g_ff, output = lax.optimization_barrier((d_kept, d_sent, g_ff, output))
    d_come = other(d_sent)
    grad_low, gain_one, shift_one = qkv_back(core_at, d_kept, d_come, moved, g_one, w_qkv, norm_gain)
    grad_low, d_kept, d_come = lax.optimization_barrier((grad_low, d_kept, d_come))
    grad_tokens = fix(grad_low).astype(F32)
    gw_qkv, sum_q, sum_v = qkv_weights(core_at, norm_one, d_kept, d_come)
    g_qkv, sums = sum_all(gw_qkv, [gain_one, gain_two, gain_three, shift_one, shift_two, shift_three,
                                   sum_q, sum_v, sum_g_one, sum_dq, sum_dv, sum_g_two, sum_dpre, sum_g], chips)
    g_qkv, g_mid, g_ff = lax.optimization_barrier((g_qkv, g_mid, g_ff))
    g_mid, g_ff = g_mid.astype(F32), g_ff.astype(F32)
    g_gain, g_shift, g_proj = sums[:3], sums[3:6], sums[6:12]
    unit_rows = sum_dpre.shape[0]
    g_units, g_out_bias = sums[12:12 + unit_rows].reshape(-1), sums[12 + unit_rows]
    cut = lambda i: g_mid[:, i * part:(i + 1) * part]
    quarter = units // 2
    pieces = [g_ff[:, i * quarter:(i + 1) * quarter] for i in range(4)]
    return (output, grad_tokens, g_qkv.reshape(rows_here, 3, part), cut(0).T, cut(1),
            g_mid[:, 2 * part:4 * part].reshape(rows_here, 2, part), cut(4).T,
            jnp.concatenate([pieces[0], pieces[2]], 1), jnp.concatenate([pieces[1], pieces[3]], 1).T,
            g_gain, g_shift, g_proj, g_units, g_out_bias)


def solution(mesh):
    grid = Mesh(mesh.devices.reshape(-1, 2, mesh.shape["tensor"]), ("chip", "core", "tensor"))
    rows = ("chip", "core", "tensor")
    dp = ("chip", "core")
    in_specs = (P(rows, None), P(dp, None, None), P(rows), P(rows), P(rows, None), P(dp, None, "tensor"), P("tensor", dp),
                P(dp, "tensor"), P(dp, None, "tensor"), P("tensor", dp), P(dp, "tensor"), P("tensor", dp),
                P(), P(), P(), P(), P())
    out_specs = (P(rows, None), P(rows, None), P(dp, None, "tensor"), P("tensor", dp), P(dp, "tensor"), P(dp, None, "tensor"),
                 P("tensor", dp), P(dp, "tensor"), P("tensor", dp), P(), P(), P(), P(), P())
    return jax.shard_map(on_device, mesh=grid, in_specs=in_specs, out_specs=out_specs, check_vma=False)
```

```python
import functools, jax, jax.numpy as jnp
from jax import lax
from jax.experimental import pallas as pl
from jax.experimental.pallas import tpu as pltpu
from jax.sharding import Mesh
from jax.sharding import PartitionSpec as P
BLK=256
HEAD=64
LANES=128
NEG=-1e30
LOG2E=1.4426950408889634
F32=jnp.float32; BF=jnp.bfloat16

def lane_ids(rows): return lax.broadcasted_iota(jnp.int32,(rows,LANES),1)

def nt(a,b): return lax.dot_general(a,b,(((1,),(1,)),((),())),preferred_element_type=F32)
def nn(a,b): return lax.dot_general(a,b,(((1,),(0,)),((),())),preferred_element_type=F32)
def tn(a,b): return lax.dot_general(a,b,(((0,),(0,)),((),())),preferred_element_type=F32)

def pick(head, lanes): return (lanes<64) if head==0 else (lanes>=64)

def places(core, half):
    return (core * half, (1 - core) * half)


def rows_at(base, offset, count):
    return pl.ds(pl.multiple_of(base + offset, BLK), count)


def self_fwd_kernel(core_ref,kept_ref,come_ref,segq_ref,segk_ref,own_ref,sent_ref,lse_ref,q_ref,k_ref,vx_ref,o_ref):
    half=kept_ref.shape[1]; rows=2*half; n=rows//BLK
    core=core_ref[0]
    for ref,base in zip((kept_ref,come_ref),places(core,half)):
        at=rows_at(base,0,half)
        q_ref[at,:]=ref[0]
        k_ref[at,:]=ref[1]
        vx_ref[at,:LANES]=ref[2]
    vx_ref[:,LANES:]=jnp.ones((rows,LANES),BF)
    lanes=lane_ids(BLK)
    for i in range(n):
        r0=i*BLK; kn=r0+BLK
        q=q_ref[r0:kn,:]
        outs=[];lses=[]
        for h in range(2):
            qm=jnp.where(pick(h,lanes),q,jnp.zeros_like(q))
            s=nt(qm,k_ref[:kn,:])
            cut = half if i>=n//2 else r0
            a=s[:,:cut] if cut>0 else None
            b=s[:,cut:]
            w=kn-cut
            qi=lax.broadcasted_iota(jnp.int32,(BLK,w),0)+(r0-cut)
            kj=lax.broadcasted_iota(jnp.int32,(BLK,w),1)
            ok=kj<=qi
            if i>=n//2:
                ok=ok&(segk_ref[:,:kn-half]==segq_ref[r0-half:kn-half,:])
            b=jnp.where(ok,b,NEG)
            m=jnp.max(b,-1,keepdims=True)
            if a is not None: m=jnp.maximum(m,jnp.max(a,-1,keepdims=True))
            pb=jnp.exp2(b-m).astype(BF)
            ox=nn(pb,vx_ref[cut:kn,:])
            if a is not None:
                pa=jnp.exp2(a-m).astype(BF)
                ox=ox+nn(pa,vx_ref[:cut,:])
            l=ox[:,LANES:]
            outs.append(ox[:,:LANES]/l); lses.append(m+jnp.log2(l))
        sel=lanes<64
        o_ref[r0:kn,:]=jnp.where(sel,outs[0],outs[1]).astype(BF)
        lse_ref[r0:kn,:]=jnp.where(sel,lses[0],lses[1])
    for ref,base in zip((own_ref,sent_ref),places(core,half)):
        ref[...]=o_ref[rows_at(base,0,half),:]


def scalar():
    return pl.BlockSpec(memory_space=pltpu.SMEM)


def pair_cost(pairs,passes,nbytes):
    return pl.CostEstimate(flops=int(pairs*passes*64),bytes_accessed=int(nbytes)//8,transcendentals=int(pairs)//8)


def self_fwd(core,kept,come,segq,segk):
    half,part=kept.shape[1:]; rows=2*half
    three=pl.BlockSpec((3,half,LANES),lambda p:(0,0,p))
    one=pl.BlockSpec((half,LANES),lambda p:(0,p))
    n=rows//BLK
    return pl.pallas_call(self_fwd_kernel,
        grid=(part//LANES,),
        in_specs=[scalar(),three,three,pl.BlockSpec(segq.shape,lambda p:(0,0)),pl.BlockSpec(segk.shape,lambda p:(0,0))],
        out_specs=[one,one,pl.BlockSpec((rows,LANES),lambda p:(0,p))],
        out_shape=[jax.ShapeDtypeStruct((half,part),BF),jax.ShapeDtypeStruct((half,part),BF),jax.ShapeDtypeStruct((rows,part),F32)],
        scratch_shapes=[pltpu.VMEM((rows,LANES),BF),pltpu.VMEM((rows,LANES),BF),pltpu.VMEM((rows,2*LANES),BF),pltpu.VMEM((rows,LANES),BF)],
        compiler_params=pltpu.CompilerParams(vmem_limit_bytes=60*2**20),
        cost_estimate=pair_cost(n*(n+1)//2*BLK*BLK*(part//HEAD),2,12*rows*part),
        name="self_fwd",
    )(core,kept,come,segq,segk)

def cross_fwd_kernel(frames,q_ref,k_ref,v_ref,o_ref,lse_ref,kx_ref,vx_ref):
    rows=q_ref.shape[0]; n=rows//BLK; kp=k_ref.shape[0]
    tail=frames//BLK*BLK
    kx_ref[...]=k_ref[...]
    vx_ref[:,:LANES]=v_ref[...]
    vx_ref[:,LANES:]=jnp.ones((kp,LANES),BF)
    if frames<kp:
        keep=lax.broadcasted_iota(jnp.int32,(kp-tail,LANES),0)+tail<frames
        kx_ref[tail:,:]=jnp.where(keep,k_ref[tail:,:],jnp.zeros((),BF))
        vx_ref[tail:,:LANES]=jnp.where(keep,v_ref[tail:,:],jnp.zeros((),BF))
    lanes=lane_ids(BLK)
    for i in range(n):
        r0=i*BLK
        q=q_ref[r0:r0+BLK,:]
        outs=[];lses=[]
        for h in range(2):
            qm=jnp.where(pick(h,lanes),q,jnp.zeros_like(q))
            s=nt(qm,kx_ref[...])
            if frames<kp:
                kj=lax.broadcasted_iota(jnp.int32,(BLK,kp-tail),1)+tail
                s=jnp.concatenate([s[:,:tail],jnp.where(kj<frames,s[:,tail:],NEG)],axis=1)
            m=jnp.max(s,-1,keepdims=True)
            p=jnp.exp2(s-m).astype(BF)
            ox=nn(p,vx_ref[...])
            l=ox[:,LANES:]
            outs.append(ox[:,:LANES]/l); lses.append(m+jnp.log2(l))
        sel=lanes<64
        o_ref[r0:r0+BLK,:]=jnp.where(sel,outs[0],outs[1]).astype(BF)
        lse_ref[r0:r0+BLK,:]=jnp.where(sel,lses[0],lses[1])

def cross_fwd(q,kv,frames,heads):
    rows=q.shape[0]; npair=heads//2; kp=kv.shape[0]
    return pl.pallas_call(functools.partial(cross_fwd_kernel,frames),
        grid=(npair,),
        in_specs=[pl.BlockSpec((rows,LANES),lambda p:(0,p)),
                  pl.BlockSpec((kp,LANES),lambda p:(0,p)),
                  pl.BlockSpec((kp,LANES),lambda p:(0,npair+p))],
        out_specs=[pl.BlockSpec((rows,LANES),lambda p:(0,p)),pl.BlockSpec((rows,LANES),lambda p:(0,p))],
        out_shape=[jax.ShapeDtypeStruct((rows,heads*64),BF),jax.ShapeDtypeStruct((rows,heads*64),F32)],
        scratch_shapes=[pltpu.VMEM((kp,LANES),BF),pltpu.VMEM((kp,2*LANES),BF)],
        compiler_params=pltpu.CompilerParams(vmem_limit_bytes=60*2**20),
        cost_estimate=pair_cost(rows*kp*heads,2,8*rows*heads*64+4*kp*heads*64),
        name="cross_fwd",
    )(q,kv,kv)

def split3(x):
    hi=x.astype(BF); r=x-hi.astype(F32); mid=r.astype(BF); lo=(r-mid.astype(F32)).astype(BF)
    return hi,mid,lo

def aug(value,head,lanes,one_lane):
    hi,mid,lo=split3(-value)
    z=jnp.zeros(lanes.shape,F32)
    b=64*head
    x=jnp.where(lanes==b,hi.astype(F32),jnp.where(lanes==b+1,mid.astype(F32),jnp.where(lanes==b+2,lo.astype(F32),z)))
    if one_lane: x=jnp.where(lanes==b+3,1.0,x)
    return x.astype(BF)

def build_q(q,do,o,lse,at,qx_ref,dox_ref,masked):
    lanes=lane_ids(BLK)
    prod=do.astype(F32)*o.astype(F32)
    for h in range(2):
        sel=pick(h,lanes)
        delta=jnp.sum(jnp.where(sel,prod,0.0),-1,keepdims=True)
        qx_ref[h,at,:LANES]=jnp.where(sel,q,jnp.zeros((),BF))
        qx_ref[h,at,LANES:]=aug(lse,h,lanes,masked)
        dox_ref[h,at,:LANES]=jnp.where(sel,do,jnp.zeros((),BF))
        dox_ref[h,at,LANES:]=aug(delta,h,lanes,False)

def build_k(k,v,r0,at,kx_ref,km_ref,vx_ref,frames):
    lanes=lane_ids(BLK)
    low=lanes%64
    ones=jnp.where(low<3,1.0,0.0)
    kones=ones
    if frames is not None and r0+BLK>frames:
        bad=lax.broadcasted_iota(jnp.int32,(BLK,LANES),0)+r0>=frames
        k=jnp.where(bad,jnp.zeros((),BF),k); v=jnp.where(bad,jnp.zeros((),BF),v)
        kones=jnp.where(bad&(low==3),NEG,ones)
    kx_ref[at,:LANES]=k; kx_ref[at,LANES:]=kones.astype(BF)
    vx_ref[at,:LANES]=v; vx_ref[at,LANES:]=ones.astype(BF)
    for h in range(2): km_ref[h,at,:]=jnp.where(pick(h,lanes),k,jnp.zeros((),BF))

def block_back(kx,vx,km,qx,dox,mask):
    s=nt(kx,qx)
    if mask is not None:
        cut=s.shape[0]-mask.shape[0]
        low=jnp.where(mask,s[cut:],NEG)
        s=jnp.concatenate([s[:cut],low],0) if cut else low
    p=jnp.exp2(s)
    dp=nt(vx,dox)
    ds=(p*dp).astype(BF)
    pb=p.astype(BF)
    dv=nn(pb,dox[:,:LANES])
    dk=nn(ds,qx[:,:LANES])
    dq=tn(ds,km)
    return dv,dk,dq

def self_bwd_kernel(core_ref,kept_ref,come_ref,do_ref,do_come_ref,o_ref,o_sent_ref,lse_ref,segq_ref,segk_ref,own_ref,sent_ref,
                    qx_ref,dox_ref,kx_ref,km_ref,vx_ref,dqa_ref,dka_ref,dva_ref):
    half=kept_ref.shape[1]; rows=2*half; n=rows//BLK
    core=core_ref[0]
    for ref,d,o,base in zip((kept_ref,come_ref),(do_ref,do_come_ref),(o_ref,o_sent_ref),places(core,half)):
        for r0 in range(0,half,BLK):
            here=slice(r0,r0+BLK); at=rows_at(base,r0,BLK)
            build_q(ref[0,here,:],d[here,:],o[here,:],lse_ref[at,:],at,qx_ref,dox_ref,False)
            build_k(ref[1,here,:],ref[2,here,:],0,at,kx_ref,km_ref,vx_ref,None)
    dka_ref[...]=jnp.zeros_like(dka_ref)
    dva_ref[...]=jnp.zeros_like(dva_ref)
    for i in range(n):
        r0=i*BLK; kn=r0+BLK; at=slice(r0,kn)
        cut=half if i>=n//2 else r0
        w=kn-cut
        mask=lax.broadcasted_iota(jnp.int32,(w,BLK),0)<=lax.broadcasted_iota(jnp.int32,(w,BLK),1)+(r0-cut)
        if i>=n//2: mask=mask&(segk_ref[:kn-half,:]==segq_ref[i-n//2])
        r=[block_back(kx_ref[:kn,:],vx_ref[:kn,:],km_ref[h,:kn,:],qx_ref[h,at,:],dox_ref[h,at,:],mask) for h in range(2)]
        dva_ref[:kn,:]+=r[0][0]+r[1][0]
        dka_ref[:kn,:]+=r[0][1]+r[1][1]
        dqa_ref[at,:]=((r[0][2]+r[1][2])*0.125).astype(BF)
    for ref,base in zip((own_ref,sent_ref),places(core,half)):
        at=rows_at(base,0,half)
        ref[0]=dqa_ref[at,:]
        ref[1]=(dka_ref[at,:]*(1/LOG2E)).astype(BF)
        ref[2]=dva_ref[at,:].astype(BF)

def self_bwd(core,kept,come,do,do_come,o,o_sent,lse,segq,segk):
    half,part=kept.shape[1:]; rows=2*half
    three=pl.BlockSpec((3,half,LANES),lambda p:(0,0,p))
    one=pl.BlockSpec((half,LANES),lambda p:(0,p))
    out=jax.ShapeDtypeStruct((3,half,part),BF)
    n=rows//BLK
    return pl.pallas_call(self_bwd_kernel,
        grid=(part//LANES,),
        in_specs=[scalar(),three,three,one,one,one,one,pl.BlockSpec((rows,LANES),lambda p:(0,p)),
                  pl.BlockSpec(segq.shape,lambda p:(0,0,0)),pl.BlockSpec(segk.shape,lambda p:(0,0))],
        out_specs=[three,three],
        out_shape=[out,out],
        scratch_shapes=[pltpu.VMEM((2,rows,2*LANES),BF),pltpu.VMEM((2,rows,2*LANES),BF),pltpu.VMEM((rows,2*LANES),BF),
                        pltpu.VMEM((2,rows,LANES),BF),pltpu.VMEM((rows,2*LANES),BF),pltpu.VMEM((rows,LANES),BF),
                        pltpu.VMEM((rows,LANES),F32),pltpu.VMEM((rows,LANES),F32)],
        compiler_params=pltpu.CompilerParams(vmem_limit_bytes=60*2**20),
        cost_estimate=pair_cost(n*(n+1)//2*BLK*BLK*(part//HEAD),5,20*rows*part),
        name="self_bwd",
    )(core,kept,come,do,do_come,o,o_sent,lse,segq,segk)

def cross_bwd_kernel(frames,q_ref,k_ref,v_ref,do_ref,o_ref,lse_ref,dq_ref,dk_ref,dv_ref,
                     qx_ref,dox_ref,kx_ref,km_ref,vx_ref,dka_ref,dva_ref):
    rows=q_ref.shape[0]; n=rows//BLK; kp=k_ref.shape[0]; nk=kp//BLK
    for r0 in range(0,rows,BLK):
        at=slice(r0,r0+BLK)
        build_q(q_ref[at,:],do_ref[at,:],o_ref[at,:],lse_ref[at,:],at,qx_ref,dox_ref,True)
    for r0 in range(0,kp,BLK):
        at=slice(r0,r0+BLK)
        build_k(k_ref[at,:],v_ref[at,:],r0,at,kx_ref,km_ref,vx_ref,frames)
    for i in range(rows//BLK):
        at=slice(i*BLK,(i+1)*BLK)
        r=[block_back(kx_ref[...],vx_ref[...],km_ref[h],qx_ref[h,at,:],dox_ref[h,at,:],None) for h in range(2)]
        dv=r[0][0]+r[1][0]; dk=r[0][1]+r[1][1]
        if i==0: dva_ref[...]=dv; dka_ref[...]=dk
        else: dva_ref[...]+=dv; dka_ref[...]+=dk
        dq_ref[at,:]=((r[0][2]+r[1][2])*0.125).astype(BF)
    dk_ref[...]=(dka_ref[...]*(1/LOG2E)).astype(BF)
    dv_ref[...]=dva_ref[...].astype(BF)

def cross_bwd(q,kv,frames,do,o,lse,heads):
    rows=q.shape[0]; npair=heads//2; kp=kv.shape[0]
    big=lambda f:pl.BlockSpec((rows,LANES),f)
    kb=lambda f:pl.BlockSpec((kp,LANES),f)
    return pl.pallas_call(functools.partial(cross_bwd_kernel,frames),
        grid=(npair,),
        in_specs=[big(lambda p:(0,p)),kb(lambda p:(0,p)),kb(lambda p:(0,npair+p)),big(lambda p:(0,p)),big(lambda p:(0,p)),big(lambda p:(0,p))],
        out_specs=[big(lambda p:(0,p)),kb(lambda p:(0,p)),kb(lambda p:(0,p))],
        out_shape=[jax.ShapeDtypeStruct((rows,heads*64),BF),jax.ShapeDtypeStruct((kp,heads*64),BF),jax.ShapeDtypeStruct((kp,heads*64),BF)],
        scratch_shapes=[pltpu.VMEM((2,rows,2*LANES),BF),pltpu.VMEM((2,rows,2*LANES),BF),pltpu.VMEM((kp,2*LANES),BF),
                        pltpu.VMEM((2,kp,LANES),BF),pltpu.VMEM((kp,2*LANES),BF),
                        pltpu.VMEM((kp,LANES),F32),pltpu.VMEM((kp,LANES),F32)],
        compiler_params=pltpu.CompilerParams(vmem_limit_bytes=60*2**20),
        cost_estimate=pair_cost(rows*kp*heads,5,12*rows*heads*64+8*kp*heads*64),
        name="cross_bwd",
    )(q,kv,kv,do,o,lse)


EPSILON = 1e-05
ROWS = 256
CHUNK = 768
BIG = 60 * 2**20


def whole(shape):
    return pl.BlockSpec(shape, lambda *_: (0,) * len(shape), pipeline_mode=pl.Buffered(1))


def by_rows(*lead_and_cols):
    *lead, cols = lead_and_cols
    return pl.BlockSpec((*lead, ROWS, cols), lambda i: (0,) * len(lead) + (i, 0))


def shaped(shape, dtype):
    return jax.ShapeDtypeStruct(shape, dtype)


def cost(flops, nbytes, trans=0):
    return pl.CostEstimate(flops=int(flops), bytes_accessed=int(nbytes), transcendentals=int(trans))


def normalize(values):
    centre = values - jnp.mean(values, -1, keepdims=True)
    scale = lax.rsqrt(jnp.mean(centre * centre, -1, keepdims=True) + EPSILON)
    return centre * scale, scale


def norm_grad(normed, scale, gain, grad):
    weighted = grad * gain
    return scale * (weighted - jnp.mean(weighted, -1, keepdims=True)
                    - normed * jnp.mean(weighted * normed, -1, keepdims=True))


def accumulate(ref, value):
    ref[...] = value + jnp.where(pl.program_id(0) == 0, jnp.zeros_like(value), ref[...])


def column_sum(values):
    return jnp.sum(values, 0, keepdims=True)


def qkv_heads(low, w_ref, bias_ref, at, out_ref):
    part = out_ref.shape[2]
    cols = nn(low, w_ref[at])
    out_ref[0] = ((cols[:, :part] + bias_ref[at, 0:1]) * (HEAD ** -0.5 * LOG2E)).astype(BF)
    out_ref[1] = cols[:, part:2 * part].astype(BF)
    out_ref[2] = (cols[:, 2 * part:] + bias_ref[at, 1:2]).astype(BF)


def qkv_sent_kernel(core_ref, x_ref, w_ref, gain_ref, shift_ref, bias_ref, norm_ref, sent_ref):
    normed, _ = normalize(x_ref[...].astype(F32))
    low = (normed * gain_ref[0:1] + shift_ref[0:1]).astype(BF)
    norm_ref[...] = low
    qkv_heads(low, w_ref, bias_ref, 1 - core_ref[0], sent_ref)


def qkv_kept_kernel(core_ref, norm_ref, w_ref, bias_ref, kept_ref):
    qkv_heads(norm_ref[...], w_ref, bias_ref, core_ref[0], kept_ref)


def qkv_sent(core, x, w, gain, shift, bias):
    rows, width = x.shape
    part = width // 2
    return pl.pallas_call(
        qkv_sent_kernel, grid=(rows // ROWS,),
        in_specs=[scalar(), by_rows(width), whole(w.shape), whole(gain.shape), whole(shift.shape), whole(bias.shape)],
        out_specs=[by_rows(width), by_rows(3, part)],
        out_shape=[shaped((rows, width), BF), shaped((3, rows, part), BF)],
        compiler_params=pltpu.CompilerParams(vmem_limit_bytes=BIG),
        cost_estimate=cost(3 * rows * width * width, 2 * (3 * width * width + 4 * rows * width)), name="qkv_sent",
    )(core, x, w, gain, shift, bias)


def qkv_kept(core, norm, w, bias):
    rows, width = norm.shape
    part = width // 2
    return pl.pallas_call(
        qkv_kept_kernel, grid=(rows // ROWS,),
        in_specs=[scalar(), by_rows(width), whole(w.shape), whole(bias.shape)],
        out_specs=by_rows(3, part), out_shape=shaped((3, rows, part), BF),
        compiler_params=pltpu.CompilerParams(vmem_limit_bytes=BIG),
        cost_estimate=cost(3 * rows * width * width, 2 * (3 * width * width + 3 * rows * width)), name="qkv_kept",
    )(core, norm, w, bias)


def memory_kernel(frames, mine_ref, own_ref, come_ref, w_ref, bias_ref, kv_ref, mem_ref):
    width = own_ref.shape[1]
    part = width // 2
    mem = jnp.where(mine_ref[0] == 1, own_ref[...], come_ref[...])
    row = lax.broadcasted_iota(jnp.int32, mem.shape, 0) + pl.program_id(0) * ROWS
    mem = jnp.where(row < frames, mem, jnp.zeros((), BF))
    mem_ref[...] = mem
    for t in range(2):
        cols = nn(mem, w_ref[t])
        kv_ref[:, t * part:(t + 1) * part] = cols[:, :part].astype(BF)
        kv_ref[:, width + t * part:width + (t + 1) * part] = (cols[:, part:] + bias_ref[4:5, t * part:(t + 1) * part]).astype(BF)


def memory_project(mine, own, come, w_mid, bias):
    frames, width = own.shape
    steps = pl.cdiv(frames, ROWS)
    return pl.pallas_call(
        functools.partial(memory_kernel, frames), grid=(steps,),
        in_specs=[scalar(), by_rows(width), by_rows(width),
                  pl.BlockSpec((2, width, width), lambda i: (0, 0, 1), pipeline_mode=pl.Buffered(1)), whole(bias.shape)],
        out_specs=[by_rows(2 * width), by_rows(width)],
        out_shape=[shaped((steps * ROWS, 2 * width), BF), shaped((steps * ROWS, width), BF)],
        compiler_params=pltpu.CompilerParams(vmem_limit_bytes=BIG),
        cost_estimate=cost(4 * frames * width * width, 2 * (2 * width * width + 5 * frames * width)), name="memory_project",
    )(mine, own, come, w_mid, bias)


def middle_kernel(core_ref, x_ref, own_ref, come_ref, wo_ref, wq_ref, gain_ref, shift_ref, bias_ref,
                  resid_ref, norm_ref, q_ref):
    part = own_ref.shape[1]
    core = core_ref[0]
    resid = x_ref[...].astype(F32) + nt(own_ref[...], wo_ref[core]) + nt(come_ref[...], wo_ref[1 - core]) + bias_ref[2:3]
    resid_ref[...] = resid
    normed, _ = normalize(resid)
    low = (normed * gain_ref[1:2] + shift_ref[1:2]).astype(BF)
    norm_ref[...] = low
    for t in range(2):
        at = slice(t * part, (t + 1) * part)
        q_ref[:, at] = ((nn(low, wq_ref[t]) + bias_ref[3:4, at]) * (HEAD ** -0.5 * LOG2E)).astype(BF)


def middle(core, x, own, come, w_mid, gain, shift, bias):
    rows, width = x.shape
    part = width // 2
    w_at = lambda c: pl.BlockSpec((2, width, part), lambda i: (0, 0, c), pipeline_mode=pl.Buffered(1))
    return pl.pallas_call(
        middle_kernel, grid=(rows // ROWS,),
        in_specs=[scalar(), by_rows(width), by_rows(part), by_rows(part), w_at(0), w_at(1),
                  whole(gain.shape), whole(shift.shape), whole(bias.shape)],
        out_specs=[by_rows(width)] * 3,
        out_shape=[shaped((rows, width), F32), shaped((rows, width), BF), shaped((rows, width), BF)],
        compiler_params=pltpu.CompilerParams(vmem_limit_bytes=BIG),
        cost_estimate=cost(4 * rows * width * width, 4 * width * width + 12 * rows * width), name="middle",
    )(core, x, own, come, w_mid, w_mid, gain, shift, bias)


def gelu_parts(v):
    z = jnp.abs(v) * (0.5 ** 0.5)
    t = 1.0 / (1.0 + 0.3275911 * z)
    bell = jnp.exp2(v * v * (-0.5 * LOG2E))
    poly = ((((1.061405429 * t - 1.453152027) * t + 1.421413741) * t - 0.284496736) * t + 0.254829592) * t
    tail = (0.5 * poly) * bell
    phi = jnp.where(v >= 0, 1.0 - tail, tail)
    return phi, phi + v * bell * 0.3989422804014327


def feed_kernel(attn_ref, resid_ref, g_ref, wo_ref, wi_ref, wm_ref, gain_ref, shift_ref, bias_ref, unit_bias_ref, out_bias_ref,
                out_ref, norm_ref, hidden_ref, dpre_ref, g2_ref, dattn_ref,
                sum_g_ref, sum_dpre_ref, sum_g2_ref, sum_gain_ref, sum_shift_ref):
    part = wo_ref.shape[2]
    units = wi_ref.shape[2]
    resid = resid_ref[...] + bias_ref[5:6]
    for t in range(2):
        resid = resid + nt(attn_ref[:, t * part:(t + 1) * part], wo_ref[t])
    normed, scale = normalize(resid)
    low = (normed * gain_ref[2:3] + shift_ref[2:3]).astype(BF)
    norm_ref[...] = low
    g_low = g_ref[...]
    out = resid + out_bias_ref[...]
    back = jnp.zeros_like(resid)
    sums = []
    spots = [(t, c) for t in range(2) for c in range(0, units, CHUNK)]

    def first(spot):
        t, c = spot
        at = slice(t * units + c, t * units + c + CHUNK)
        return nn(low, wi_ref[t, :, c:c + CHUNK]) + unit_bias_ref[:, at], nn(g_low, wm_ref[t, :, c:c + CHUNK])

    ahead = first(spots[0])
    for k, (t, c) in enumerate(spots):
        at = slice(t * units + c, t * units + c + CHUNK)
        pre, back_hidden = ahead
        if k + 1 < len(spots):
            ahead = first(spots[k + 1])
        phi, slope = gelu_parts(pre)
        hidden = (pre * phi).astype(BF)
        hidden_ref[:, at] = hidden
        out = out + nt(hidden, wm_ref[t, :, c:c + CHUNK])
        dpre = back_hidden * slope
        sums.append(column_sum(dpre))
        dpre = dpre.astype(BF)
        dpre_ref[:, at] = dpre
        back = back + nt(dpre, wi_ref[t, :, c:c + CHUNK])
    out_ref[...] = out.astype(BF)
    sums = jnp.concatenate(sums, 1)
    wide = sum_dpre_ref.shape[1]
    accumulate(sum_dpre_ref, jnp.concatenate([sums[:, i * wide:(i + 1) * wide] for i in range(sum_dpre_ref.shape[0])], 0))
    g = g_low.astype(F32)
    accumulate(sum_g_ref, column_sum(g))
    accumulate(sum_gain_ref, column_sum(back * normed))
    accumulate(sum_shift_ref, column_sum(back))
    g2 = g + norm_grad(normed, scale, gain_ref[2:3], back)
    accumulate(sum_g2_ref, column_sum(g2))
    g2_ref[...] = g2
    g2_low = g2.astype(BF)
    for t in range(2):
        dattn_ref[:, t * part:(t + 1) * part] = nn(g2_low, wo_ref[t]).astype(BF)


def feed(attn, resid, g, w_mid, w_ff, gain, shift, bias, unit_bias, out_bias):
    rows, width = resid.shape
    part = width // 2
    units = w_ff.shape[2] // 2
    w_at = lambda cols, c: pl.BlockSpec((2, width, cols), lambda i: (0, 0, c), pipeline_mode=pl.Buffered(1))
    line = lambda count: (pl.BlockSpec((count, width), lambda i: (0, 0)), shaped((count, width), F32))
    lines = [line(1), line(2 * units // width), line(1), line(1), line(1)]
    return pl.pallas_call(
        feed_kernel, grid=(rows // ROWS,),
        in_specs=[by_rows(width), by_rows(width), by_rows(width), w_at(part, 4), w_at(units, 0), w_at(units, 1),
                  whole(gain.shape), whole(shift.shape), whole(bias.shape), whole(unit_bias.shape), whole(out_bias.shape)],
        out_specs=[by_rows(width), by_rows(width), by_rows(2 * units), by_rows(2 * units), by_rows(width), by_rows(width)] + [a for a, _ in lines],
        out_shape=[shaped((rows, width), BF), shaped((rows, width), BF), shaped((rows, 2 * units), BF), shaped((rows, 2 * units), BF),
                   shaped((rows, width), F32), shaped((rows, width), BF)] + [b for _, b in lines],
        compiler_params=pltpu.CompilerParams(vmem_limit_bytes=BIG),
        cost_estimate=cost(2 * rows * width * (2 * width + 8 * units), 2 * width * (width + 4 * units) + 2 * rows * (8 * width + 4 * units), 4 * rows * units),
        name="feed",
    )(attn, resid, g, w_mid, w_ff, w_ff, gain, shift, bias, unit_bias, out_bias)


def feed_weights_kernel(norm_ref, g_ref, dpre_ref, hidden_ref, out_ref):
    cols = dpre_ref.shape[1]
    out_ref[0, :, :cols] = tn(norm_ref[...], dpre_ref[...]).astype(BF)
    out_ref[0, :, cols:] = tn(g_ref[...], hidden_ref[...]).astype(BF)


def feed_weights(norm, g, dpre, hidden):
    rows, width = norm.shape
    units = dpre.shape[1] // 2
    cols = units // 2
    return pl.pallas_call(
        feed_weights_kernel, grid=(2, 2),
        in_specs=[whole(norm.shape), whole(g.shape), pl.BlockSpec((rows, cols), lambda t, c: (0, 2 * t + c)),
                  pl.BlockSpec((rows, cols), lambda t, c: (0, 2 * t + c))],
        out_specs=pl.BlockSpec((1, width, 2 * cols), lambda t, c: (t, 0, c)),
        out_shape=shaped((2, width, 2 * units), BF),
        compiler_params=pltpu.CompilerParams(vmem_limit_bytes=BIG),
        cost_estimate=cost(8 * rows * width * units, 2 * (4 * width * units + 4 * rows * units)), name="feed_weights",
    )(norm, g, dpre, hidden)


def middle_back_kernel(core_ref, dq_ref, resid_ref, g2_ref, wq_ref, wo_ref, gain_ref,
                       g1_ref, kept_ref, sent_ref, sum_dq_ref, sum_g1_ref, sum_gain_ref, sum_shift_ref):
    part = kept_ref.shape[1]
    core = core_ref[0]
    dq = dq_ref[...]
    back = nt(dq[:, :part], wq_ref[0]) + nt(dq[:, part:], wq_ref[1])
    accumulate(sum_dq_ref, column_sum(dq.astype(F32)))
    normed, scale = normalize(resid_ref[...])
    accumulate(sum_gain_ref, column_sum(back * normed))
    accumulate(sum_shift_ref, column_sum(back))
    g1 = g2_ref[...] + norm_grad(normed, scale, gain_ref[1:2], back)
    g1_ref[...] = g1
    accumulate(sum_g1_ref, column_sum(g1))
    low = g1.astype(BF)
    kept_ref[...] = nn(low, wo_ref[core]).astype(BF)
    sent_ref[...] = nn(low, wo_ref[1 - core]).astype(BF)


def middle_back(core, dq, resid, g2, w_mid, gain):
    rows, width = resid.shape
    part = width // 2
    w_at = lambda c: pl.BlockSpec((2, width, part), lambda i: (0, 0, c), pipeline_mode=pl.Buffered(1))
    line = pl.BlockSpec((1, width), lambda i: (0, 0))
    return pl.pallas_call(
        middle_back_kernel, grid=(rows // ROWS,),
        in_specs=[scalar(), by_rows(width), by_rows(width), by_rows(width), w_at(1), w_at(0), whole(gain.shape)],
        out_specs=[by_rows(width), by_rows(part), by_rows(part)] + [line] * 4,
        out_shape=[shaped((rows, width), F32), shaped((rows, part), BF), shaped((rows, part), BF)] + [shaped((1, width), F32)] * 4,
        compiler_params=pltpu.CompilerParams(vmem_limit_bytes=BIG),
        cost_estimate=cost(4 * rows * width * width, 4 * width * width + 18 * rows * width), name="middle_back",
    )(core, dq, resid, g2, w_mid, w_mid, gain)


def memory_weights_kernel(mem_ref, dk_ref, dv_ref, out_ref, sum_dv_ref):
    part = dk_ref.shape[1]
    mem = mem_ref[...]
    out_ref[0, :, :part] = tn(mem, dk_ref[...]).astype(BF)
    out_ref[0, :, part:] = tn(mem, dv_ref[...]).astype(BF)
    sum_dv_ref[...] = column_sum(dv_ref[...].astype(F32))


def memory_weights(mem, dk, dv):
    frames, width = mem.shape
    part = width // 2
    half = pl.BlockSpec((frames, part), lambda t: (0, t))
    return pl.pallas_call(
        memory_weights_kernel, grid=(2,),
        in_specs=[whole(mem.shape), half, half],
        out_specs=[pl.BlockSpec((1, width, width), lambda t: (t, 0, 0)), pl.BlockSpec((1, part), lambda t: (0, t))],
        out_shape=[shaped((2, width, width), BF), shaped((1, width), F32)],
        compiler_params=pltpu.CompilerParams(vmem_limit_bytes=BIG),
        cost_estimate=cost(4 * width * width * frames, 4 * width * width + 6 * frames * width), name="memory_weights",
    )(mem, dk, dv)


def middle_weights_kernel(core_ref, g1_ref, own_ref, come_ref, norm_ref, dq_ref, g2_ref, attn_ref, out_ref):
    part = own_ref.shape[1]
    attn_self = jnp.where(pl.program_id(0) == core_ref[0], own_ref[...], come_ref[...])
    out_ref[0, :, :part] = tn(g1_ref[...].astype(BF), attn_self).astype(BF)
    out_ref[0, :, part:2 * part] = tn(norm_ref[...], dq_ref[...]).astype(BF)
    out_ref[0, :, 2 * part:] = tn(g2_ref[...].astype(BF), attn_ref[...]).astype(BF)


def middle_weights(core, g1, own, come, norm, dq, g2, attn):
    rows, width = norm.shape
    part = width // 2
    half = pl.BlockSpec((rows, part), lambda t: (0, t))
    return pl.pallas_call(
        middle_weights_kernel, grid=(2,),
        in_specs=[scalar(), whole(g1.shape), whole(own.shape), whole(come.shape), whole(norm.shape), half, whole(g2.shape), half],
        out_specs=pl.BlockSpec((1, width, 3 * part), lambda t: (t, 0, 1)),
        out_shape=shaped((2, width, 6 * part), BF),
        compiler_params=pltpu.CompilerParams(vmem_limit_bytes=BIG),
        cost_estimate=cost(6 * width * width * rows, 6 * width * width + 20 * width * rows), name="middle_weights",
    )(core, g1, own, come, norm, dq, g2, attn)


def qkv_back_kernel(core_ref, own_ref, come_ref, x_ref, g1_ref, w_ref, gain_ref, grad_ref, sum_gain_ref, sum_shift_ref):
    part = own_ref.shape[2]
    core = core_ref[0]
    back = jnp.zeros(x_ref.shape, F32)
    for ref, at in ((own_ref, core), (come_ref, 1 - core)):
        for j in range(3):
            back = back + nt(ref[j], w_ref[at, :, j * part:(j + 1) * part])
    normed, scale = normalize(x_ref[...].astype(F32))
    accumulate(sum_gain_ref, column_sum(back * normed))
    accumulate(sum_shift_ref, column_sum(back))
    grad_ref[...] = (g1_ref[...] + norm_grad(normed, scale, gain_ref[0:1], back)).astype(BF)


def qkv_back(core, own, come, x, g1, w, gain):
    rows, width = x.shape
    part = width // 2
    line = pl.BlockSpec((1, width), lambda i: (0, 0))
    return pl.pallas_call(
        qkv_back_kernel, grid=(rows // ROWS,),
        in_specs=[scalar(), by_rows(3, part), by_rows(3, part), by_rows(width), by_rows(width), whole(w.shape), whole(gain.shape)],
        out_specs=[by_rows(width), line, line],
        out_shape=[shaped((rows, width), BF), shaped((1, width), F32), shaped((1, width), F32)],
        compiler_params=pltpu.CompilerParams(vmem_limit_bytes=BIG),
        cost_estimate=cost(6 * rows * width * width, 2 * (3 * width * width + 7 * rows * width)), name="qkv_back",
    )(core, own, come, x, g1, w, gain)


def qkv_weights_kernel(core_ref, norm_ref, own_ref, come_ref, _, out_ref, sum_q_ref, sum_v_ref):
    part = own_ref.shape[2]
    mine = pl.program_id(0) == core_ref[0]
    norm = norm_ref[...]
    for j in range(3):
        grad = jnp.where(mine, own_ref[j], come_ref[j])
        out_ref[0, :, j * part:(j + 1) * part] = tn(norm, grad).astype(BF)
        if j != 1:
            (sum_q_ref if j == 0 else sum_v_ref)[...] = column_sum(grad.astype(F32))


def qkv_weights(core, norm, own, come, late):
    rows, width = norm.shape
    part = width // 2
    return pl.pallas_call(
        qkv_weights_kernel, grid=(2,),
        in_specs=[scalar(), whole(norm.shape), whole(own.shape), whole(come.shape), pl.BlockSpec(memory_space=pl.ANY)],
        out_specs=[pl.BlockSpec((1, width, 3 * part), lambda t: (t, 0, 0)), pl.BlockSpec((1, part), lambda t: (0, t)), pl.BlockSpec((1, part), lambda t: (0, t))],
        out_shape=[shaped(late.shape, BF), shaped((1, width), F32), shaped((1, width), F32)],
        compiler_params=pltpu.CompilerParams(vmem_limit_bytes=BIG),
        cost_estimate=cost(6 * rows * width * width, 2 * (3 * width * width + 4 * rows * width)), name="qkv_weights",
        input_output_aliases={4: 0},
    )(core, norm, own, come, late)


def bit_names(chips):
    return ["t"] + ["k%d" % b for b in reversed(range((chips - 1).bit_length()))] + ["core"]


def my_bit(name):
    if name == "t":
        return lax.axis_index("tensor")
    if name == "core":
        return lax.axis_index("core")
    return lax.axis_index("chip") // 2 ** int(name[1:]) % 2


def partner(name):
    bit = my_bit(name)
    if name == "t":
        return {"tensor": 1 - bit}
    if name == "core":
        return {"core": 1 - bit}
    return {"chip": lax.axis_index("chip") + 2 ** int(name[1:]) * (1 - 2 * bit)}


def greet(names, *others):
    barrier = pltpu.get_barrier_semaphore()
    for device in [partner(name) for name in names] + list(others):
        pl.semaphore_signal(barrier, inc=1, device_id=device, device_id_type=pl.DeviceIdType.MESH)
    pl.semaphore_wait(barrier, len(names) + len(others))


def exchange_orders(names):
    low = [n for n in reversed(names) if n[0] == "k"]
    return [["core", "t"] + low, ["core"] + low + ["t"], ["core"] + low[1:] + ["t"] + low[:1]]


def stream_cols(cols, count):
    tiles = cols // LANES
    cuts = [tiles * i // count * LANES for i in range(count + 1)]
    return [slice(a, b) for a, b in zip(cuts, cuts[1:])]


def gather_kernel(names, orders, own_ref, seg_ref, x_ref, out_ref, seg_out_ref, moved_ref, block, segs, local_sem, send_sem, recv_sem):
    core, tensor = lax.axis_index("core"), lax.axis_index("tensor")
    greet(names, {"core": 1 - core, "tensor": 1 - tensor})
    spare = len(orders)
    swap = pltpu.make_async_remote_copy(x_ref, moved_ref, send_sem.at[spare, 2], recv_sem.at[spare, 2],
                                        device_id={"core": tensor, "tensor": core}, device_id_type=pl.DeviceIdType.MESH)
    stay = pltpu.make_async_copy(x_ref, moved_ref, local_sem.at[1])

    @pl.when(core != tensor)
    def _():
        swap.start()

    @pl.when(core == tensor)
    def _():
        stay.start()

    pieces, _, part = own_ref.shape
    for i in range(pieces):
        block[:, i * part:(i + 1) * part] = own_ref[i]
    lanes = stream_cols(block.shape[1], len(orders))
    place = tuple(my_bit(n) for n in names)
    known = [[] for _ in orders]
    sent = []
    flying = [None] * len(orders)

    def send(src, dst, st, step, name):
        copy = pltpu.make_async_remote_copy(src, dst, send_sem.at[st, step], recv_sem.at[st, step],
                                            device_id=partner(name), device_id_type=pl.DeviceIdType.MESH)
        copy.start()
        sent.append(copy)
        return copy

    def start(st, step):
        name = orders[st][step]
        at = tuple(slice(None) if n in known[st] else my_bit(n) for n in names)
        dst = out_ref.at[at + (slice(None), lanes[st])]
        flying[st] = send(dst if step else block.at[:, lanes[st]], dst, st, step, name)
        known[st].append(name)

    for st in range(len(orders)):
        start(st, 0)
    local = pltpu.make_async_copy(block, out_ref.at[place], local_sem.at[0])
    local.start()
    segs[core, tensor] = seg_ref[...]
    along = send(segs.at[core, tensor], segs.at[core, tensor], spare, 0, "t")
    local.wait()
    for step in range(len(names)):
        for st in range(len(orders)):
            flying[st].wait_recv()
            if step + 1 < len(names):
                start(st, step + 1)
        if step == 0:
            along.wait_recv()
            along = send(segs.at[core], segs.at[core], spare, 1, "core")
    along.wait_recv()
    seg_out_ref[...] = segs[tensor, 1]
    for copy in sent:
        copy.wait_send()

    @pl.when(core != tensor)
    def _():
        swap.wait()

    @pl.when(core == tensor)
    def _():
        stay.wait()


def gather_all(shard, seg, x, chips):
    names = bit_names(chips)
    orders = [list(reversed(o)) for o in exchange_orders(names)]
    pieces, rows, part = shard.shape
    cols = pieces * part
    dma = pltpu.SemaphoreType.DMA
    vmem = pl.BlockSpec(memory_space=pltpu.VMEM)
    seg = seg.reshape(-1, LANES)
    hbm = pl.BlockSpec(memory_space=pl.ANY)
    full, seg, moved = pl.pallas_call(
        functools.partial(gather_kernel, names, orders),
        in_specs=[vmem, vmem, hbm], out_specs=[hbm, vmem, hbm],
        out_shape=[shaped((2,) * len(names) + (rows, cols), shard.dtype), shaped(seg.shape, seg.dtype), shaped(x.shape, x.dtype)],
        scratch_shapes=[pltpu.VMEM((rows, cols), shard.dtype), pltpu.VMEM((2, 2) + seg.shape, seg.dtype),
                        dma((2,)), dma((len(orders) + 1, len(names))), dma((len(orders) + 1, len(names)))],
        compiler_params=pltpu.CompilerParams(collective_id=0, has_side_effects=True, vmem_limit_bytes=BIG),
        cost_estimate=cost(0, 1e6), name="gather_all",
    )(shard, seg, x)
    return full.reshape(2, -1, cols), seg.reshape(-1), moved


def sum_kernel(names, orders, smalls, pieces, grad_ref, ff_ref, *refs):
    small_refs, (qkv_ref, *out_refs), scratch = refs[:smalls], refs[smalls:smalls + pieces + 1], refs[smalls + pieces + 1:]
    small_out_ref, ff_in_ref, ff_out_ref, *scratch = scratch
    greet(names)
    count, steps = len(orders), len(names)
    recv = [scratch[st * steps:(st + 1) * steps] for st in range(count)]
    held = [scratch[(count + st) * steps:(count + st + 1) * steps] for st in range(count)]
    small_recv, small_held, send_sem, recv_sem = scratch[2 * count * steps:]
    lanes = stream_cols(grad_ref.shape[-1], count)
    left = [list(names) for _ in orders]
    here = [grad_ref.at[(slice(None),) * (steps + 1) + (lanes[st],)] for st in range(count)]
    sent = []
    flying = [None] * (count + 1)

    def start(st, step):
        name = orders[st][step] if st < count else orders[0][step]
        if st < count:
            src = here[st].at[tuple(1 - my_bit(n) if n == name else slice(None) for n in left[st])]
            dst = recv[st][step]
        else:
            src = small_held.at[step]
            dst = small_recv.at[step]
        copy = pltpu.make_async_remote_copy(src, dst, send_sem.at[st, step], recv_sem.at[st, step],
                                            device_id=partner(name), device_id_type=pl.DeviceIdType.MESH)
        copy.start()
        sent.append(copy)
        flying[st] = copy

    for st in range(count):
        start(st, 0)
    row = 0
    for ref in small_refs:
        small_held[0, row:row + ref.shape[0]] = ref[...]
        row += ref.shape[0]
    small_held[0, row:] = jnp.zeros((small_held.shape[1] - row, small_held.shape[2]), F32)
    start(count, 0)
    quarter = ff_ref.shape[1] // 4
    for i in range(4):
        ref, at = (ff_out_ref if i % 2 else ff_in_ref), i // 2 * quarter
        ref[:, at:at + quarter] = ff_ref[:, i * quarter:(i + 1) * quarter].astype(F32)
    for step in range(steps):
        for st in range(count):
            name = orders[st][step]
            flying[st].wait_recv()
            at = tuple(my_bit(n) if n == name else slice(None) for n in left[st])
            kept = here[st].at[at]
            total = kept[...].astype(F32) + recv[st][step][...].astype(F32)
            if step + 1 < steps:
                held[st][step][...] = total.astype(BF)
                here[st] = held[st][step]
                left[st].remove(name)
                start(st, step + 1)
            else:
                part = qkv_ref.shape[2]
                for at in range(lanes[st].start, lanes[st].stop, part):
                    value = total[:, at - lanes[st].start:at - lanes[st].start + part]
                    if at < 3 * part:
                        qkv_ref[at // part] = value
                    else:
                        out_refs[at // part - 3][...] = value
        flying[count].wait_recv()
        total = small_held[step] + small_recv[step]
        if step + 1 < steps:
            small_held[step + 1] = total
            start(count, step + 1)
        else:
            small_out_ref[...] = total
    for copy in sent:
        copy.wait_send()


def sum_all(grad, ff, small, chips):
    names = bit_names(chips)
    orders = exchange_orders(names)
    cols = grad.shape[2]
    rows = grad.shape[1] // (2 * chips)
    steps = len(names)
    part = small[0].shape[1] // 2
    pieces = cols // part - 3
    bufs = [pltpu.VMEM((2,) * (steps - 1 - step) + (rows, lane.stop - lane.start), BF)
            for lane in stream_cols(cols, len(orders)) for step in range(steps)]
    small_rows = (sum(s.shape[0] for s in small) + 7) // 8 * 8
    small_shape = (small_rows, small[0].shape[1])
    dma = pltpu.SemaphoreType.DMA
    vmem = pl.BlockSpec(memory_space=pltpu.VMEM)
    return pl.pallas_call(
        functools.partial(sum_kernel, names, orders, len(small), pieces),
        in_specs=[vmem] * (2 + len(small)), out_specs=[vmem] * (pieces + 4),
        out_shape=[shaped((3, rows, part), F32)] + [shaped((rows, part), F32)] * pieces
        + [shaped(small_shape, F32)] + [shaped((rows, ff.shape[1] // 2), F32)] * 2,
        scratch_shapes=bufs + bufs + [pltpu.VMEM((steps,) + small_shape, F32), pltpu.VMEM((steps,) + small_shape, F32),
                                      dma((len(orders) + 1, steps)), dma((len(orders) + 1, steps))],
        compiler_params=pltpu.CompilerParams(collective_id=1, has_side_effects=True, vmem_limit_bytes=BIG),
        cost_estimate=cost(0, 1e6), name="sum_all",
    )(grad.reshape((2,) * steps + (rows, cols)), ff, *small)


ALL = ("tensor", "chip", "core")


def fetch(shard):
    full = lax.all_gather(shard, ALL, axis=0, tiled=True)
    return full.reshape(2, -1, shard.shape[1])


def spread_sum(grad):
    return lax.psum_scatter(grad.reshape(-1, grad.shape[2]), ALL, scatter_dimension=0, tiled=True)


def on_device(tokens, memory, seg_ids, positions, grad_output, attn_in, attn_out, cross_q, cross_kv,
              cross_out, mlp_in, mlp_out, norm_gain, norm_bias, proj_bias, mlp_bias, out_bias):
    width = tokens.shape[1]
    rows_here, _, part = attn_in.shape
    units = mlp_in.shape[1]
    heads = width // HEAD
    frames = memory.shape[1]
    core = lax.axis_index("core")
    tensor = lax.axis_index("tensor")
    core_at = core.astype(jnp.int32).reshape(1)
    swap = [(0, 0), (1, 2), (2, 1), (3, 3)]
    fix = lambda x: lax.ppermute(x, ("core", "tensor"), swap)
    other = lambda x: lax.ppermute(x, "core", [(0, 1), (1, 0)])

    chips = lax.axis_size("chip")
    mid = jnp.concatenate([attn_out.T, cross_q, cross_kv.reshape(rows_here, 2 * part), cross_out.T], 1)
    first, mid = lax.optimization_barrier((attn_in.transpose(1, 0, 2), mid))
    w_mid = fetch(mid)
    w_qkv, seg_cont, moved = gather_all(first, seg_ids, tokens, chips)
    late_in, late_out, w_qkv = lax.optimization_barrier((mlp_in, mlp_out, w_qkv))
    w_ff = fetch(jnp.concatenate([late_in, late_out.T], 1))
    bias_halves = proj_bias[:2].reshape(2, 2, part).transpose(1, 0, 2)

    norm_one, sent = qkv_sent(core_at, moved, w_qkv, norm_gain, norm_bias, bias_halves)
    come = other(sent)
    kept = qkv_kept(core_at, norm_one, w_qkv, bias_halves)
    grad_in = fix(grad_output)
    mem_come = other(memory[0])
    o_kept, o_sent, lse_self = self_fwd(core_at, kept, come, seg_cont[:, None], seg_cont[None, :])
    o_come = other(o_sent)
    kv, mem = memory_project((core == tensor).astype(jnp.int32).reshape(1), memory[0], mem_come, w_mid, proj_bias)
    kv, o_come = lax.optimization_barrier((kv, o_come))
    resid_one, norm_two, q_cross = middle(core_at, moved, o_kept, o_come, w_mid, norm_gain, norm_bias, proj_bias)
    attn_cross, lse_cross = cross_fwd(q_cross, kv, frames, heads)
    (out, norm_three, hidden, dpre, g_two, dattn, sum_g, sum_dpre, sum_g_two, gain_three, shift_three) = feed(
        attn_cross, resid_one, grad_in, w_mid, w_ff, norm_gain, norm_bias, proj_bias, mlp_bias[None], out_bias[None])
    output = fix(out)
    gw_ff = feed_weights(norm_three, grad_in, dpre, hidden)
    dattn, gw_ff = lax.optimization_barrier((dattn, gw_ff))
    g_ff = spread_sum(gw_ff)
    dq, dk, dv = cross_bwd(q_cross, kv, frames, dattn, attn_cross, lse_cross, heads)
    g_one, do_kept, do_sent, sum_dq, sum_g_one, gain_two, shift_two = middle_back(core_at, dq, resid_one, g_two, w_mid, norm_gain)
    do_come = other(do_sent)
    gw_kv, sum_dv = memory_weights(mem, dk, dv)
    do_come, gw_kv = lax.optimization_barrier((do_come, gw_kv))
    g_kv = spread_sum(gw_kv)
    d_kept, d_sent = self_bwd(core_at, kept, come, do_kept, do_come, o_kept, o_sent, lse_self,
                              seg_cont.reshape(-1, 1, BLK), seg_cont[:, None])
    d_kept, d_sent, g_ff, output = lax.optimization_barrier((d_kept, d_sent, g_ff, output))
    d_come = other(d_sent)
    dq_late, d_kept = lax.optimization_barrier((dq, d_kept))
    late = middle_weights(core_at, g_one, o_kept, o_come, norm_two, dq_late, g_two, attn_cross)
    d_come, late = lax.optimization_barrier((d_come, late))
    grad_low, gain_one, shift_one = qkv_back(core_at, d_kept, d_come, moved, g_one, w_qkv, norm_gain)
    grad_low, d_kept, d_come = lax.optimization_barrier((grad_low, d_kept, d_come))
    grad_tokens = fix(grad_low).astype(F32)
    late, sum_q, sum_v = qkv_weights(core_at, norm_one, d_kept, d_come, late)
    g_qkv, g_attn_out, g_cross_q, g_cross_out, sums, g_mlp_in, g_mlp_out = sum_all(
        late, g_ff, [gain_one, gain_two, gain_three, shift_one, shift_two, shift_three,
                     sum_q, sum_v, sum_g_one, sum_dq, sum_dv, sum_g_two, sum_dpre, sum_g], chips)
    g_qkv, g_kv = lax.optimization_barrier((g_qkv, g_kv))
    g_gain, g_shift, g_proj = sums[:3], sums[3:6], sums[6:12]
    unit_rows = sum_dpre.shape[0]
    g_units, g_out_bias = sums[12:12 + unit_rows].reshape(-1), sums[12 + unit_rows]
    return (output, grad_tokens, g_qkv.transpose(1, 0, 2), g_attn_out.T, g_cross_q,
            g_kv.astype(F32).reshape(rows_here, 2, part), g_cross_out.T, g_mlp_in, g_mlp_out.T,
            g_gain, g_shift, g_proj, g_units, g_out_bias)


def solution(mesh):
    grid = Mesh(mesh.devices.reshape(-1, 2, mesh.shape["tensor"]), ("chip", "core", "tensor"))
    rows = ("chip", "core", "tensor")
    dp = ("chip", "core")
    in_specs = (P(rows, None), P(dp, None, None), P(rows), P(rows), P(rows, None), P(dp, None, "tensor"), P("tensor", dp),
                P(dp, "tensor"), P(dp, None, "tensor"), P("tensor", dp), P(dp, "tensor"), P("tensor", dp),
                P(), P(), P(), P(), P())
    out_specs = (P(rows, None), P(rows, None), P(dp, None, "tensor"), P("tensor", dp), P(dp, "tensor"), P(dp, None, "tensor"),
                 P("tensor", dp), P(dp, "tensor"), P("tensor", dp), P(), P(), P(), P(), P())
    return jax.shard_map(on_device, mesh=grid, in_specs=in_specs, out_specs=out_specs, check_vma=False)
```

```python
import functools, jax, jax.numpy as jnp
from jax import lax
from jax.experimental import pallas as pl
from jax.experimental.pallas import tpu as pltpu
from jax.sharding import Mesh
from jax.sharding import PartitionSpec as P
BLK=256
HEAD=64
LANES=128
NEG=-1e30
LOG2E=1.4426950408889634
F32=jnp.float32; BF=jnp.bfloat16

def lane_ids(rows): return lax.broadcasted_iota(jnp.int32,(rows,LANES),1)

def nt(a,b): return lax.dot_general(a,b,(((1,),(1,)),((),())),preferred_element_type=F32)
def nn(a,b): return lax.dot_general(a,b,(((1,),(0,)),((),())),preferred_element_type=F32)
def tn(a,b): return lax.dot_general(a,b,(((0,),(0,)),((),())),preferred_element_type=F32)

def pick(head, lanes): return (lanes<64) if head==0 else (lanes>=64)

def places(core, half):
    return (core * half, (1 - core) * half)


def rows_at(base, offset, count):
    return pl.ds(pl.multiple_of(base + offset, BLK), count)


def self_fwd_kernel(core_ref,kept_ref,come_ref,segq_ref,segk_ref,own_ref,sent_ref,lse_ref,q_ref,k_ref,vx_ref,o_ref):
    half=kept_ref.shape[1]; rows=2*half; n=rows//BLK
    core=core_ref[0]
    for ref,base in zip((kept_ref,come_ref),places(core,half)):
        at=rows_at(base,0,half)
        q_ref[at,:]=ref[0]
        k_ref[at,:]=ref[1]
        vx_ref[at,:LANES]=ref[2]
    vx_ref[:,LANES:]=jnp.ones((rows,LANES),BF)
    lanes=lane_ids(BLK)
    for i in range(n):
        r0=i*BLK; kn=r0+BLK
        q=q_ref[r0:kn,:]
        outs=[];lses=[]
        for h in range(2):
            qm=jnp.where(pick(h,lanes),q,jnp.zeros_like(q))
            s=nt(qm,k_ref[:kn,:])
            cut = half if i>=n//2 else r0
            a=s[:,:cut] if cut>0 else None
            b=s[:,cut:]
            w=kn-cut
            qi=lax.broadcasted_iota(jnp.int32,(BLK,w),0)+(r0-cut)
            kj=lax.broadcasted_iota(jnp.int32,(BLK,w),1)
            ok=kj<=qi
            if i>=n//2:
                ok=ok&(segk_ref[:,:kn-half]==segq_ref[r0-half:kn-half,:])
            b=jnp.where(ok,b,NEG)
            m=jnp.max(b,-1,keepdims=True)
            if a is not None: m=jnp.maximum(m,jnp.max(a,-1,keepdims=True))
            pb=jnp.exp2(b-m).astype(BF)
            ox=nn(pb,vx_ref[cut:kn,:])
            if a is not None:
                pa=jnp.exp2(a-m).astype(BF)
                ox=ox+nn(pa,vx_ref[:cut,:])
            l=ox[:,LANES:]
            outs.append(ox[:,:LANES]/l); lses.append(m+jnp.log2(l))
        sel=lanes<64
        o_ref[r0:kn,:]=jnp.where(sel,outs[0],outs[1]).astype(BF)
        lse_ref[r0:kn,:]=jnp.where(sel,lses[0],lses[1])
    for ref,base in zip((own_ref,sent_ref),places(core,half)):
        ref[...]=o_ref[rows_at(base,0,half),:]


def scalar():
    return pl.BlockSpec(memory_space=pltpu.SMEM)


def pair_cost(pairs,passes,nbytes):
    return pl.CostEstimate(flops=int(pairs*passes*64),bytes_accessed=int(nbytes)//8,transcendentals=int(pairs)//8)


def self_fwd(core,kept,come,segq,segk):
    half,part=kept.shape[1:]; rows=2*half
    three=pl.BlockSpec((3,half,LANES),lambda p:(0,0,p))
    one=pl.BlockSpec((half,LANES),lambda p:(0,p))
    n=rows//BLK
    return pl.pallas_call(self_fwd_kernel,
        grid=(part//LANES,),
        in_specs=[scalar(),three,three,pl.BlockSpec(segq.shape,lambda p:(0,0)),pl.BlockSpec(segk.shape,lambda p:(0,0))],
        out_specs=[one,one,pl.BlockSpec((rows,LANES),lambda p:(0,p))],
        out_shape=[jax.ShapeDtypeStruct((half,part),BF),jax.ShapeDtypeStruct((half,part),BF),jax.ShapeDtypeStruct((rows,part),F32)],
        scratch_shapes=[pltpu.VMEM((rows,LANES),BF),pltpu.VMEM((rows,LANES),BF),pltpu.VMEM((rows,2*LANES),BF),pltpu.VMEM((rows,LANES),BF)],
        compiler_params=pltpu.CompilerParams(vmem_limit_bytes=60*2**20),
        cost_estimate=pair_cost(n*(n+1)//2*BLK*BLK*(part//HEAD),2,12*rows*part),
        name="self_fwd",
    )(core,kept,come,segq,segk)

def cross_fwd_kernel(frames,q_ref,k_ref,v_ref,o_ref,lse_ref,kx_ref,vx_ref):
    rows=q_ref.shape[0]; n=rows//BLK; kp=k_ref.shape[0]
    tail=frames//BLK*BLK
    kx_ref[...]=k_ref[...]
    vx_ref[:,:LANES]=v_ref[...]
    vx_ref[:,LANES:]=jnp.ones((kp,LANES),BF)
    if frames<kp:
        keep=lax.broadcasted_iota(jnp.int32,(kp-tail,LANES),0)+tail<frames
        kx_ref[tail:,:]=jnp.where(keep,k_ref[tail:,:],jnp.zeros((),BF))
        vx_ref[tail:,:LANES]=jnp.where(keep,v_ref[tail:,:],jnp.zeros((),BF))
    lanes=lane_ids(BLK)
    for i in range(n):
        r0=i*BLK
        q=q_ref[r0:r0+BLK,:]
        outs=[];lses=[]
        for h in range(2):
            qm=jnp.where(pick(h,lanes),q,jnp.zeros_like(q))
            s=nt(qm,kx_ref[...])
            if frames<kp:
                kj=lax.broadcasted_iota(jnp.int32,(BLK,kp-tail),1)+tail
                s=jnp.concatenate([s[:,:tail],jnp.where(kj<frames,s[:,tail:],NEG)],axis=1)
            m=jnp.max(s,-1,keepdims=True)
            p=jnp.exp2(s-m).astype(BF)
            ox=nn(p,vx_ref[...])
            l=ox[:,LANES:]
            outs.append(ox[:,:LANES]/l); lses.append(m+jnp.log2(l))
        sel=lanes<64
        o_ref[r0:r0+BLK,:]=jnp.where(sel,outs[0],outs[1]).astype(BF)
        lse_ref[r0:r0+BLK,:]=jnp.where(sel,lses[0],lses[1])

def cross_fwd(q,kv,frames,heads):
    rows=q.shape[0]; npair=heads//2; kp=kv.shape[0]
    return pl.pallas_call(functools.partial(cross_fwd_kernel,frames),
        grid=(npair,),
        in_specs=[pl.BlockSpec((rows,LANES),lambda p:(0,p)),
                  pl.BlockSpec((kp,LANES),lambda p:(0,p)),
                  pl.BlockSpec((kp,LANES),lambda p:(0,npair+p))],
        out_specs=[pl.BlockSpec((rows,LANES),lambda p:(0,p)),pl.BlockSpec((rows,LANES),lambda p:(0,p))],
        out_shape=[jax.ShapeDtypeStruct((rows,heads*64),BF),jax.ShapeDtypeStruct((rows,heads*64),F32)],
        scratch_shapes=[pltpu.VMEM((kp,LANES),BF),pltpu.VMEM((kp,2*LANES),BF)],
        compiler_params=pltpu.CompilerParams(vmem_limit_bytes=60*2**20),
        cost_estimate=pair_cost(rows*kp*heads,2,8*rows*heads*64+4*kp*heads*64),
        name="cross_fwd",
    )(q,kv,kv)

def split3(x):
    hi=x.astype(BF); r=x-hi.astype(F32); mid=r.astype(BF); lo=(r-mid.astype(F32)).astype(BF)
    return hi,mid,lo

def aug(value,head,lanes,one_lane):
    hi,mid,lo=split3(-value)
    z=jnp.zeros(lanes.shape,F32)
    b=64*head
    x=jnp.where(lanes==b,hi.astype(F32),jnp.where(lanes==b+1,mid.astype(F32),jnp.where(lanes==b+2,lo.astype(F32),z)))
    if one_lane: x=jnp.where(lanes==b+3,1.0,x)
    return x.astype(BF)

def build_q(q,do,o,lse,at,qx_ref,dox_ref,masked):
    lanes=lane_ids(BLK)
    prod=do.astype(F32)*o.astype(F32)
    for h in range(2):
        sel=pick(h,lanes)
        delta=jnp.sum(jnp.where(sel,prod,0.0),-1,keepdims=True)
        qx_ref[h,at,:LANES]=jnp.where(sel,q,jnp.zeros((),BF))
        qx_ref[h,at,LANES:]=aug(lse,h,lanes,masked)
        dox_ref[h,at,:LANES]=jnp.where(sel,do,jnp.zeros((),BF))
        dox_ref[h,at,LANES:]=aug(delta,h,lanes,False)

def build_k(k,v,r0,at,kx_ref,km_ref,vx_ref,frames):
    lanes=lane_ids(BLK)
    low=lanes%64
    ones=jnp.where(low<3,1.0,0.0)
    kones=ones
    if frames is not None and r0+BLK>frames:
        bad=lax.broadcasted_iota(jnp.int32,(BLK,LANES),0)+r0>=frames
        k=jnp.where(bad,jnp.zeros((),BF),k); v=jnp.where(bad,jnp.zeros((),BF),v)
        kones=jnp.where(bad&(low==3),NEG,ones)
    kx_ref[at,:LANES]=k; kx_ref[at,LANES:]=kones.astype(BF)
    vx_ref[at,:LANES]=v; vx_ref[at,LANES:]=ones.astype(BF)
    for h in range(2): km_ref[h,at,:]=jnp.where(pick(h,lanes),k,jnp.zeros((),BF))

def block_back(kx,vx,km,qx,dox,mask):
    s=nt(kx,qx)
    if mask is not None:
        cut=s.shape[0]-mask.shape[0]
        low=jnp.where(mask,s[cut:],NEG)
        s=jnp.concatenate([s[:cut],low],0) if cut else low
    p=jnp.exp2(s)
    dp=nt(vx,dox)
    ds=(p*dp).astype(BF)
    pb=p.astype(BF)
    dv=nn(pb,dox[:,:LANES])
    dk=nn(ds,qx[:,:LANES])
    dq=tn(ds,km)
    return dv,dk,dq

def self_bwd_kernel(core_ref,kept_ref,come_ref,do_ref,do_come_ref,o_ref,o_sent_ref,lse_ref,segq_ref,segk_ref,own_ref,sent_ref,
                    qx_ref,dox_ref,kx_ref,km_ref,vx_ref,dqa_ref,dka_ref,dva_ref):
    half=kept_ref.shape[1]; rows=2*half; n=rows//BLK
    core=core_ref[0]
    for ref,d,o,base in zip((kept_ref,come_ref),(do_ref,do_come_ref),(o_ref,o_sent_ref),places(core,half)):
        for r0 in range(0,half,BLK):
            here=slice(r0,r0+BLK); at=rows_at(base,r0,BLK)
            build_q(ref[0,here,:],d[here,:],o[here,:],lse_ref[at,:],at,qx_ref,dox_ref,False)
            build_k(ref[1,here,:],ref[2,here,:],0,at,kx_ref,km_ref,vx_ref,None)
    dka_ref[...]=jnp.zeros_like(dka_ref)
    dva_ref[...]=jnp.zeros_like(dva_ref)
    for i in range(n):
        r0=i*BLK; kn=r0+BLK; at=slice(r0,kn)
        cut=half if i>=n//2 else r0
        w=kn-cut
        mask=lax.broadcasted_iota(jnp.int32,(w,BLK),0)<=lax.broadcasted_iota(jnp.int32,(w,BLK),1)+(r0-cut)
        if i>=n//2: mask=mask&(segk_ref[:kn-half,:]==segq_ref[i-n//2])
        r=[block_back(kx_ref[:kn,:],vx_ref[:kn,:],km_ref[h,:kn,:],qx_ref[h,at,:],dox_ref[h,at,:],mask) for h in range(2)]
        dva_ref[:kn,:]+=r[0][0]+r[1][0]
        dka_ref[:kn,:]+=r[0][1]+r[1][1]
        dqa_ref[at,:]=((r[0][2]+r[1][2])*0.125).astype(BF)
    for ref,base in zip((own_ref,sent_ref),places(core,half)):
        at=rows_at(base,0,half)
        ref[0]=dqa_ref[at,:]
        ref[1]=(dka_ref[at,:]*(1/LOG2E)).astype(BF)
        ref[2]=dva_ref[at,:].astype(BF)

def self_bwd(core,kept,come,do,do_come,o,o_sent,lse,segq,segk):
    half,part=kept.shape[1:]; rows=2*half
    three=pl.BlockSpec((3,half,LANES),lambda p:(0,0,p))
    one=pl.BlockSpec((half,LANES),lambda p:(0,p))
    out=jax.ShapeDtypeStruct((3,half,part),BF)
    n=rows//BLK
    return pl.pallas_call(self_bwd_kernel,
        grid=(part//LANES,),
        in_specs=[scalar(),three,three,one,one,one,one,pl.BlockSpec((rows,LANES),lambda p:(0,p)),
                  pl.BlockSpec(segq.shape,lambda p:(0,0,0)),pl.BlockSpec(segk.shape,lambda p:(0,0))],
        out_specs=[three,three],
        out_shape=[out,out],
        scratch_shapes=[pltpu.VMEM((2,rows,2*LANES),BF),pltpu.VMEM((2,rows,2*LANES),BF),pltpu.VMEM((rows,2*LANES),BF),
                        pltpu.VMEM((2,rows,LANES),BF),pltpu.VMEM((rows,2*LANES),BF),pltpu.VMEM((rows,LANES),BF),
                        pltpu.VMEM((rows,LANES),F32),pltpu.VMEM((rows,LANES),F32)],
        compiler_params=pltpu.CompilerParams(vmem_limit_bytes=60*2**20),
        cost_estimate=pair_cost(n*(n+1)//2*BLK*BLK*(part//HEAD),5,20*rows*part),
        name="self_bwd",
    )(core,kept,come,do,do_come,o,o_sent,lse,segq,segk)

def cross_bwd_kernel(frames,q_ref,k_ref,v_ref,do_ref,o_ref,lse_ref,dq_ref,dk_ref,dv_ref,
                     qx_ref,dox_ref,kx_ref,km_ref,vx_ref,dka_ref,dva_ref):
    rows=q_ref.shape[0]; n=rows//BLK; kp=k_ref.shape[0]; nk=kp//BLK
    for r0 in range(0,rows,BLK):
        at=slice(r0,r0+BLK)
        build_q(q_ref[at,:],do_ref[at,:],o_ref[at,:],lse_ref[at,:],at,qx_ref,dox_ref,True)
    for r0 in range(0,kp,BLK):
        at=slice(r0,r0+BLK)
        build_k(k_ref[at,:],v_ref[at,:],r0,at,kx_ref,km_ref,vx_ref,frames)
    for i in range(rows//BLK):
        at=slice(i*BLK,(i+1)*BLK)
        r=[block_back(kx_ref[...],vx_ref[...],km_ref[h],qx_ref[h,at,:],dox_ref[h,at,:],None) for h in range(2)]
        dv=r[0][0]+r[1][0]; dk=r[0][1]+r[1][1]
        if i==0: dva_ref[...]=dv; dka_ref[...]=dk
        else: dva_ref[...]+=dv; dka_ref[...]+=dk
        dq_ref[at,:]=((r[0][2]+r[1][2])*0.125).astype(BF)
    dk_ref[...]=(dka_ref[...]*(1/LOG2E)).astype(BF)
    dv_ref[...]=dva_ref[...].astype(BF)

def cross_bwd(q,kv,frames,do,o,lse,heads):
    rows=q.shape[0]; npair=heads//2; kp=kv.shape[0]
    big=lambda f:pl.BlockSpec((rows,LANES),f)
    kb=lambda f:pl.BlockSpec((kp,LANES),f)
    return pl.pallas_call(functools.partial(cross_bwd_kernel,frames),
        grid=(npair,),
        in_specs=[big(lambda p:(0,p)),kb(lambda p:(0,p)),kb(lambda p:(0,npair+p)),big(lambda p:(0,p)),big(lambda p:(0,p)),big(lambda p:(0,p))],
        out_specs=[big(lambda p:(0,p)),kb(lambda p:(0,p)),kb(lambda p:(0,p))],
        out_shape=[jax.ShapeDtypeStruct((rows,heads*64),BF),jax.ShapeDtypeStruct((kp,heads*64),BF),jax.ShapeDtypeStruct((kp,heads*64),BF)],
        scratch_shapes=[pltpu.VMEM((2,rows,2*LANES),BF),pltpu.VMEM((2,rows,2*LANES),BF),pltpu.VMEM((kp,2*LANES),BF),
                        pltpu.VMEM((2,kp,LANES),BF),pltpu.VMEM((kp,2*LANES),BF),
                        pltpu.VMEM((kp,LANES),F32),pltpu.VMEM((kp,LANES),F32)],
        compiler_params=pltpu.CompilerParams(vmem_limit_bytes=60*2**20),
        cost_estimate=pair_cost(rows*kp*heads,5,12*rows*heads*64+8*kp*heads*64),
        name="cross_bwd",
    )(q,kv,kv,do,o,lse)


EPSILON = 1e-05
ROWS = 256
CHUNK = 768
BIG = 60 * 2**20


def whole(shape):
    return pl.BlockSpec(shape, lambda *_: (0,) * len(shape), pipeline_mode=pl.Buffered(1))


def by_rows(*lead_and_cols):
    *lead, cols = lead_and_cols
    return pl.BlockSpec((*lead, ROWS, cols), lambda i: (0,) * len(lead) + (i, 0))


def shaped(shape, dtype):
    return jax.ShapeDtypeStruct(shape, dtype)


def cost(flops, nbytes, trans=0):
    return pl.CostEstimate(flops=int(flops), bytes_accessed=int(nbytes), transcendentals=int(trans))


def normalize(values):
    centre = values - jnp.mean(values, -1, keepdims=True)
    scale = lax.rsqrt(jnp.mean(centre * centre, -1, keepdims=True) + EPSILON)
    return centre * scale, scale


def norm_grad(normed, scale, gain, grad):
    weighted = grad * gain
    return scale * (weighted - jnp.mean(weighted, -1, keepdims=True)
                    - normed * jnp.mean(weighted * normed, -1, keepdims=True))


def accumulate(ref, value):
    ref[...] = value + jnp.where(pl.program_id(0) == 0, jnp.zeros_like(value), ref[...])


def column_sum(values):
    return jnp.sum(values, 0, keepdims=True)


def qkv_heads(low, w_ref, bias_ref, at, out_ref):
    part = out_ref.shape[2]
    cols = nn(low, w_ref[at])
    out_ref[0] = ((cols[:, :part] + bias_ref[at, 0:1]) * (HEAD ** -0.5 * LOG2E)).astype(BF)
    out_ref[1] = cols[:, part:2 * part].astype(BF)
    out_ref[2] = (cols[:, 2 * part:] + bias_ref[at, 1:2]).astype(BF)


def qkv_sent_kernel(core_ref, x_ref, w_ref, gain_ref, shift_ref, bias_ref, norm_ref, sent_ref):
    normed, _ = normalize(x_ref[...].astype(F32))
    low = (normed * gain_ref[0:1] + shift_ref[0:1]).astype(BF)
    norm_ref[...] = low
    qkv_heads(low, w_ref, bias_ref, 1 - core_ref[0], sent_ref)


def qkv_kept_kernel(core_ref, norm_ref, w_ref, bias_ref, kept_ref):
    qkv_heads(norm_ref[...], w_ref, bias_ref, core_ref[0], kept_ref)


def qkv_sent(core, x, w, gain, shift, bias):
    rows, width = x.shape
    part = width // 2
    return pl.pallas_call(
        qkv_sent_kernel, grid=(rows // ROWS,),
        in_specs=[scalar(), by_rows(width), whole(w.shape), whole(gain.shape), whole(shift.shape), whole(bias.shape)],
        out_specs=[by_rows(width), by_rows(3, part)],
        out_shape=[shaped((rows, width), BF), shaped((3, rows, part), BF)],
        compiler_params=pltpu.CompilerParams(vmem_limit_bytes=BIG),
        cost_estimate=cost(3 * rows * width * width, 2 * (3 * width * width + 4 * rows * width)), name="qkv_sent",
    )(core, x, w, gain, shift, bias)


def qkv_kept(core, norm, w, bias):
    rows, width = norm.shape
    part = width // 2
    return pl.pallas_call(
        qkv_kept_kernel, grid=(rows // ROWS,),
        in_specs=[scalar(), by_rows(width), whole(w.shape), whole(bias.shape)],
        out_specs=by_rows(3, part), out_shape=shaped((3, rows, part), BF),
        compiler_params=pltpu.CompilerParams(vmem_limit_bytes=BIG),
        cost_estimate=cost(3 * rows * width * width, 2 * (3 * width * width + 3 * rows * width)), name="qkv_kept",
    )(core, norm, w, bias)


def memory_kernel(frames, mine_ref, own_ref, come_ref, w_ref, bias_ref, kv_ref, mem_ref):
    width = own_ref.shape[1]
    part = width // 2
    mem = jnp.where(mine_ref[0] == 1, own_ref[...], come_ref[...])
    row = lax.broadcasted_iota(jnp.int32, mem.shape, 0) + pl.program_id(0) * ROWS
    mem = jnp.where(row < frames, mem, jnp.zeros((), BF))
    mem_ref[...] = mem
    for t in range(2):
        cols = nn(mem, w_ref[t])
        kv_ref[:, t * part:(t + 1) * part] = cols[:, :part].astype(BF)
        kv_ref[:, width + t * part:width + (t + 1) * part] = (cols[:, part:] + bias_ref[4:5, t * part:(t + 1) * part]).astype(BF)


def memory_project(mine, own, come, w_mid, bias):
    frames, width = own.shape
    steps = pl.cdiv(frames, ROWS)
    return pl.pallas_call(
        functools.partial(memory_kernel, frames), grid=(steps,),
        in_specs=[scalar(), by_rows(width), by_rows(width),
                  pl.BlockSpec((2, width, width), lambda i: (0, 0, 1), pipeline_mode=pl.Buffered(1)), whole(bias.shape)],
        out_specs=[by_rows(2 * width), by_rows(width)],
        out_shape=[shaped((steps * ROWS, 2 * width), BF), shaped((steps * ROWS, width), BF)],
        compiler_params=pltpu.CompilerParams(vmem_limit_bytes=BIG),
        cost_estimate=cost(4 * frames * width * width, 2 * (2 * width * width + 5 * frames * width)), name="memory_project",
    )(mine, own, come, w_mid, bias)


def middle_kernel(core_ref, x_ref, own_ref, come_ref, wo_ref, wq_ref, gain_ref, shift_ref, bias_ref,
                  resid_ref, norm_ref, q_ref):
    part = own_ref.shape[1]
    core = core_ref[0]
    resid = x_ref[...].astype(F32) + nt(own_ref[...], wo_ref[core]) + nt(come_ref[...], wo_ref[1 - core]) + bias_ref[2:3]
    resid_ref[...] = resid
    normed, _ = normalize(resid)
    low = (normed * gain_ref[1:2] + shift_ref[1:2]).astype(BF)
    norm_ref[...] = low
    for t in range(2):
        at = slice(t * part, (t + 1) * part)
        q_ref[:, at] = ((nn(low, wq_ref[t]) + bias_ref[3:4, at]) * (HEAD ** -0.5 * LOG2E)).astype(BF)


def middle(core, x, own, come, w_mid, gain, shift, bias):
    rows, width = x.shape
    part = width // 2
    w_at = lambda c: pl.BlockSpec((2, width, part), lambda i: (0, 0, c), pipeline_mode=pl.Buffered(1))
    return pl.pallas_call(
        middle_kernel, grid=(rows // ROWS,),
        in_specs=[scalar(), by_rows(width), by_rows(part), by_rows(part), w_at(0), w_at(1),
                  whole(gain.shape), whole(shift.shape), whole(bias.shape)],
        out_specs=[by_rows(width)] * 3,
        out_shape=[shaped((rows, width), F32), shaped((rows, width), BF), shaped((rows, width), BF)],
        compiler_params=pltpu.CompilerParams(vmem_limit_bytes=BIG),
        cost_estimate=cost(4 * rows * width * width, 4 * width * width + 12 * rows * width), name="middle",
    )(core, x, own, come, w_mid, w_mid, gain, shift, bias)


def gelu_parts(v):
    z = jnp.abs(v) * (0.5 ** 0.5)
    t = 1.0 / (1.0 + 0.3275911 * z)
    bell = jnp.exp2(v * v * (-0.5 * LOG2E))
    poly = ((((1.061405429 * t - 1.453152027) * t + 1.421413741) * t - 0.284496736) * t + 0.254829592) * t
    tail = (0.5 * poly) * bell
    phi = jnp.where(v >= 0, 1.0 - tail, tail)
    return phi, phi + v * bell * 0.3989422804014327


def feed_kernel(mine_ref, attn_ref, resid_ref, g_own_ref, g_come_ref, wo_ref, wi_ref, wm_ref, gain_ref, shift_ref, bias_ref, unit_bias_ref, out_bias_ref,
                out_ref, norm_ref, hidden_ref, dpre_ref, g2_ref, dattn_ref, g_ref,
                sum_g_ref, sum_dpre_ref, sum_g2_ref, sum_gain_ref, sum_shift_ref):
    part = wo_ref.shape[2]
    units = wi_ref.shape[2]
    resid = resid_ref[...] + bias_ref[5:6]
    for t in range(2):
        resid = resid + nt(attn_ref[:, t * part:(t + 1) * part], wo_ref[t])
    normed, scale = normalize(resid)
    low = (normed * gain_ref[2:3] + shift_ref[2:3]).astype(BF)
    norm_ref[...] = low
    g_low = jnp.where(mine_ref[0] == 1, g_own_ref[...], g_come_ref[...])
    g_ref[...] = g_low
    out = resid + out_bias_ref[...]
    back = jnp.zeros_like(resid)
    sums = []
    spots = [(t, c) for t in range(2) for c in range(0, units, CHUNK)]

    def first(spot):
        t, c = spot
        at = slice(t * units + c, t * units + c + CHUNK)
        return nn(low, wi_ref[t, :, c:c + CHUNK]) + unit_bias_ref[:, at], nn(g_low, wm_ref[t, :, c:c + CHUNK])

    ahead = first(spots[0])
    for k, (t, c) in enumerate(spots):
        at = slice(t * units + c, t * units + c + CHUNK)
        pre, back_hidden = ahead
        if k + 1 < len(spots):
            ahead = first(spots[k + 1])
        phi, slope = gelu_parts(pre)
        hidden = (pre * phi).astype(BF)
        hidden_ref[:, at] = hidden
        out = out + nt(hidden, wm_ref[t, :, c:c + CHUNK])
        dpre = back_hidden * slope
        sums.append(column_sum(dpre))
        dpre = dpre.astype(BF)
        dpre_ref[:, at] = dpre
        back = back + nt(dpre, wi_ref[t, :, c:c + CHUNK])
    out_ref[...] = out.astype(BF)
    sums = jnp.concatenate(sums, 1)
    wide = sum_dpre_ref.shape[1]
    accumulate(sum_dpre_ref, jnp.concatenate([sums[:, i * wide:(i + 1) * wide] for i in range(sum_dpre_ref.shape[0])], 0))
    g = g_low.astype(F32)
    accumulate(sum_g_ref, column_sum(g))
    accumulate(sum_gain_ref, column_sum(back * normed))
    accumulate(sum_shift_ref, column_sum(back))
    g2 = g + norm_grad(normed, scale, gain_ref[2:3], back)
    accumulate(sum_g2_ref, column_sum(g2))
    g2_ref[...] = g2
    g2_low = g2.astype(BF)
    for t in range(2):
        dattn_ref[:, t * part:(t + 1) * part] = nn(g2_low, wo_ref[t]).astype(BF)


def feed(mine, attn, resid, g_own, g_come, w_mid, w_ff, gain, shift, bias, unit_bias, out_bias):
    rows, width = resid.shape
    part = width // 2
    units = w_ff.shape[2] // 2
    w_at = lambda cols, c: pl.BlockSpec((2, width, cols), lambda i: (0, 0, c), pipeline_mode=pl.Buffered(1))
    line = lambda count: (pl.BlockSpec((count, width), lambda i: (0, 0)), shaped((count, width), F32))
    lines = [line(1), line(2 * units // width), line(1), line(1), line(1)]
    return pl.pallas_call(
        feed_kernel, grid=(rows // ROWS,),
        in_specs=[scalar(), by_rows(width), by_rows(width), by_rows(width), by_rows(width), w_at(part, 4), w_at(units, 0), w_at(units, 1),
                  whole(gain.shape), whole(shift.shape), whole(bias.shape), whole(unit_bias.shape), whole(out_bias.shape)],
        out_specs=[by_rows(width), by_rows(width), by_rows(2 * units), by_rows(2 * units), by_rows(width), by_rows(width), by_rows(width)] + [a for a, _ in lines],
        out_shape=[shaped((rows, width), BF), shaped((rows, width), BF), shaped((rows, 2 * units), BF), shaped((rows, 2 * units), BF),
                   shaped((rows, width), F32), shaped((rows, width), BF), shaped((rows, width), BF)] + [b for _, b in lines],
        compiler_params=pltpu.CompilerParams(vmem_limit_bytes=BIG),
        cost_estimate=cost(2 * rows * width * (2 * width + 8 * units), 2 * width * (width + 4 * units) + 2 * rows * (8 * width + 4 * units), 4 * rows * units),
        name="feed",
    )(mine, attn, resid, g_own, g_come, w_mid, w_ff, w_ff, gain, shift, bias, unit_bias, out_bias)


def feed_weights_kernel(norm_ref, g_ref, dpre_ref, hidden_ref, out_ref):
    cols = dpre_ref.shape[1]
    out_ref[0, :, :cols] = tn(norm_ref[...], dpre_ref[...]).astype(BF)
    out_ref[0, :, cols:] = tn(g_ref[...], hidden_ref[...]).astype(BF)


def feed_weights(norm, g, dpre, hidden):
    rows, width = norm.shape
    units = dpre.shape[1] // 2
    cols = units // 2
    return pl.pallas_call(
        feed_weights_kernel, grid=(2, 2),
        in_specs=[whole(norm.shape), whole(g.shape), pl.BlockSpec((rows, cols), lambda t, c: (0, 2 * t + c)),
                  pl.BlockSpec((rows, cols), lambda t, c: (0, 2 * t + c))],
        out_specs=pl.BlockSpec((1, width, 2 * cols), lambda t, c: (t, 0, c)),
        out_shape=shaped((2, width, 2 * units), BF),
        compiler_params=pltpu.CompilerParams(vmem_limit_bytes=BIG),
        cost_estimate=cost(8 * rows * width * units, 2 * (4 * width * units + 4 * rows * units)), name="feed_weights",
    )(norm, g, dpre, hidden)


def middle_back_kernel(core_ref, dq_ref, resid_ref, g2_ref, wq_ref, wo_ref, gain_ref,
                       g1_ref, kept_ref, sent_ref, sum_dq_ref, sum_g1_ref, sum_gain_ref, sum_shift_ref):
    part = kept_ref.shape[1]
    core = core_ref[0]
    dq = dq_ref[...]
    back = nt(dq[:, :part], wq_ref[0]) + nt(dq[:, part:], wq_ref[1])
    accumulate(sum_dq_ref, column_sum(dq.astype(F32)))
    normed, scale = normalize(resid_ref[...])
    accumulate(sum_gain_ref, column_sum(back * normed))
    accumulate(sum_shift_ref, column_sum(back))
    g1 = g2_ref[...] + norm_grad(normed, scale, gain_ref[1:2], back)
    g1_ref[...] = g1
    accumulate(sum_g1_ref, column_sum(g1))
    low = g1.astype(BF)
    kept_ref[...] = nn(low, wo_ref[core]).astype(BF)
    sent_ref[...] = nn(low, wo_ref[1 - core]).astype(BF)


def middle_back(core, dq, resid, g2, w_mid, gain):
    rows, width = resid.shape
    part = width // 2
    w_at = lambda c: pl.BlockSpec((2, width, part), lambda i: (0, 0, c), pipeline_mode=pl.Buffered(1))
    line = pl.BlockSpec((1, width), lambda i: (0, 0))
    return pl.pallas_call(
        middle_back_kernel, grid=(rows // ROWS,),
        in_specs=[scalar(), by_rows(width), by_rows(width), by_rows(width), w_at(1), w_at(0), whole(gain.shape)],
        out_specs=[by_rows(width), by_rows(part), by_rows(part)] + [line] * 4,
        out_shape=[shaped((rows, width), F32), shaped((rows, part), BF), shaped((rows, part), BF)] + [shaped((1, width), F32)] * 4,
        compiler_params=pltpu.CompilerParams(vmem_limit_bytes=BIG),
        cost_estimate=cost(4 * rows * width * width, 4 * width * width + 18 * rows * width), name="middle_back",
    )(core, dq, resid, g2, w_mid, w_mid, gain)


def middle_weights_kernel(core_ref, g1_ref, own_ref, come_ref, norm_ref, dq_ref, mem_ref, dk_ref, dv_ref, g2_ref, attn_ref,
                          out_ref, sum_dv_ref):
    part = own_ref.shape[1]
    attn_self = jnp.where(pl.program_id(0) == core_ref[0], own_ref[...], come_ref[...])
    out_ref[0, :, :part] = tn(g1_ref[...].astype(BF), attn_self).astype(BF)
    out_ref[0, :, part:2 * part] = tn(norm_ref[...], dq_ref[...]).astype(BF)
    mem = mem_ref[...]
    out_ref[0, :, 2 * part:3 * part] = tn(mem, dk_ref[...]).astype(BF)
    out_ref[0, :, 3 * part:4 * part] = tn(mem, dv_ref[...]).astype(BF)
    out_ref[0, :, 4 * part:] = tn(g2_ref[...].astype(BF), attn_ref[...]).astype(BF)
    sum_dv_ref[...] = column_sum(dv_ref[...].astype(F32))


def middle_weights(core, g1, own, come, norm, dq, mem, dk, dv, g2, attn):
    rows, width = norm.shape
    frames = mem.shape[0]
    part = width // 2
    half = lambda n: pl.BlockSpec((n, part), lambda t: (0, t))
    return pl.pallas_call(
        middle_weights_kernel, grid=(2,),
        in_specs=[scalar(), whole(g1.shape), whole(own.shape), whole(come.shape), whole(norm.shape), half(rows), whole(mem.shape),
                  half(frames), half(frames), whole(g2.shape), half(rows)],
        out_specs=[pl.BlockSpec((1, width, 5 * part), lambda t: (t, 0, 0)), pl.BlockSpec((1, part), lambda t: (0, t))],
        out_shape=[shaped((2, width, 5 * part), BF), shaped((1, width), F32)],
        compiler_params=pltpu.CompilerParams(vmem_limit_bytes=BIG),
        cost_estimate=cost(2 * width * width * (3 * rows + 2 * frames), 10 * width * width + 2 * width * (10 * rows + 3 * frames)),
        name="middle_weights",
    )(core, g1, own, come, norm, dq, mem, dk, dv, g2, attn)


def qkv_back_kernel(core_ref, own_ref, come_ref, x_ref, g1_ref, w_ref, gain_ref, grad_ref, sum_gain_ref, sum_shift_ref):
    part = own_ref.shape[2]
    core = core_ref[0]
    back = jnp.zeros(x_ref.shape, F32)
    for ref, at in ((own_ref, core), (come_ref, 1 - core)):
        for j in range(3):
            back = back + nt(ref[j], w_ref[at, :, j * part:(j + 1) * part])
    normed, scale = normalize(x_ref[...].astype(F32))
    accumulate(sum_gain_ref, column_sum(back * normed))
    accumulate(sum_shift_ref, column_sum(back))
    grad_ref[...] = (g1_ref[...] + norm_grad(normed, scale, gain_ref[0:1], back)).astype(BF)


def qkv_back(core, own, come, x, g1, w, gain):
    rows, width = x.shape
    part = width // 2
    line = pl.BlockSpec((1, width), lambda i: (0, 0))
    return pl.pallas_call(
        qkv_back_kernel, grid=(rows // ROWS,),
        in_specs=[scalar(), by_rows(3, part), by_rows(3, part), by_rows(width), by_rows(width), whole(w.shape), whole(gain.shape)],
        out_specs=[by_rows(width), line, line],
        out_shape=[shaped((rows, width), BF), shaped((1, width), F32), shaped((1, width), F32)],
        compiler_params=pltpu.CompilerParams(vmem_limit_bytes=BIG),
        cost_estimate=cost(6 * rows * width * width, 2 * (3 * width * width + 7 * rows * width)), name="qkv_back",
    )(core, own, come, x, g1, w, gain)


def qkv_weights_kernel(core_ref, norm_ref, own_ref, come_ref, out_ref, sum_q_ref, sum_v_ref):
    part = own_ref.shape[2]
    mine = pl.program_id(0) == core_ref[0]
    norm = norm_ref[...]
    for j in range(3):
        grad = jnp.where(mine, own_ref[j], come_ref[j])
        out_ref[0, :, j * part:(j + 1) * part] = tn(norm, grad).astype(BF)
        if j != 1:
            (sum_q_ref if j == 0 else sum_v_ref)[...] = column_sum(grad.astype(F32))


def qkv_weights(core, norm, own, come):
    rows, width = norm.shape
    part = width // 2
    return pl.pallas_call(
        qkv_weights_kernel, grid=(2,),
        in_specs=[scalar(), whole(norm.shape), whole(own.shape), whole(come.shape)],
        out_specs=[pl.BlockSpec((1, width, 3 * part), lambda t: (t, 0, 0)), pl.BlockSpec((1, part), lambda t: (0, t)), pl.BlockSpec((1, part), lambda t: (0, t))],
        out_shape=[shaped((2, width, 3 * part), BF), shaped((1, width), F32), shaped((1, width), F32)],
        compiler_params=pltpu.CompilerParams(vmem_limit_bytes=BIG),
        cost_estimate=cost(6 * rows * width * width, 2 * (3 * width * width + 4 * rows * width)), name="qkv_weights",
    )(core, norm, own, come)


def bit_names(chips):
    return ["t"] + ["k%d" % b for b in reversed(range((chips - 1).bit_length()))] + ["core"]


def my_bit(name):
    if name == "t":
        return lax.axis_index("tensor")
    if name == "core":
        return lax.axis_index("core")
    return lax.axis_index("chip") // 2 ** int(name[1:]) % 2


def partner(name):
    bit = my_bit(name)
    if name == "t":
        return {"tensor": 1 - bit}
    if name == "core":
        return {"core": 1 - bit}
    return {"chip": lax.axis_index("chip") + 2 ** int(name[1:]) * (1 - 2 * bit)}


def greet(names, *others):
    barrier = pltpu.get_barrier_semaphore()
    for device in [partner(name) for name in names] + list(others):
        pl.semaphore_signal(barrier, inc=1, device_id=device, device_id_type=pl.DeviceIdType.MESH)
    pl.semaphore_wait(barrier, len(names) + len(others))


def exchange_orders(names):
    low = [n for n in reversed(names) if n[0] == "k"]
    return [["core", "t"] + low, ["core"] + low + ["t"], ["core"] + low[1:] + ["t"] + low[:1]]


def stream_cols(cols, count):
    tiles = cols // LANES
    cuts = [tiles * i // count * LANES for i in range(count + 1)]
    return [slice(a, b) for a, b in zip(cuts, cuts[1:])]


def gather_kernel(names, orders, own_ref, seg_ref, x_ref, out_ref, seg_out_ref, moved_ref, block, segs, local_sem, send_sem, recv_sem):
    core, tensor = lax.axis_index("core"), lax.axis_index("tensor")
    greet(names, {"core": 1 - core, "tensor": 1 - tensor})
    spare = len(orders)
    swap = pltpu.make_async_remote_copy(x_ref, moved_ref, send_sem.at[spare, 2], recv_sem.at[spare, 2],
                                        device_id={"core": tensor, "tensor": core}, device_id_type=pl.DeviceIdType.MESH)
    stay = pltpu.make_async_copy(x_ref, moved_ref, local_sem.at[1])

    @pl.when(core != tensor)
    def _():
        swap.start()

    @pl.when(core == tensor)
    def _():
        stay.start()

    pieces, _, part = own_ref.shape
    for i in range(pieces):
        block[:, i * part:(i + 1) * part] = own_ref[i]
    lanes = stream_cols(block.shape[1], len(orders))
    place = tuple(my_bit(n) for n in names)
    known = [[] for _ in orders]
    sent = []
    flying = [None] * len(orders)

    def send(src, dst, st, step, name):
        copy = pltpu.make_async_remote_copy(src, dst, send_sem.at[st, step], recv_sem.at[st, step],
                                            device_id=partner(name), device_id_type=pl.DeviceIdType.MESH)
        copy.start()
        sent.append(copy)
        return copy

    def start(st, step):
        name = orders[st][step]
        at = tuple(slice(None) if n in known[st] else my_bit(n) for n in names)
        dst = out_ref.at[at + (slice(None), lanes[st])]
        flying[st] = send(dst if step else block.at[:, lanes[st]], dst, st, step, name)
        known[st].append(name)

    for st in range(len(orders)):
        start(st, 0)
    local = pltpu.make_async_copy(block, out_ref.at[place], local_sem.at[0])
    local.start()
    segs[core, tensor] = seg_ref[...]
    along = send(segs.at[core, tensor], segs.at[core, tensor], spare, 0, "t")
    local.wait()
    for step in range(len(names)):
        for st in range(len(orders)):
            flying[st].wait_recv()
            if step + 1 < len(names):
                start(st, step + 1)
        if step == 0:
            along.wait_recv()
            along = send(segs.at[core], segs.at[core], spare, 1, "core")
    along.wait_recv()
    seg_out_ref[...] = segs[tensor, 1]
    for copy in sent:
        copy.wait_send()

    @pl.when(core != tensor)
    def _():
        swap.wait()

    @pl.when(core == tensor)
    def _():
        stay.wait()


def gather_all(shard, seg, x, chips):
    names = bit_names(chips)
    orders = [list(reversed(o)) for o in exchange_orders(names)]
    pieces, rows, part = shard.shape
    cols = pieces * part
    dma = pltpu.SemaphoreType.DMA
    vmem = pl.BlockSpec(memory_space=pltpu.VMEM)
    seg = seg.reshape(-1, LANES)
    hbm = pl.BlockSpec(memory_space=pl.ANY)
    full, seg, moved = pl.pallas_call(
        functools.partial(gather_kernel, names, orders),
        in_specs=[vmem, vmem, hbm], out_specs=[hbm, vmem, hbm],
        out_shape=[shaped((2,) * len(names) + (rows, cols), shard.dtype), shaped(seg.shape, seg.dtype), shaped(x.shape, x.dtype)],
        scratch_shapes=[pltpu.VMEM((rows, cols), shard.dtype), pltpu.VMEM((2, 2) + seg.shape, seg.dtype),
                        dma((2,)), dma((len(orders) + 1, len(names))), dma((len(orders) + 1, len(names)))],
        compiler_params=pltpu.CompilerParams(collective_id=0, has_side_effects=True, vmem_limit_bytes=BIG),
        cost_estimate=cost(0, 1e6), name="gather_all",
    )(shard, seg, x)
    return full.reshape(2, -1, cols), seg.reshape(-1), moved


class Sums:
    def __init__(self, names, send_sem, recv_sem):
        self.names, self.sems, self.streams = names, (send_sem, recv_sem), []

    def add(self, sent_ref, kept_ref, order, recv, held, out):
        self.streams.append(dict(sent=sent_ref, kept=kept_ref, order=order, recv=recv, held=held, out=out, left=list(self.names),
                                 step=0, copies=[]))
        return len(self.streams) - 1

    def start(self, k):
        s = self.streams[k]
        name = s["order"][s["step"]]
        src = s["sent"] if s["kept"] is None else s["sent"].at[tuple(1 - my_bit(n) if n == name else slice(None) for n in s["left"])]
        copy = pltpu.make_async_remote_copy(src, s["recv"][s["step"]], self.sems[0].at[k, s["step"]], self.sems[1].at[k, s["step"]],
                                            device_id=partner(name), device_id_type=pl.DeviceIdType.MESH)
        copy.start()
        s["copies"].append(copy)

    def advance(self, k):
        s = self.streams[k]
        step = s["step"]
        if step == len(self.names):
            return
        s["copies"][-1].wait_recv()
        name = s["order"][step]
        if s["kept"] is None:
            total = s["sent"][...] + s["recv"][step][...]
        else:
            kept = s["kept"].at[tuple(my_bit(n) if n == name else slice(None) for n in s["left"])]
            total = kept[...].astype(F32) + s["recv"][step][...].astype(F32)
            s["left"].remove(name)
        s["step"] += 1
        if s["step"] == len(self.names):
            s["out"](total)
            return
        held = s["held"][step]
        held[...] = total.astype(held.dtype)
        if s["kept"] is not None:
            s["kept"] = held
        s["sent"] = held
        self.start(k)

    def finish(self):
        for _ in self.names:
            for k in range(len(self.streams)):
                self.advance(k)
        for s in self.streams:
            for copy in s["copies"]:
                copy.wait_send()


def part_streams(cols, part, count):
    return [slice(a.start * part, a.stop * part) for a in stream_parts(cols // part, count)]


def stream_parts(parts, count):
    cuts = [parts * i // count for i in range(count + 1)]
    return [slice(a, b) for a, b in zip(cuts, cuts[1:])]


def sum_bufs(steps, rows, lanes):
    recv = [pltpu.VMEM((2,) * (steps - 1 - i) + (rows, lane.stop - lane.start), BF) for lane in lanes for i in range(steps)]
    held = [pltpu.VMEM((2,) * (steps - 1 - i) + (rows, lane.stop - lane.start), BF) for lane in lanes for i in range(steps - 1)]
    return recv + held


def split_bufs(bufs, steps, count):
    recv, held = bufs[:count * steps], bufs[count * steps:]
    return [(recv[st * steps:(st + 1) * steps], held[st * (steps - 1):(st + 1) * (steps - 1)]) for st in range(count)]


def put_pieces(lane, part, place):
    def out(total):
        for at in range(lane.start, lane.stop, part):
            place(at // part, total[:, at - lane.start:at - lane.start + part])
    return out


def unpack_ff(ff_ref, ff_in_ref, ff_out_ref):
    quarter = ff_ref.shape[1] // 4
    for i in range(4):
        ref, at = (ff_out_ref if i % 2 else ff_in_ref), i // 2 * quarter
        ref[:, at:at + quarter] = ff_ref[:, i * quarter:(i + 1) * quarter].astype(F32)


def fill_rows(ref, values):
    row = 0
    for value in values:
        ref[row:row + value.shape[0]] = value
        row += value.shape[0]
    if row < ref.shape[0]:
        ref[row:] = jnp.zeros((ref.shape[0] - row, ref.shape[1]), F32)


def sum_kernel(names, orders, lanes, smalls, pieces, grad_ref, ff_ref, *refs):
    small_refs, refs = refs[:smalls], refs[smalls:]
    qkv_ref, *out_refs = refs[:pieces + 1]
    small_out_ref, ff_in_ref, ff_out_ref, small_first, small_recv, small_held, send_sem, recv_sem, *bufs = refs[pieces + 1:]
    greet(names)
    steps = len(names)

    def place(i, value):
        if i < 3:
            qkv_ref[i] = value
        else:
            out_refs[i - 3][...] = value

    def small_out(total):
        small_out_ref[...] = total

    sums = Sums(names, send_sem, recv_sem)
    part = qkv_ref.shape[2]
    for lane, order, (recv, held) in zip(lanes, orders, split_bufs(bufs, steps, len(lanes))):
        ref = grad_ref.at[(slice(None),) * (steps + 1) + (lane,)]
        sums.start(sums.add(ref, ref, order, recv, held, put_pieces(lane, part, place)))
    fill_rows(small_first, [ref[...] for ref in small_refs])
    sums.start(sums.add(small_first, None, orders[0], [small_recv.at[i] for i in range(steps)],
                        [small_held.at[i] for i in range(steps - 1)], small_out))
    unpack_ff(ff_ref, ff_in_ref, ff_out_ref)
    sums.finish()


def small_bufs(steps, small):
    shape = ((sum(s.shape[0] for s in small) + 7) // 8 * 8, small[-1].shape[1])
    return shape, [pltpu.VMEM(shape, F32), pltpu.VMEM((steps,) + shape, F32), pltpu.VMEM((steps,) + shape, F32)]


def sum_all(grad, ff, small, chips):
    names = bit_names(chips)
    orders = exchange_orders(names)
    cols = grad.shape[2]
    rows = grad.shape[1] // (2 * chips)
    steps = len(names)
    part = small[0].shape[1] // 2
    pieces = cols // part - 3
    lanes = part_streams(cols, part, len(orders))
    shape, extra = small_bufs(steps, small)
    dma = pltpu.SemaphoreType.DMA
    vmem = pl.BlockSpec(memory_space=pltpu.VMEM)
    return pl.pallas_call(
        functools.partial(sum_kernel, names, orders, lanes, len(small), pieces),
        in_specs=[vmem] * (2 + len(small)), out_specs=[vmem] * (pieces + 4),
        out_shape=[shaped((3, rows, part), F32)] + [shaped((rows, part), F32)] * pieces
        + [shaped(shape, F32)] + [shaped((rows, ff.shape[1] // 2), F32)] * 2,
        scratch_shapes=extra + [dma((len(orders) + 1, steps)), dma((len(orders) + 1, steps))] + sum_bufs(steps, rows, lanes),
        compiler_params=pltpu.CompilerParams(collective_id=1, has_side_effects=True, vmem_limit_bytes=BIG),
        cost_estimate=cost(0, 1e6), name="sum_all",
    )(grad.reshape((2,) * steps + (rows, cols)), ff, *small)


def end_kernel(names, orders, mid_lanes, qkv_lanes, smalls, mid_hbm, kept_hbm, come_hbm, x_hbm, norm_hbm, g1_hbm, w_hbm,
               gain_ref, ff_ref, *refs):
    small_refs, refs = refs[:smalls], refs[smalls:]
    qkv_ref, refs = refs[0], refs[1:]
    pieces = len(mid_lanes)
    parts = mid_hbm.shape[-1] // qkv_ref.shape[2]
    mid_refs, refs = refs[:parts], refs[parts:]
    (small_out_ref, ff_in_ref, ff_out_ref, moved_ref, mid, kept, come, x, norm, g1, w, grad_qkv, grad_low, small_first, small_recv,
     small_held, load_sem, send_sem, recv_sem, *bufs) = refs
    core, tensor = lax.axis_index("core"), lax.axis_index("tensor")
    steps = len(names)
    part = qkv_ref.shape[2]
    loads = [pltpu.make_async_copy(src, dst, load_sem.at[i]) for i, (src, dst) in enumerate(
        ((mid_hbm, mid), (w_hbm, w), (kept_hbm, kept), (come_hbm, come), (x_hbm, x), (g1_hbm, g1), (norm_hbm, norm)))]
    for load in loads[1:] + loads[:1]:
        load.start()
    greet(names, {"core": 1 - core, "tensor": 1 - tensor})
    sums = Sums(names, send_sem, recv_sem)
    split = len(mid_lanes) * (2 * steps - 1)
    everything = (slice(None),) * (steps + 1)

    def mid_place(i, value):
        mid_refs[i][...] = value

    def qkv_place(i, value):
        qkv_ref[i] = value

    def small_out(total):
        small_out_ref[...] = total

    for lane, order, (recv, held) in zip(mid_lanes, orders, split_bufs(bufs[:split], steps, len(mid_lanes))):
        at = everything + (lane,)
        sums.start(sums.add(mid_hbm.at[at], mid.at[at], order, recv, held, put_pieces(lane, part, mid_place)))

    def step_mid():
        for k in range(pieces):
            sums.advance(k)

    for load in loads[1:6]:
        load.wait()
    rows, width = x.shape
    gains, shifts = 0.0, 0.0
    for b in range(rows // ROWS):
        at = slice(b * ROWS, (b + 1) * ROWS)
        back = jnp.zeros((ROWS, width), F32)
        for ref, t in ((kept, core), (come, 1 - core)):
            for j in range(3):
                back = back + nt(ref[j, at, :], w[t, :, j * part:(j + 1) * part])
        normed, scale = normalize(x[at, :].astype(F32))
        gains = gains + column_sum(back * normed)
        shifts = shifts + column_sum(back)
        grad_low[at, :] = (g1[at, :] + norm_grad(normed, scale, gain_ref[0:1], back)).astype(BF)
        if b == 1:
            loads[0].wait()
            step_mid()
    spare = len(sums.streams) + len(qkv_lanes) + 1
    swap = pltpu.make_async_remote_copy(grad_low, moved_ref, send_sem.at[spare, 0], recv_sem.at[spare, 0],
                                        device_id={"core": tensor, "tensor": core}, device_id_type=pl.DeviceIdType.MESH)
    stay = pltpu.make_async_copy(grad_low, moved_ref, load_sem.at[7])

    @pl.when(core != tensor)
    def _():
        swap.start()

    @pl.when(core == tensor)
    def _():
        stay.start()

    step_mid()
    loads[6].wait()
    bias = []
    for ref, t in ((kept, core), (come, 1 - core)):
        for j in range(3):
            grad = tn(norm[...], ref[j]).astype(BF)
            grad_qkv[(t,) + everything[1:] + (slice(j * part, (j + 1) * part),)] = grad.reshape(grad_qkv.shape[1:-1] + (part,))
            bias.append(column_sum(ref[j].astype(F32)))
        step_mid()
    for lane, order, (recv, held) in zip(qkv_lanes, orders, split_bufs(bufs[split:], steps, len(qkv_lanes))):
        ref = grad_qkv.at[everything + (lane,)]
        sums.start(sums.add(ref, ref, order, recv, held, put_pieces(lane, part, qkv_place)))

    def line(j):
        return jnp.concatenate([jnp.where(core == 0, bias[j], bias[3 + j]), jnp.where(core == 0, bias[3 + j], bias[j])], 1)

    small = [ref[...] for ref in small_refs]
    fill_rows(small_first, [gains, *small[:2], shifts, *small[2:4], line(0), line(2), *small[4:]])
    sums.start(sums.add(small_first, None, orders[0], [small_recv.at[i] for i in range(steps)],
                        [small_held.at[i] for i in range(steps - 1)], small_out))
    unpack_ff(ff_ref, ff_in_ref, ff_out_ref)
    sums.finish()

    @pl.when(core != tensor)
    def _():
        swap.wait()

    @pl.when(core == tensor)
    def _():
        stay.wait()


def end_all(mid, kept, come, x, norm, g1, w, gain, ff, small, chips):
    names = bit_names(chips)
    orders = exchange_orders(names)
    steps = len(names)
    rows, width = x.shape
    part = width // 2
    here = width // (2 * chips)
    mid_cols = mid.shape[2]
    mid_lanes = part_streams(mid_cols, part, len(orders))
    qkv_lanes = part_streams(3 * part, part, len(orders))
    pieces = mid_cols // part
    shape, extra = small_bufs(steps, small + [jnp.zeros((4, width), F32)])
    dma = pltpu.SemaphoreType.DMA
    vmem, hbm = pl.BlockSpec(memory_space=pltpu.VMEM), pl.BlockSpec(memory_space=pl.ANY)
    lead = (2,) * steps
    mid = mid.reshape(lead + (here, mid_cols))
    count = len(orders) * 2 + 2
    return pl.pallas_call(
        functools.partial(end_kernel, names, orders, mid_lanes, qkv_lanes, len(small)),
        in_specs=[hbm] * 7 + [vmem] * (2 + len(small)), out_specs=[vmem] * (pieces + 4) + [hbm],
        out_shape=[shaped((3, here, part), F32)] + [shaped((here, part), F32)] * pieces
        + [shaped(shape, F32)] + [shaped((here, ff.shape[1] // 2), F32)] * 2 + [shaped((rows, width), BF)],
        scratch_shapes=[pltpu.VMEM(v.shape, v.dtype) for v in (mid, kept, come, x, norm, g1, w)]
        + [pltpu.VMEM(lead + (here, 3 * part), BF), pltpu.VMEM((rows, width), BF)] + extra
        + [dma((8,)), dma((count, steps)), dma((count, steps))]
        + sum_bufs(steps, here, mid_lanes) + sum_bufs(steps, here, qkv_lanes),
        compiler_params=pltpu.CompilerParams(collective_id=1, has_side_effects=True, vmem_limit_bytes=BIG),
        cost_estimate=cost(0, 1e6), name="end_all",
    )(mid, kept, come, x, norm, g1, w, gain, ff, *small)


ALL = ("tensor", "chip", "core")


def fetch(shard):
    full = lax.all_gather(shard, ALL, axis=0, tiled=True)
    return full.reshape(2, -1, shard.shape[1])


def spread_sum(grad):
    return lax.psum_scatter(grad.reshape(-1, grad.shape[2]), ALL, scatter_dimension=0, tiled=True)


def on_device(tokens, memory, seg_ids, positions, grad_output, attn_in, attn_out, cross_q, cross_kv,
              cross_out, mlp_in, mlp_out, norm_gain, norm_bias, proj_bias, mlp_bias, out_bias):
    width = tokens.shape[1]
    rows_here, _, part = attn_in.shape
    units = mlp_in.shape[1]
    heads = width // HEAD
    frames = memory.shape[1]
    core = lax.axis_index("core")
    tensor = lax.axis_index("tensor")
    core_at = core.astype(jnp.int32).reshape(1)
    swap = [(0, 0), (1, 2), (2, 1), (3, 3)]
    mine = (core == tensor).astype(jnp.int32).reshape(1)
    fix = lambda x: lax.ppermute(x, ("core", "tensor"), swap)
    other = lambda x: lax.ppermute(x, "core", [(0, 1), (1, 0)])

    chips = lax.axis_size("chip")
    mid = jnp.concatenate([attn_out.T, cross_q, cross_kv.reshape(rows_here, 2 * part), cross_out.T], 1)
    first, mid = lax.optimization_barrier((attn_in.transpose(1, 0, 2), mid))
    w_mid = fetch(mid)
    w_qkv, seg_cont, moved = gather_all(first, seg_ids, tokens, chips)
    late_in, late_out, w_qkv = lax.optimization_barrier((mlp_in, mlp_out, w_qkv))
    w_ff = fetch(jnp.concatenate([late_in, late_out.T], 1))
    bias_halves = proj_bias[:2].reshape(2, 2, part).transpose(1, 0, 2)

    norm_one, sent = qkv_sent(core_at, moved, w_qkv, norm_gain, norm_bias, bias_halves)
    come = other(sent)
    kept = qkv_kept(core_at, norm_one, w_qkv, bias_halves)
    grad_come = lax.ppermute(grad_output, ("core", "tensor"), [(1, 2), (2, 1)])
    mem_come = other(memory[0])
    o_kept, o_sent, lse_self = self_fwd(core_at, kept, come, seg_cont[:, None], seg_cont[None, :])
    o_come = other(o_sent)
    kv, mem = memory_project(mine, memory[0], mem_come, w_mid, proj_bias)
    kv, o_come = lax.optimization_barrier((kv, o_come))
    resid_one, norm_two, q_cross = middle(core_at, moved, o_kept, o_come, w_mid, norm_gain, norm_bias, proj_bias)
    attn_cross, lse_cross = cross_fwd(q_cross, kv, frames, heads)
    (out, norm_three, hidden, dpre, g_two, dattn, grad_in, sum_g, sum_dpre, sum_g_two, gain_three, shift_three) = feed(
        mine, attn_cross, resid_one, grad_output, grad_come, w_mid, w_ff, norm_gain, norm_bias, proj_bias, mlp_bias[None], out_bias[None])
    output = fix(out)
    gw_ff = feed_weights(norm_three, grad_in, dpre, hidden)
    dattn, gw_ff = lax.optimization_barrier((dattn, gw_ff))
    g_ff = spread_sum(gw_ff)
    dq, dk, dv = cross_bwd(q_cross, kv, frames, dattn, attn_cross, lse_cross, heads)
    g_one, do_kept, do_sent, sum_dq, sum_g_one, gain_two, shift_two = middle_back(core_at, dq, resid_one, g_two, w_mid, norm_gain)
    do_come = other(do_sent)
    d_kept, d_sent = self_bwd(core_at, kept, come, do_kept, do_come, o_kept, o_sent, lse_self,
                              seg_cont.reshape(-1, 1, BLK), seg_cont[:, None])
    d_kept, d_sent, output = lax.optimization_barrier((d_kept, d_sent, output))
    d_come = other(d_sent)
    dq_late, d_kept = lax.optimization_barrier((dq, d_kept))
    gw_mid, sum_dv = middle_weights(core_at, g_one, o_kept, o_come, norm_two, dq_late, mem, dk, dv, g_two, attn_cross)
    early = [gain_two, gain_three, shift_two, shift_three, sum_g_one, sum_dq, sum_dv, sum_g_two, sum_dpre, sum_g]
    if rows_here % 16 == 0:
        (g_qkv, g_attn_out, g_cross_q, g_cross_k, g_cross_v, g_cross_out, sums, g_mlp_in, g_mlp_out, grad_low) = end_all(
            gw_mid, d_kept, d_come, moved, norm_one, g_one, w_qkv, norm_gain, g_ff, early, chips)
    else:
        grad_low, gain_one, shift_one = qkv_back(core_at, d_kept, d_come, moved, g_one, w_qkv, norm_gain)
        grad_low = fix(grad_low)
        gw_qkv, sum_q, sum_v = qkv_weights(core_at, norm_one, d_kept, d_come)
        g_qkv, g_attn_out, g_cross_q, g_cross_k, g_cross_v, g_cross_out, sums, g_mlp_in, g_mlp_out = sum_all(
            jnp.concatenate([gw_qkv, gw_mid], 2), g_ff,
            [gain_one, *early[:2], shift_one, *early[2:4], sum_q, sum_v, *early[4:]], chips)
    grad_tokens = grad_low.astype(F32)
    g_gain, g_shift, g_proj = sums[:3], sums[3:6], sums[6:12]
    unit_rows = sum_dpre.shape[0]
    g_units, g_out_bias = sums[12:12 + unit_rows].reshape(-1), sums[12 + unit_rows]
    return (output, grad_tokens, g_qkv.transpose(1, 0, 2), g_attn_out.T, g_cross_q,
            jnp.stack([g_cross_k, g_cross_v], 1), g_cross_out.T, g_mlp_in, g_mlp_out.T,
            g_gain, g_shift, g_proj, g_units, g_out_bias)


def solution(mesh):
    grid = Mesh(mesh.devices.reshape(-1, 2, mesh.shape["tensor"]), ("chip", "core", "tensor"))
    rows = ("chip", "core", "tensor")
    dp = ("chip", "core")
    in_specs = (P(rows, None), P(dp, None, None), P(rows), P(rows), P(rows, None), P(dp, None, "tensor"), P("tensor", dp),
                P(dp, "tensor"), P(dp, None, "tensor"), P("tensor", dp), P(dp, "tensor"), P("tensor", dp),
                P(), P(), P(), P(), P())
    out_specs = (P(rows, None), P(rows, None), P(dp, None, "tensor"), P("tensor", dp), P(dp, "tensor"), P(dp, None, "tensor"),
                 P("tensor", dp), P(dp, "tensor"), P("tensor", dp), P(), P(), P(), P(), P())
    return jax.shard_map(on_device, mesh=grid, in_specs=in_specs, out_specs=out_specs, check_vma=False)
```

```python
import functools, jax, jax.numpy as jnp
from jax import lax
from jax.experimental import pallas as pl
from jax.experimental.pallas import tpu as pltpu
from jax.sharding import Mesh
from jax.sharding import PartitionSpec as P
BLK=256
HEAD=64
LANES=128
NEG=-1e30
LOG2E=1.4426950408889634
F32=jnp.float32; BF=jnp.bfloat16

def lane_ids(rows): return lax.broadcasted_iota(jnp.int32,(rows,LANES),1)

def nt(a,b): return lax.dot_general(a,b,(((1,),(1,)),((),())),preferred_element_type=F32)
def nn(a,b): return lax.dot_general(a,b,(((1,),(0,)),((),())),preferred_element_type=F32)
def tn(a,b): return lax.dot_general(a,b,(((0,),(0,)),((),())),preferred_element_type=F32)

def pick(head, lanes): return (lanes<64) if head==0 else (lanes>=64)

def places(core, half):
    return (core * half, (1 - core) * half)


def rows_at(base, offset, count):
    return pl.ds(pl.multiple_of(base + offset, BLK), count)


def self_fwd_kernel(core_ref,kept_ref,come_ref,segq_ref,segk_ref,own_ref,sent_ref,lse_ref,q_ref,k_ref,vx_ref,o_ref):
    half=kept_ref.shape[1]; rows=2*half; n=rows//BLK
    core=core_ref[0]
    for ref,base in zip((kept_ref,come_ref),places(core,half)):
        at=rows_at(base,0,half)
        q_ref[at,:]=ref[0]
        k_ref[at,:]=ref[1]
        vx_ref[at,:LANES]=ref[2]
    vx_ref[:,LANES:]=jnp.ones((rows,LANES),BF)
    lanes=lane_ids(BLK)
    for i in range(n):
        r0=i*BLK; kn=r0+BLK
        q=q_ref[r0:kn,:]
        outs=[];lses=[]
        for h in range(2):
            qm=jnp.where(pick(h,lanes),q,jnp.zeros_like(q))
            s=nt(qm,k_ref[:kn,:])
            cut = half if i>=n//2 else r0
            a=s[:,:cut] if cut>0 else None
            b=s[:,cut:]
            w=kn-cut
            qi=lax.broadcasted_iota(jnp.int32,(BLK,w),0)+(r0-cut)
            kj=lax.broadcasted_iota(jnp.int32,(BLK,w),1)
            ok=kj<=qi
            if i>=n//2:
                ok=ok&(segk_ref[:,:kn-half]==segq_ref[r0-half:kn-half,:])
            b=jnp.where(ok,b,NEG)
            m=jnp.max(b,-1,keepdims=True)
            if a is not None: m=jnp.maximum(m,jnp.max(a,-1,keepdims=True))
            pb=jnp.exp2(b-m).astype(BF)
            ox=nn(pb,vx_ref[cut:kn,:])
            if a is not None:
                pa=jnp.exp2(a-m).astype(BF)
                ox=ox+nn(pa,vx_ref[:cut,:])
            l=ox[:,LANES:]
            outs.append(ox[:,:LANES]/l); lses.append(m+jnp.log2(l))
        sel=lanes<64
        o_ref[r0:kn,:]=jnp.where(sel,outs[0],outs[1]).astype(BF)
        lse_ref[r0:kn,:]=jnp.where(sel,lses[0],lses[1])
    for ref,base in zip((own_ref,sent_ref),places(core,half)):
        ref[...]=o_ref[rows_at(base,0,half),:]


def scalar():
    return pl.BlockSpec(memory_space=pltpu.SMEM)


def pair_cost(pairs,passes,nbytes):
    return pl.CostEstimate(flops=int(pairs*passes*64),bytes_accessed=int(nbytes)//8,transcendentals=int(pairs)//8)


def self_fwd(core,kept,come,segq,segk):
    half,part=kept.shape[1:]; rows=2*half
    three=pl.BlockSpec((3,half,LANES),lambda p:(0,0,p))
    one=pl.BlockSpec((half,LANES),lambda p:(0,p))
    n=rows//BLK
    return pl.pallas_call(self_fwd_kernel,
        grid=(part//LANES,),
        in_specs=[scalar(),three,three,pl.BlockSpec(segq.shape,lambda p:(0,0)),pl.BlockSpec(segk.shape,lambda p:(0,0))],
        out_specs=[one,one,pl.BlockSpec((rows,LANES),lambda p:(0,p))],
        out_shape=[jax.ShapeDtypeStruct((half,part),BF),jax.ShapeDtypeStruct((half,part),BF),jax.ShapeDtypeStruct((rows,part),F32)],
        scratch_shapes=[pltpu.VMEM((rows,LANES),BF),pltpu.VMEM((rows,LANES),BF),pltpu.VMEM((rows,2*LANES),BF),pltpu.VMEM((rows,LANES),BF)],
        compiler_params=pltpu.CompilerParams(vmem_limit_bytes=60*2**20),
        cost_estimate=pair_cost(n*(n+1)//2*BLK*BLK*(part//HEAD),2,12*rows*part),
        name="self_fwd",
    )(core,kept,come,segq,segk)

def cross_fwd_kernel(frames,q_ref,k_ref,v_ref,o_ref,lse_ref,kx_ref,vx_ref):
    rows=q_ref.shape[0]; n=rows//BLK; kp=k_ref.shape[0]
    tail=frames//BLK*BLK
    kx_ref[...]=k_ref[...]
    vx_ref[:,:LANES]=v_ref[...]
    vx_ref[:,LANES:]=jnp.ones((kp,LANES),BF)
    if frames<kp:
        keep=lax.broadcasted_iota(jnp.int32,(kp-tail,LANES),0)+tail<frames
        kx_ref[tail:,:]=jnp.where(keep,k_ref[tail:,:],jnp.zeros((),BF))
        vx_ref[tail:,:LANES]=jnp.where(keep,v_ref[tail:,:],jnp.zeros((),BF))
    lanes=lane_ids(BLK)
    for i in range(n):
        r0=i*BLK
        q=q_ref[r0:r0+BLK,:]
        outs=[];lses=[]
        for h in range(2):
            qm=jnp.where(pick(h,lanes),q,jnp.zeros_like(q))
            s=nt(qm,kx_ref[...])
            if frames<kp:
                kj=lax.broadcasted_iota(jnp.int32,(BLK,kp-tail),1)+tail
                s=jnp.concatenate([s[:,:tail],jnp.where(kj<frames,s[:,tail:],NEG)],axis=1)
            m=jnp.max(s,-1,keepdims=True)
            p=jnp.exp2(s-m).astype(BF)
            ox=nn(p,vx_ref[...])
            l=ox[:,LANES:]
            outs.append(ox[:,:LANES]/l); lses.append(m+jnp.log2(l))
        sel=lanes<64
        o_ref[r0:r0+BLK,:]=jnp.where(sel,outs[0],outs[1]).astype(BF)
        lse_ref[r0:r0+BLK,:]=jnp.where(sel,lses[0],lses[1])

def cross_fwd(q,kv,frames,heads):
    rows=q.shape[0]; npair=heads//2; kp=kv.shape[0]
    return pl.pallas_call(functools.partial(cross_fwd_kernel,frames),
        grid=(npair,),
        in_specs=[pl.BlockSpec((rows,LANES),lambda p:(0,p)),
                  pl.BlockSpec((kp,LANES),lambda p:(0,p)),
                  pl.BlockSpec((kp,LANES),lambda p:(0,npair+p))],
        out_specs=[pl.BlockSpec((rows,LANES),lambda p:(0,p)),pl.BlockSpec((rows,LANES),lambda p:(0,p))],
        out_shape=[jax.ShapeDtypeStruct((rows,heads*64),BF),jax.ShapeDtypeStruct((rows,heads*64),F32)],
        scratch_shapes=[pltpu.VMEM((kp,LANES),BF),pltpu.VMEM((kp,2*LANES),BF)],
        compiler_params=pltpu.CompilerParams(vmem_limit_bytes=60*2**20),
        cost_estimate=pair_cost(rows*kp*heads,2,8*rows*heads*64+4*kp*heads*64),
        name="cross_fwd",
    )(q,kv,kv)

def split3(x):
    hi=x.astype(BF); r=x-hi.astype(F32); mid=r.astype(BF); lo=(r-mid.astype(F32)).astype(BF)
    return hi,mid,lo

def aug(value,head,lanes,one_lane):
    hi,mid,lo=split3(-value)
    z=jnp.zeros(lanes.shape,F32)
    b=64*head
    x=jnp.where(lanes==b,hi.astype(F32),jnp.where(lanes==b+1,mid.astype(F32),jnp.where(lanes==b+2,lo.astype(F32),z)))
    if one_lane: x=jnp.where(lanes==b+3,1.0,x)
    return x.astype(BF)

def build_q(q,do,o,lse,at,qx_ref,dox_ref,masked):
    lanes=lane_ids(BLK)
    prod=do.astype(F32)*o.astype(F32)
    for h in range(2):
        sel=pick(h,lanes)
        delta=jnp.sum(jnp.where(sel,prod,0.0),-1,keepdims=True)
        qx_ref[h,at,:LANES]=jnp.where(sel,q,jnp.zeros((),BF))
        qx_ref[h,at,LANES:]=aug(lse,h,lanes,masked)
        dox_ref[h,at,:LANES]=jnp.where(sel,do,jnp.zeros((),BF))
        dox_ref[h,at,LANES:]=aug(delta,h,lanes,False)

def build_k(k,v,r0,at,kx_ref,km_ref,vx_ref,frames):
    lanes=lane_ids(BLK)
    low=lanes%64
    ones=jnp.where(low<3,1.0,0.0)
    kones=ones
    if frames is not None and r0+BLK>frames:
        bad=lax.broadcasted_iota(jnp.int32,(BLK,LANES),0)+r0>=frames
        k=jnp.where(bad,jnp.zeros((),BF),k); v=jnp.where(bad,jnp.zeros((),BF),v)
        kones=jnp.where(bad&(low==3),NEG,ones)
    kx_ref[at,:LANES]=k; kx_ref[at,LANES:]=kones.astype(BF)
    vx_ref[at,:LANES]=v; vx_ref[at,LANES:]=ones.astype(BF)
    for h in range(2): km_ref[h,at,:]=jnp.where(pick(h,lanes),k,jnp.zeros((),BF))

def block_back(kx,vx,km,qx,dox,mask):
    s=nt(kx,qx)
    if mask is not None:
        cut=s.shape[0]-mask.shape[0]
        low=jnp.where(mask,s[cut:],NEG)
        s=jnp.concatenate([s[:cut],low],0) if cut else low
    p=jnp.exp2(s)
    dp=nt(vx,dox)
    ds=(p*dp).astype(BF)
    pb=p.astype(BF)
    dv=nn(pb,dox[:,:LANES])
    dk=nn(ds,qx[:,:LANES])
    dq=tn(ds,km)
    return dv,dk,dq

def self_bwd_kernel(core_ref,kept_ref,come_ref,do_ref,do_come_ref,o_ref,o_sent_ref,lse_ref,segq_ref,segk_ref,own_ref,sent_ref,
                    qx_ref,dox_ref,kx_ref,km_ref,vx_ref,dqa_ref,dka_ref,dva_ref):
    half=kept_ref.shape[1]; rows=2*half; n=rows//BLK
    core=core_ref[0]
    for ref,d,o,base in zip((kept_ref,come_ref),(do_ref,do_come_ref),(o_ref,o_sent_ref),places(core,half)):
        for r0 in range(0,half,BLK):
            here=slice(r0,r0+BLK); at=rows_at(base,r0,BLK)
            build_q(ref[0,here,:],d[here,:],o[here,:],lse_ref[at,:],at,qx_ref,dox_ref,False)
            build_k(ref[1,here,:],ref[2,here,:],0,at,kx_ref,km_ref,vx_ref,None)
    dka_ref[...]=jnp.zeros_like(dka_ref)
    dva_ref[...]=jnp.zeros_like(dva_ref)
    for i in range(n):
        r0=i*BLK; kn=r0+BLK; at=slice(r0,kn)
        cut=half if i>=n//2 else r0
        w=kn-cut
        mask=lax.broadcasted_iota(jnp.int32,(w,BLK),0)<=lax.broadcasted_iota(jnp.int32,(w,BLK),1)+(r0-cut)
        if i>=n//2: mask=mask&(segk_ref[:kn-half,:]==segq_ref[i-n//2])
        r=[block_back(kx_ref[:kn,:],vx_ref[:kn,:],km_ref[h,:kn,:],qx_ref[h,at,:],dox_ref[h,at,:],mask) for h in range(2)]
        dva_ref[:kn,:]+=r[0][0]+r[1][0]
        dka_ref[:kn,:]+=r[0][1]+r[1][1]
        dqa_ref[at,:]=((r[0][2]+r[1][2])*0.125).astype(BF)
    for ref,base in zip((own_ref,sent_ref),places(core,half)):
        at=rows_at(base,0,half)
        ref[0]=dqa_ref[at,:]
        ref[1]=(dka_ref[at,:]*(1/LOG2E)).astype(BF)
        ref[2]=dva_ref[at,:].astype(BF)

def self_bwd(core,kept,come,do,do_come,o,o_sent,lse,segq,segk):
    half,part=kept.shape[1:]; rows=2*half
    three=pl.BlockSpec((3,half,LANES),lambda p:(0,0,p))
    one=pl.BlockSpec((half,LANES),lambda p:(0,p))
    out=jax.ShapeDtypeStruct((3,half,part),BF)
    n=rows//BLK
    return pl.pallas_call(self_bwd_kernel,
        grid=(part//LANES,),
        in_specs=[scalar(),three,three,one,one,one,one,pl.BlockSpec((rows,LANES),lambda p:(0,p)),
                  pl.BlockSpec(segq.shape,lambda p:(0,0,0)),pl.BlockSpec(segk.shape,lambda p:(0,0))],
        out_specs=[three,three],
        out_shape=[out,out],
        scratch_shapes=[pltpu.VMEM((2,rows,2*LANES),BF),pltpu.VMEM((2,rows,2*LANES),BF),pltpu.VMEM((rows,2*LANES),BF),
                        pltpu.VMEM((2,rows,LANES),BF),pltpu.VMEM((rows,2*LANES),BF),pltpu.VMEM((rows,LANES),BF),
                        pltpu.VMEM((rows,LANES),F32),pltpu.VMEM((rows,LANES),F32)],
        compiler_params=pltpu.CompilerParams(vmem_limit_bytes=60*2**20),
        cost_estimate=pair_cost(n*(n+1)//2*BLK*BLK*(part//HEAD),5,20*rows*part),
        name="self_bwd",
    )(core,kept,come,do,do_come,o,o_sent,lse,segq,segk)

def cross_bwd_kernel(frames,q_ref,k_ref,v_ref,do_ref,o_ref,lse_ref,dq_ref,dk_ref,dv_ref,
                     qx_ref,dox_ref,kx_ref,km_ref,vx_ref,dka_ref,dva_ref):
    rows=q_ref.shape[0]; n=rows//BLK; kp=k_ref.shape[0]; nk=kp//BLK
    for r0 in range(0,rows,BLK):
        at=slice(r0,r0+BLK)
        build_q(q_ref[at,:],do_ref[at,:],o_ref[at,:],lse_ref[at,:],at,qx_ref,dox_ref,True)
    for r0 in range(0,kp,BLK):
        at=slice(r0,r0+BLK)
        build_k(k_ref[at,:],v_ref[at,:],r0,at,kx_ref,km_ref,vx_ref,frames)
    for i in range(rows//BLK):
        at=slice(i*BLK,(i+1)*BLK)
        r=[block_back(kx_ref[...],vx_ref[...],km_ref[h],qx_ref[h,at,:],dox_ref[h,at,:],None) for h in range(2)]
        dv=r[0][0]+r[1][0]; dk=r[0][1]+r[1][1]
        if i==0: dva_ref[...]=dv; dka_ref[...]=dk
        else: dva_ref[...]+=dv; dka_ref[...]+=dk
        dq_ref[at,:]=((r[0][2]+r[1][2])*0.125).astype(BF)
    dk_ref[...]=(dka_ref[...]*(1/LOG2E)).astype(BF)
    dv_ref[...]=dva_ref[...].astype(BF)

def cross_bwd(q,kv,frames,do,o,lse,heads):
    rows=q.shape[0]; npair=heads//2; kp=kv.shape[0]
    big=lambda f:pl.BlockSpec((rows,LANES),f)
    kb=lambda f:pl.BlockSpec((kp,LANES),f)
    return pl.pallas_call(functools.partial(cross_bwd_kernel,frames),
        grid=(npair,),
        in_specs=[big(lambda p:(0,p)),kb(lambda p:(0,p)),kb(lambda p:(0,npair+p)),big(lambda p:(0,p)),big(lambda p:(0,p)),big(lambda p:(0,p))],
        out_specs=[big(lambda p:(0,p)),kb(lambda p:(0,p)),kb(lambda p:(0,p))],
        out_shape=[jax.ShapeDtypeStruct((rows,heads*64),BF),jax.ShapeDtypeStruct((kp,heads*64),BF),jax.ShapeDtypeStruct((kp,heads*64),BF)],
        scratch_shapes=[pltpu.VMEM((2,rows,2*LANES),BF),pltpu.VMEM((2,rows,2*LANES),BF),pltpu.VMEM((kp,2*LANES),BF),
                        pltpu.VMEM((2,kp,LANES),BF),pltpu.VMEM((kp,2*LANES),BF),
                        pltpu.VMEM((kp,LANES),F32),pltpu.VMEM((kp,LANES),F32)],
        compiler_params=pltpu.CompilerParams(vmem_limit_bytes=60*2**20),
        cost_estimate=pair_cost(rows*kp*heads,5,12*rows*heads*64+8*kp*heads*64),
        name="cross_bwd",
    )(q,kv,kv,do,o,lse)


EPSILON = 1e-05
ROWS = 256
CHUNK = 768
BIG = 60 * 2**20


def whole(shape):
    return pl.BlockSpec(shape, lambda *_: (0,) * len(shape), pipeline_mode=pl.Buffered(1))


def by_rows(*lead_and_cols):
    *lead, cols = lead_and_cols
    return pl.BlockSpec((*lead, ROWS, cols), lambda i: (0,) * len(lead) + (i, 0))


def shaped(shape, dtype):
    return jax.ShapeDtypeStruct(shape, dtype)


def cost(flops, nbytes, trans=0):
    return pl.CostEstimate(flops=int(flops), bytes_accessed=int(nbytes), transcendentals=int(trans))


def normalize(values):
    centre = values - jnp.mean(values, -1, keepdims=True)
    scale = lax.rsqrt(jnp.mean(centre * centre, -1, keepdims=True) + EPSILON)
    return centre * scale, scale


def norm_grad(normed, scale, gain, grad):
    weighted = grad * gain
    return scale * (weighted - jnp.mean(weighted, -1, keepdims=True)
                    - normed * jnp.mean(weighted * normed, -1, keepdims=True))


def accumulate(ref, value):
    ref[...] = value + jnp.where(pl.program_id(0) == 0, jnp.zeros_like(value), ref[...])


def column_sum(values):
    return jnp.sum(values, 0, keepdims=True)


def qkv_heads(low, w_ref, bias_ref, at, out_ref):
    part = out_ref.shape[2]
    cols = nn(low, w_ref[at])
    out_ref[0] = ((cols[:, :part] + bias_ref[at, 0:1]) * (HEAD ** -0.5 * LOG2E)).astype(BF)
    out_ref[1] = cols[:, part:2 * part].astype(BF)
    out_ref[2] = (cols[:, 2 * part:] + bias_ref[at, 1:2]).astype(BF)


def qkv_sent_kernel(core_ref, mine_ref, x_own_ref, x_come_ref, w_ref, gain_ref, shift_ref, bias_ref, norm_ref, sent_ref, x_ref):
    x = jnp.where(mine_ref[0] == 1, x_own_ref[...], x_come_ref[...])
    x_ref[...] = x
    normed, _ = normalize(x.astype(F32))
    low = (normed * gain_ref[0:1] + shift_ref[0:1]).astype(BF)
    norm_ref[...] = low
    qkv_heads(low, w_ref, bias_ref, 1 - core_ref[0], sent_ref)


def qkv_kept_kernel(core_ref, norm_ref, w_ref, bias_ref, kept_ref):
    qkv_heads(norm_ref[...], w_ref, bias_ref, core_ref[0], kept_ref)


def qkv_sent(core, mine, x_own, x_come, w, gain, shift, bias):
    rows, width = x_own.shape
    part = width // 2
    return pl.pallas_call(
        qkv_sent_kernel, grid=(rows // ROWS,),
        in_specs=[scalar(), scalar(), by_rows(width), by_rows(width), whole(w.shape), whole(gain.shape), whole(shift.shape), whole(bias.shape)],
        out_specs=[by_rows(width), by_rows(3, part), by_rows(width)],
        out_shape=[shaped((rows, width), BF), shaped((3, rows, part), BF), shaped((rows, width), BF)],
        compiler_params=pltpu.CompilerParams(vmem_limit_bytes=BIG),
        cost_estimate=cost(3 * rows * width * width, 2 * (3 * width * width + 4 * rows * width)), name="qkv_sent",
    )(core, mine, x_own, x_come, w, gain, shift, bias)


def qkv_kept(core, norm, w, bias):
    rows, width = norm.shape
    part = width // 2
    return pl.pallas_call(
        qkv_kept_kernel, grid=(rows // ROWS,),
        in_specs=[scalar(), by_rows(width), whole(w.shape), whole(bias.shape)],
        out_specs=by_rows(3, part), out_shape=shaped((3, rows, part), BF),
        compiler_params=pltpu.CompilerParams(vmem_limit_bytes=BIG),
        cost_estimate=cost(3 * rows * width * width, 2 * (3 * width * width + 3 * rows * width)), name="qkv_kept",
    )(core, norm, w, bias)


def memory_kernel(frames, mine_ref, own_ref, come_ref, w_ref, bias_ref, kv_ref, mem_ref):
    width = own_ref.shape[1]
    part = width // 2
    mem = jnp.where(mine_ref[0] == 1, own_ref[...], come_ref[...])
    row = lax.broadcasted_iota(jnp.int32, mem.shape, 0) + pl.program_id(0) * ROWS
    mem = jnp.where(row < frames, mem, jnp.zeros((), BF))
    mem_ref[...] = mem
    for t in range(2):
        cols = nn(mem, w_ref[t])
        kv_ref[:, t * part:(t + 1) * part] = cols[:, :part].astype(BF)
        kv_ref[:, width + t * part:width + (t + 1) * part] = (cols[:, part:] + bias_ref[4:5, t * part:(t + 1) * part]).astype(BF)


def memory_project(mine, own, come, w_mid, bias):
    frames, width = own.shape
    steps = pl.cdiv(frames, ROWS)
    return pl.pallas_call(
        functools.partial(memory_kernel, frames), grid=(steps,),
        in_specs=[scalar(), by_rows(width), by_rows(width),
                  pl.BlockSpec((2, width, width), lambda i: (0, 0, 1), pipeline_mode=pl.Buffered(1)), whole(bias.shape)],
        out_specs=[by_rows(2 * width), by_rows(width)],
        out_shape=[shaped((steps * ROWS, 2 * width), BF), shaped((steps * ROWS, width), BF)],
        compiler_params=pltpu.CompilerParams(vmem_limit_bytes=BIG),
        cost_estimate=cost(4 * frames * width * width, 2 * (2 * width * width + 5 * frames * width)), name="memory_project",
    )(mine, own, come, w_mid, bias)


def middle_kernel(core_ref, x_ref, own_ref, come_ref, wo_ref, wq_ref, gain_ref, shift_ref, bias_ref,
                  resid_ref, norm_ref, q_ref):
    part = own_ref.shape[1]
    core = core_ref[0]
    resid = x_ref[...].astype(F32) + nt(own_ref[...], wo_ref[core]) + nt(come_ref[...], wo_ref[1 - core]) + bias_ref[2:3]
    resid_ref[...] = resid
    normed, _ = normalize(resid)
    low = (normed * gain_ref[1:2] + shift_ref[1:2]).astype(BF)
    norm_ref[...] = low
    for t in range(2):
        at = slice(t * part, (t + 1) * part)
        q_ref[:, at] = ((nn(low, wq_ref[t]) + bias_ref[3:4, at]) * (HEAD ** -0.5 * LOG2E)).astype(BF)


def middle(core, x, own, come, w_mid, gain, shift, bias):
    rows, width = x.shape
    part = width // 2
    w_at = lambda c: pl.BlockSpec((2, width, part), lambda i: (0, 0, c), pipeline_mode=pl.Buffered(1))
    return pl.pallas_call(
        middle_kernel, grid=(rows // ROWS,),
        in_specs=[scalar(), by_rows(width), by_rows(part), by_rows(part), w_at(0), w_at(1),
                  whole(gain.shape), whole(shift.shape), whole(bias.shape)],
        out_specs=[by_rows(width)] * 3,
        out_shape=[shaped((rows, width), F32), shaped((rows, width), BF), shaped((rows, width), BF)],
        compiler_params=pltpu.CompilerParams(vmem_limit_bytes=BIG),
        cost_estimate=cost(4 * rows * width * width, 4 * width * width + 12 * rows * width), name="middle",
    )(core, x, own, come, w_mid, w_mid, gain, shift, bias)


def gelu_parts(v):
    z = jnp.abs(v) * (0.5 ** 0.5)
    t = 1.0 / (1.0 + 0.3275911 * z)
    bell = jnp.exp2(v * v * (-0.5 * LOG2E))
    poly = ((((1.061405429 * t - 1.453152027) * t + 1.421413741) * t - 0.284496736) * t + 0.254829592) * t
    tail = (0.5 * poly) * bell
    phi = jnp.where(v >= 0, 1.0 - tail, tail)
    return phi, phi + v * bell * 0.3989422804014327


def feed_kernel(mine_ref, attn_ref, resid_ref, g_own_ref, g_come_ref, wo_ref, wi_ref, wm_ref, gain_ref, shift_ref, bias_ref, unit_bias_ref, out_bias_ref,
                out_ref, norm_ref, hidden_ref, dpre_ref, g2_ref, dattn_ref, g_ref,
                sum_g_ref, sum_dpre_ref, sum_g2_ref, sum_gain_ref, sum_shift_ref):
    part = wo_ref.shape[2]
    units = wi_ref.shape[2]
    resid = resid_ref[...] + bias_ref[5:6]
    for t in range(2):
        resid = resid + nt(attn_ref[:, t * part:(t + 1) * part], wo_ref[t])
    normed, scale = normalize(resid)
    low = (normed * gain_ref[2:3] + shift_ref[2:3]).astype(BF)
    norm_ref[...] = low
    g_low = jnp.where(mine_ref[0] == 1, g_own_ref[...], g_come_ref[...])
    g_ref[...] = g_low
    out = resid + out_bias_ref[...]
    back = jnp.zeros_like(resid)
    sums = []
    spots = [(t, c) for t in range(2) for c in range(0, units, CHUNK)]

    def first(spot):
        t, c = spot
        at = slice(t * units + c, t * units + c + CHUNK)
        return nn(low, wi_ref[t, :, c:c + CHUNK]) + unit_bias_ref[:, at], nn(g_low, wm_ref[t, :, c:c + CHUNK])

    ahead = first(spots[0])
    for k, (t, c) in enumerate(spots):
        at = slice(t * units + c, t * units + c + CHUNK)
        pre, back_hidden = ahead
        if k + 1 < len(spots):
            ahead = first(spots[k + 1])
        phi, slope = gelu_parts(pre)
        hidden = (pre * phi).astype(BF)
        hidden_ref[:, at] = hidden
        out = out + nt(hidden, wm_ref[t, :, c:c + CHUNK])
        dpre = back_hidden * slope
        sums.append(column_sum(dpre))
        dpre = dpre.astype(BF)
        dpre_ref[:, at] = dpre
        back = back + nt(dpre, wi_ref[t, :, c:c + CHUNK])
    out_ref[...] = out.astype(BF)
    sums = jnp.concatenate(sums, 1)
    wide = sum_dpre_ref.shape[1]
    accumulate(sum_dpre_ref, jnp.concatenate([sums[:, i * wide:(i + 1) * wide] for i in range(sum_dpre_ref.shape[0])], 0))
    g = g_low.astype(F32)
    accumulate(sum_g_ref, column_sum(g))
    accumulate(sum_gain_ref, column_sum(back * normed))
    accumulate(sum_shift_ref, column_sum(back))
    g2 = g + norm_grad(normed, scale, gain_ref[2:3], back)
    accumulate(sum_g2_ref, column_sum(g2))
    g2_ref[...] = g2
    g2_low = g2.astype(BF)
    for t in range(2):
        dattn_ref[:, t * part:(t + 1) * part] = nn(g2_low, wo_ref[t]).astype(BF)


def feed(mine, attn, resid, g_own, g_come, w_mid, w_ff, gain, shift, bias, unit_bias, out_bias):
    rows, width = resid.shape
    part = width // 2
    units = w_ff.shape[2] // 2
    w_at = lambda cols, c: pl.BlockSpec((2, width, cols), lambda i: (0, 0, c), pipeline_mode=pl.Buffered(1))
    line = lambda count: (pl.BlockSpec((count, width), lambda i: (0, 0)), shaped((count, width), F32))
    lines = [line(1), line(2 * units // width), line(1), line(1), line(1)]
    return pl.pallas_call(
        feed_kernel, grid=(rows // ROWS,),
        in_specs=[scalar(), by_rows(width), by_rows(width), by_rows(width), by_rows(width), w_at(part, 4), w_at(units, 0), w_at(units, 1),
                  whole(gain.shape), whole(shift.shape), whole(bias.shape), whole(unit_bias.shape), whole(out_bias.shape)],
        out_specs=[by_rows(width), by_rows(width), by_rows(2 * units), by_rows(2 * units), by_rows(width), by_rows(width), by_rows(width)] + [a for a, _ in lines],
        out_shape=[shaped((rows, width), BF), shaped((rows, width), BF), shaped((rows, 2 * units), BF), shaped((rows, 2 * units), BF),
                   shaped((rows, width), F32), shaped((rows, width), BF), shaped((rows, width), BF)] + [b for _, b in lines],
        compiler_params=pltpu.CompilerParams(vmem_limit_bytes=BIG),
        cost_estimate=cost(2 * rows * width * (2 * width + 8 * units), 2 * width * (width + 4 * units) + 2 * rows * (8 * width + 4 * units), 4 * rows * units),
        name="feed",
    )(mine, attn, resid, g_own, g_come, w_mid, w_ff, w_ff, gain, shift, bias, unit_bias, out_bias)


def feed_weights_kernel(norm_ref, g_ref, dpre_ref, hidden_ref, out_ref):
    cols = dpre_ref.shape[1]
    out_ref[0, :, :cols] = tn(norm_ref[...], dpre_ref[...]).astype(BF)
    out_ref[0, :, cols:] = tn(g_ref[...], hidden_ref[...]).astype(BF)


def feed_weights(norm, g, dpre, hidden):
    rows, width = norm.shape
    units = dpre.shape[1] // 2
    cols = units // 2
    return pl.pallas_call(
        feed_weights_kernel, grid=(2, 2),
        in_specs=[whole(norm.shape), whole(g.shape), pl.BlockSpec((rows, cols), lambda t, c: (0, 2 * t + c)),
                  pl.BlockSpec((rows, cols), lambda t, c: (0, 2 * t + c))],
        out_specs=pl.BlockSpec((1, width, 2 * cols), lambda t, c: (t, 0, c)),
        out_shape=shaped((2, width, 2 * units), BF),
        compiler_params=pltpu.CompilerParams(vmem_limit_bytes=BIG),
        cost_estimate=cost(8 * rows * width * units, 2 * (4 * width * units + 4 * rows * units)), name="feed_weights",
    )(norm, g, dpre, hidden)


def middle_back_kernel(core_ref, dq_ref, resid_ref, g2_ref, wq_ref, wo_ref, gain_ref,
                       g1_ref, kept_ref, sent_ref, sum_dq_ref, sum_g1_ref, sum_gain_ref, sum_shift_ref):
    part = kept_ref.shape[1]
    core = core_ref[0]
    dq = dq_ref[...]
    back = nt(dq[:, :part], wq_ref[0]) + nt(dq[:, part:], wq_ref[1])
    accumulate(sum_dq_ref, column_sum(dq.astype(F32)))
    normed, scale = normalize(resid_ref[...])
    accumulate(sum_gain_ref, column_sum(back * normed))
    accumulate(sum_shift_ref, column_sum(back))
    g1 = g2_ref[...] + norm_grad(normed, scale, gain_ref[1:2], back)
    g1_ref[...] = g1
    accumulate(sum_g1_ref, column_sum(g1))
    low = g1.astype(BF)
    kept_ref[...] = nn(low, wo_ref[core]).astype(BF)
    sent_ref[...] = nn(low, wo_ref[1 - core]).astype(BF)


def middle_back(core, dq, resid, g2, w_mid, gain):
    rows, width = resid.shape
    part = width // 2
    w_at = lambda c: pl.BlockSpec((2, width, part), lambda i: (0, 0, c), pipeline_mode=pl.Buffered(1))
    line = pl.BlockSpec((1, width), lambda i: (0, 0))
    return pl.pallas_call(
        middle_back_kernel, grid=(rows // ROWS,),
        in_specs=[scalar(), by_rows(width), by_rows(width), by_rows(width), w_at(1), w_at(0), whole(gain.shape)],
        out_specs=[by_rows(width), by_rows(part), by_rows(part)] + [line] * 4,
        out_shape=[shaped((rows, width), F32), shaped((rows, part), BF), shaped((rows, part), BF)] + [shaped((1, width), F32)] * 4,
        compiler_params=pltpu.CompilerParams(vmem_limit_bytes=BIG),
        cost_estimate=cost(4 * rows * width * width, 4 * width * width + 18 * rows * width), name="middle_back",
    )(core, dq, resid, g2, w_mid, w_mid, gain)


def middle_weights_kernel(core_ref, g1_ref, own_ref, come_ref, norm_ref, dq_ref, mem_ref, dk_ref, dv_ref, g2_ref, attn_ref,
                          out_ref, sum_dv_ref):
    part = own_ref.shape[1]
    attn_self = jnp.where(pl.program_id(0) == core_ref[0], own_ref[...], come_ref[...])
    out_ref[0, :, :part] = tn(g1_ref[...].astype(BF), attn_self).astype(BF)
    out_ref[0, :, part:2 * part] = tn(norm_ref[...], dq_ref[...]).astype(BF)
    mem = mem_ref[...]
    out_ref[0, :, 2 * part:3 * part] = tn(mem, dk_ref[...]).astype(BF)
    out_ref[0, :, 3 * part:4 * part] = tn(mem, dv_ref[...]).astype(BF)
    out_ref[0, :, 4 * part:] = tn(g2_ref[...].astype(BF), attn_ref[...]).astype(BF)
    sum_dv_ref[...] = column_sum(dv_ref[...].astype(F32))


def middle_weights(core, g1, own, come, norm, dq, mem, dk, dv, g2, attn):
    rows, width = norm.shape
    frames = mem.shape[0]
    part = width // 2
    half = lambda n: pl.BlockSpec((n, part), lambda t: (0, t))
    return pl.pallas_call(
        middle_weights_kernel, grid=(2,),
        in_specs=[scalar(), whole(g1.shape), whole(own.shape), whole(come.shape), whole(norm.shape), half(rows), whole(mem.shape),
                  half(frames), half(frames), whole(g2.shape), half(rows)],
        out_specs=[pl.BlockSpec((1, width, 5 * part), lambda t: (t, 0, 0)), pl.BlockSpec((1, part), lambda t: (0, t))],
        out_shape=[shaped((2, width, 5 * part), BF), shaped((1, width), F32)],
        compiler_params=pltpu.CompilerParams(vmem_limit_bytes=BIG),
        cost_estimate=cost(2 * width * width * (3 * rows + 2 * frames), 10 * width * width + 2 * width * (10 * rows + 3 * frames)),
        name="middle_weights",
    )(core, g1, own, come, norm, dq, mem, dk, dv, g2, attn)


def qkv_back_kernel(core_ref, own_ref, come_ref, x_ref, g1_ref, w_ref, gain_ref, grad_ref, sum_gain_ref, sum_shift_ref):
    part = own_ref.shape[2]
    core = core_ref[0]
    back = jnp.zeros(x_ref.shape, F32)
    for ref, at in ((own_ref, core), (come_ref, 1 - core)):
        for j in range(3):
            back = back + nt(ref[j], w_ref[at, :, j * part:(j + 1) * part])
    normed, scale = normalize(x_ref[...].astype(F32))
    accumulate(sum_gain_ref, column_sum(back * normed))
    accumulate(sum_shift_ref, column_sum(back))
    grad_ref[...] = (g1_ref[...] + norm_grad(normed, scale, gain_ref[0:1], back)).astype(BF)


def qkv_back(core, own, come, x, g1, w, gain):
    rows, width = x.shape
    part = width // 2
    line = pl.BlockSpec((1, width), lambda i: (0, 0))
    return pl.pallas_call(
        qkv_back_kernel, grid=(rows // ROWS,),
        in_specs=[scalar(), by_rows(3, part), by_rows(3, part), by_rows(width), by_rows(width), whole(w.shape), whole(gain.shape)],
        out_specs=[by_rows(width), line, line],
        out_shape=[shaped((rows, width), BF), shaped((1, width), F32), shaped((1, width), F32)],
        compiler_params=pltpu.CompilerParams(vmem_limit_bytes=BIG),
        cost_estimate=cost(6 * rows * width * width, 2 * (3 * width * width + 7 * rows * width)), name="qkv_back",
    )(core, own, come, x, g1, w, gain)


def qkv_weights_kernel(core_ref, norm_ref, own_ref, come_ref, out_ref, sum_q_ref, sum_v_ref):
    part = own_ref.shape[2]
    mine = pl.program_id(0) == core_ref[0]
    norm = norm_ref[...]
    for j in range(3):
        grad = jnp.where(mine, own_ref[j], come_ref[j])
        out_ref[0, :, j * part:(j + 1) * part] = tn(norm, grad).astype(BF)
        if j != 1:
            (sum_q_ref if j == 0 else sum_v_ref)[...] = column_sum(grad.astype(F32))


def qkv_weights(core, norm, own, come):
    rows, width = norm.shape
    part = width // 2
    return pl.pallas_call(
        qkv_weights_kernel, grid=(2,),
        in_specs=[scalar(), whole(norm.shape), whole(own.shape), whole(come.shape)],
        out_specs=[pl.BlockSpec((1, width, 3 * part), lambda t: (t, 0, 0)), pl.BlockSpec((1, part), lambda t: (0, t)), pl.BlockSpec((1, part), lambda t: (0, t))],
        out_shape=[shaped((2, width, 3 * part), BF), shaped((1, width), F32), shaped((1, width), F32)],
        compiler_params=pltpu.CompilerParams(vmem_limit_bytes=BIG),
        cost_estimate=cost(6 * rows * width * width, 2 * (3 * width * width + 4 * rows * width)), name="qkv_weights",
    )(core, norm, own, come)


def bit_names(chips):
    return ["t"] + ["k%d" % b for b in reversed(range((chips - 1).bit_length()))] + ["core"]


def my_bit(name):
    if name == "t":
        return lax.axis_index("tensor")
    if name == "core":
        return lax.axis_index("core")
    return lax.axis_index("chip") // 2 ** int(name[1:]) % 2


def partner(name):
    bit = my_bit(name)
    if name == "t":
        return {"tensor": 1 - bit}
    if name == "core":
        return {"core": 1 - bit}
    return {"chip": lax.axis_index("chip") + 2 ** int(name[1:]) * (1 - 2 * bit)}


def greet(names, *others):
    barrier = pltpu.get_barrier_semaphore()
    for device in [partner(name) for name in names] + list(others):
        pl.semaphore_signal(barrier, inc=1, device_id=device, device_id_type=pl.DeviceIdType.MESH)
    pl.semaphore_wait(barrier, len(names) + len(others))


def exchange_orders(names):
    low = [n for n in reversed(names) if n[0] == "k"]
    return [["core", "t"] + low, ["core"] + low + ["t"], ["core"] + low[1:] + ["t"] + low[:1]]


def stream_cols(cols, count):
    tiles = cols // LANES
    cuts = [tiles * i // count * LANES for i in range(count + 1)]
    return [slice(a, b) for a, b in zip(cuts, cuts[1:])]


CHUNKS = 8


class Swap:
    def __init__(self, src_ref, dst_ref, send_sem, recv_sem):
        core, tensor = lax.axis_index("core"), lax.axis_index("tensor")
        cut = src_ref.shape[0] // CHUNKS
        self.differ, self.started = core != tensor, 0
        self.copies = [pltpu.make_async_remote_copy(
            src_ref.at[i * cut:(i + 1) * cut], dst_ref.at[i * cut:(i + 1) * cut], send_sem.at[i], recv_sem.at[i],
            device_id={"core": tensor, "tensor": core}, device_id_type=pl.DeviceIdType.MESH) for i in range(CHUNKS)]

    def some(self, count):
        chosen = self.copies[self.started:self.started + count]
        self.started += len(chosen)
        if chosen:
            @pl.when(self.differ)
            def _():
                for copy in chosen:
                    copy.start()

    def wait(self):
        @pl.when(self.differ)
        def _():
            for copy in self.copies:
                copy.wait()


def gather_kernel(names, orders, own_ref, seg_ref, x_ref, out_ref, seg_out_ref, moved_ref, block, segs, local_sem, send_sem, recv_sem,
                  swap_send, swap_recv):
    core, tensor = lax.axis_index("core"), lax.axis_index("tensor")
    greet(names, {"core": 1 - core, "tensor": 1 - tensor})
    spare = len(orders)
    swap = Swap(x_ref, moved_ref, swap_send, swap_recv)
    pieces, _, part = own_ref.shape
    for i in range(pieces):
        block[:, i * part:(i + 1) * part] = own_ref[i]
    lanes = stream_cols(block.shape[1], len(orders))
    place = tuple(my_bit(n) for n in names)
    known = [[] for _ in orders]
    sent = []
    flying = [None] * len(orders)

    def send(src, dst, st, step, name):
        copy = pltpu.make_async_remote_copy(src, dst, send_sem.at[st, step], recv_sem.at[st, step],
                                            device_id=partner(name), device_id_type=pl.DeviceIdType.MESH)
        copy.start()
        sent.append(copy)
        return copy

    def start(st, step):
        name = orders[st][step]
        at = tuple(slice(None) if n in known[st] else my_bit(n) for n in names)
        dst = out_ref.at[at + (slice(None), lanes[st])]
        flying[st] = send(dst if step else block.at[:, lanes[st]], dst, st, step, name)
        known[st].append(name)

    for st in range(len(orders)):
        start(st, 0)
    local = pltpu.make_async_copy(block, out_ref.at[place], local_sem.at[0])
    local.start()
    segs[core, tensor] = seg_ref[...]
    along = send(segs.at[core, tensor], segs.at[core, tensor], spare, 0, "t")
    swap.some(2)
    local.wait()
    for step in range(len(names)):
        for st in range(len(orders)):
            flying[st].wait_recv()
            if step + 1 < len(names):
                start(st, step + 1)
        swap.some(2)
        if step == 0:
            along.wait_recv()
            along = send(segs.at[core], segs.at[core], spare, 1, "core")
    along.wait_recv()
    seg_out_ref[...] = segs[tensor, 1]
    for copy in sent:
        copy.wait_send()
    swap.wait()


def gather_all(shard, seg, x, chips):
    names = bit_names(chips)
    orders = [list(reversed(o)) for o in exchange_orders(names)]
    pieces, rows, part = shard.shape
    cols = pieces * part
    dma = pltpu.SemaphoreType.DMA
    vmem = pl.BlockSpec(memory_space=pltpu.VMEM)
    seg = seg.reshape(-1, LANES)
    hbm = pl.BlockSpec(memory_space=pl.ANY)
    full, seg, moved = pl.pallas_call(
        functools.partial(gather_kernel, names, orders),
        in_specs=[vmem, vmem, hbm], out_specs=[hbm, vmem, hbm],
        out_shape=[shaped((2,) * len(names) + (rows, cols), shard.dtype), shaped(seg.shape, seg.dtype), shaped(x.shape, x.dtype)],
        scratch_shapes=[pltpu.VMEM((rows, cols), shard.dtype), pltpu.VMEM((2, 2) + seg.shape, seg.dtype),
                        dma((2,)), dma((len(orders) + 1, len(names))), dma((len(orders) + 1, len(names))),
                        dma((CHUNKS,)), dma((CHUNKS,))],
        compiler_params=pltpu.CompilerParams(collective_id=0, has_side_effects=True, vmem_limit_bytes=BIG),
        cost_estimate=cost(0, 1e6), name="gather_all",
    )(shard, seg, x)
    return full.reshape(2, -1, cols), seg.reshape(-1), moved


class Sums:
    def __init__(self, names, send_sem, recv_sem):
        self.names, self.sems, self.streams = names, (send_sem, recv_sem), []

    def add(self, sent_ref, kept_ref, order, recv, held, out):
        self.streams.append(dict(sent=sent_ref, kept=kept_ref, order=order, recv=recv, held=held, out=out, left=list(self.names),
                                 step=0, copies=[]))
        return len(self.streams) - 1

    def start(self, k):
        s = self.streams[k]
        name = s["order"][s["step"]]
        src = s["sent"] if s["kept"] is None else s["sent"].at[tuple(1 - my_bit(n) if n == name else slice(None) for n in s["left"])]
        copy = pltpu.make_async_remote_copy(src, s["recv"][s["step"]], self.sems[0].at[k, s["step"]], self.sems[1].at[k, s["step"]],
                                            device_id=partner(name), device_id_type=pl.DeviceIdType.MESH)
        copy.start()
        s["copies"].append(copy)

    def advance(self, k):
        s = self.streams[k]
        step = s["step"]
        if step == len(self.names):
            return
        s["copies"][-1].wait_recv()
        name = s["order"][step]
        if s["kept"] is None:
            total = s["sent"][...] + s["recv"][step][...]
        else:
            kept = s["kept"].at[tuple(my_bit(n) if n == name else slice(None) for n in s["left"])]
            total = kept[...].astype(F32) + s["recv"][step][...].astype(F32)
            s["left"].remove(name)
        s["step"] += 1
        if s["step"] == len(self.names):
            s["out"](total)
            return
        held = s["held"][step]
        held[...] = total.astype(held.dtype)
        if s["kept"] is not None:
            s["kept"] = held
        s["sent"] = held
        self.start(k)

    def finish(self):
        for _ in self.names:
            for k in range(len(self.streams)):
                self.advance(k)
        for s in self.streams:
            for copy in s["copies"]:
                copy.wait_send()


def part_streams(cols, part, count):
    return [slice(a.start * part, a.stop * part) for a in stream_parts(cols // part, count)]


def stream_parts(parts, count):
    cuts = [parts * i // count for i in range(count + 1)]
    return [slice(a, b) for a, b in zip(cuts, cuts[1:])]


def sum_bufs(steps, rows, lanes):
    recv = [pltpu.VMEM((2,) * (steps - 1 - i) + (rows, lane.stop - lane.start), BF) for lane in lanes for i in range(steps)]
    held = [pltpu.VMEM((2,) * (steps - 1 - i) + (rows, lane.stop - lane.start), BF) for lane in lanes for i in range(steps - 1)]
    return recv + held


def split_bufs(bufs, steps, count):
    recv, held = bufs[:count * steps], bufs[count * steps:]
    return [(recv[st * steps:(st + 1) * steps], held[st * (steps - 1):(st + 1) * (steps - 1)]) for st in range(count)]


def put_pieces(lane, part, place):
    def out(total):
        for at in range(lane.start, lane.stop, part):
            place(at // part, total[:, at - lane.start:at - lane.start + part])
    return out


def unpack_ff(ff_ref, ff_in_ref, ff_out_ref):
    quarter = ff_ref.shape[1] // 4
    for i in range(4):
        ref, at = (ff_out_ref if i % 2 else ff_in_ref), i // 2 * quarter
        ref[:, at:at + quarter] = ff_ref[:, i * quarter:(i + 1) * quarter].astype(F32)


def fill_rows(ref, values):
    row = 0
    for value in values:
        ref[row:row + value.shape[0]] = value
        row += value.shape[0]
    if row < ref.shape[0]:
        ref[row:] = jnp.zeros((ref.shape[0] - row, ref.shape[1]), F32)


def sum_kernel(names, orders, lanes, smalls, pieces, grad_ref, ff_ref, *refs):
    small_refs, refs = refs[:smalls], refs[smalls:]
    qkv_ref, *out_refs = refs[:pieces + 1]
    small_out_ref, ff_in_ref, ff_out_ref, small_first, small_recv, small_held, send_sem, recv_sem, *bufs = refs[pieces + 1:]
    greet(names)
    steps = len(names)

    def place(i, value):
        if i < 3:
            qkv_ref[i] = value
        else:
            out_refs[i - 3][...] = value

    def small_out(total):
        small_out_ref[...] = total

    sums = Sums(names, send_sem, recv_sem)
    part = qkv_ref.shape[2]
    for lane, order, (recv, held) in zip(lanes, orders, split_bufs(bufs, steps, len(lanes))):
        ref = grad_ref.at[(slice(None),) * (steps + 1) + (lane,)]
        sums.start(sums.add(ref, ref, order, recv, held, put_pieces(lane, part, place)))
    fill_rows(small_first, [ref[...] for ref in small_refs])
    sums.start(sums.add(small_first, None, orders[0], [small_recv.at[i] for i in range(steps)],
                        [small_held.at[i] for i in range(steps - 1)], small_out))
    unpack_ff(ff_ref, ff_in_ref, ff_out_ref)
    sums.finish()


def small_bufs(steps, small):
    shape = ((sum(s.shape[0] for s in small) + 7) // 8 * 8, small[-1].shape[1])
    return shape, [pltpu.VMEM(shape, F32), pltpu.VMEM((steps,) + shape, F32), pltpu.VMEM((steps,) + shape, F32)]


def sum_all(grad, ff, small, chips):
    names = bit_names(chips)
    orders = exchange_orders(names)
    cols = grad.shape[2]
    rows = grad.shape[1] // (2 * chips)
    steps = len(names)
    part = small[0].shape[1] // 2
    pieces = cols // part - 3
    lanes = part_streams(cols, part, len(orders))
    shape, extra = small_bufs(steps, small)
    dma = pltpu.SemaphoreType.DMA
    vmem = pl.BlockSpec(memory_space=pltpu.VMEM)
    return pl.pallas_call(
        functools.partial(sum_kernel, names, orders, lanes, len(small), pieces),
        in_specs=[vmem] * (2 + len(small)), out_specs=[vmem] * (pieces + 4),
        out_shape=[shaped((3, rows, part), F32)] + [shaped((rows, part), F32)] * pieces
        + [shaped(shape, F32)] + [shaped((rows, ff.shape[1] // 2), F32)] * 2,
        scratch_shapes=extra + [dma((len(orders) + 1, steps)), dma((len(orders) + 1, steps))] + sum_bufs(steps, rows, lanes),
        compiler_params=pltpu.CompilerParams(collective_id=1, has_side_effects=True, vmem_limit_bytes=BIG),
        cost_estimate=cost(0, 1e6), name="sum_all",
    )(grad.reshape((2,) * steps + (rows, cols)), ff, *small)


def end_kernel(names, orders, mid_lanes, qkv_lanes, smalls, mid_hbm, kept_hbm, come_hbm, x_hbm, norm_hbm, g1_hbm, w_hbm,
               gain_ref, ff_ref, *refs):
    small_refs, refs = refs[:smalls], refs[smalls:]
    qkv_ref, refs = refs[0], refs[1:]
    pieces = len(mid_lanes)
    parts = mid_hbm.shape[-1] // qkv_ref.shape[2]
    mid_refs, refs = refs[:parts], refs[parts:]
    (small_out_ref, ff_in_ref, ff_out_ref, moved_ref, mid, kept, come, x, norm, g1, w, grad_qkv, grad_low, small_first, small_recv,
     small_held, load_sem, send_sem, recv_sem, swap_send, swap_recv, *bufs) = refs
    core, tensor = lax.axis_index("core"), lax.axis_index("tensor")
    steps = len(names)
    part = qkv_ref.shape[2]
    loads = [pltpu.make_async_copy(src, dst, load_sem.at[i]) for i, (src, dst) in enumerate(
        ((mid_hbm, mid), (w_hbm, w), (kept_hbm, kept), (come_hbm, come), (x_hbm, x), (g1_hbm, g1), (norm_hbm, norm)))]
    for load in loads[1:] + loads[:1]:
        load.start()
    greet(names, {"core": 1 - core, "tensor": 1 - tensor})
    sums = Sums(names, send_sem, recv_sem)
    split = len(mid_lanes) * (2 * steps - 1)
    everything = (slice(None),) * (steps + 1)

    def mid_place(i, value):
        mid_refs[i][...] = value

    def qkv_place(i, value):
        qkv_ref[i] = value

    def small_out(total):
        small_out_ref[...] = total

    for lane, order, (recv, held) in zip(mid_lanes, orders, split_bufs(bufs[:split], steps, len(mid_lanes))):
        at = everything + (lane,)
        sums.start(sums.add(mid_hbm.at[at], mid.at[at], order, recv, held, put_pieces(lane, part, mid_place)))

    def step_mid():
        for k in range(pieces):
            sums.advance(k)

    for load in loads[1:6]:
        load.wait()
    rows, width = x.shape
    gains, shifts = 0.0, 0.0
    for b in range(rows // ROWS):
        at = slice(b * ROWS, (b + 1) * ROWS)
        back = jnp.zeros((ROWS, width), F32)
        for ref, t in ((kept, core), (come, 1 - core)):
            for j in range(3):
                back = back + nt(ref[j, at, :], w[t, :, j * part:(j + 1) * part])
        normed, scale = normalize(x[at, :].astype(F32))
        gains = gains + column_sum(back * normed)
        shifts = shifts + column_sum(back)
        grad_low[at, :] = (g1[at, :] + norm_grad(normed, scale, gain_ref[0:1], back)).astype(BF)
        if b == 1:
            loads[0].wait()
            step_mid()
    swap = Swap(grad_low, moved_ref, swap_send, swap_recv)
    stay = pltpu.make_async_copy(grad_low, moved_ref, load_sem.at[7])
    swap.some(CHUNKS)

    @pl.when(core == tensor)
    def _():
        stay.start()

    step_mid()
    loads[6].wait()
    bias = []
    for ref, t in ((kept, core), (come, 1 - core)):
        for j in range(3):
            grad = tn(norm[...], ref[j]).astype(BF)
            grad_qkv[(t,) + everything[1:] + (slice(j * part, (j + 1) * part),)] = grad.reshape(grad_qkv.shape[1:-1] + (part,))
            bias.append(column_sum(ref[j].astype(F32)))
        step_mid()
        swap.some(2)
    for lane, order, (recv, held) in zip(qkv_lanes, orders, split_bufs(bufs[split:], steps, len(qkv_lanes))):
        ref = grad_qkv.at[everything + (lane,)]
        sums.start(sums.add(ref, ref, order, recv, held, put_pieces(lane, part, qkv_place)))

    def line(j):
        return jnp.concatenate([jnp.where(core == 0, bias[j], bias[3 + j]), jnp.where(core == 0, bias[3 + j], bias[j])], 1)

    small = [ref[...] for ref in small_refs]
    fill_rows(small_first, [gains, *small[:2], shifts, *small[2:4], line(0), line(2), *small[4:]])
    sums.start(sums.add(small_first, None, orders[0], [small_recv.at[i] for i in range(steps)],
                        [small_held.at[i] for i in range(steps - 1)], small_out))
    unpack_ff(ff_ref, ff_in_ref, ff_out_ref)
    swap.some(CHUNKS)
    sums.finish()
    swap.wait()

    @pl.when(core == tensor)
    def _():
        stay.wait()


def end_all(mid, kept, come, x, norm, g1, w, gain, ff, small, chips):
    names = bit_names(chips)
    orders = exchange_orders(names)
    steps = len(names)
    rows, width = x.shape
    part = width // 2
    here = width // (2 * chips)
    mid_cols = mid.shape[2]
    mid_lanes = part_streams(mid_cols, part, len(orders))
    qkv_lanes = part_streams(3 * part, part, len(orders))
    pieces = mid_cols // part
    shape, extra = small_bufs(steps, small + [jnp.zeros((4, width), F32)])
    dma = pltpu.SemaphoreType.DMA
    vmem, hbm = pl.BlockSpec(memory_space=pltpu.VMEM), pl.BlockSpec(memory_space=pl.ANY)
    lead = (2,) * steps
    mid = mid.reshape(lead + (here, mid_cols))
    count = len(orders) * 2 + 2
    return pl.pallas_call(
        functools.partial(end_kernel, names, orders, mid_lanes, qkv_lanes, len(small)),
        in_specs=[hbm] * 7 + [vmem] * (2 + len(small)), out_specs=[vmem] * (pieces + 4) + [hbm],
        out_shape=[shaped((3, here, part), F32)] + [shaped((here, part), F32)] * pieces
        + [shaped(shape, F32)] + [shaped((here, ff.shape[1] // 2), F32)] * 2 + [shaped((rows, width), BF)],
        scratch_shapes=[pltpu.VMEM(v.shape, v.dtype) for v in (mid, kept, come, x, norm, g1, w)]
        + [pltpu.VMEM(lead + (here, 3 * part), BF), pltpu.VMEM((rows, width), BF)] + extra
        + [dma((8,)), dma((count, steps)), dma((count, steps)), dma((CHUNKS,)), dma((CHUNKS,))]
        + sum_bufs(steps, here, mid_lanes) + sum_bufs(steps, here, qkv_lanes),
        compiler_params=pltpu.CompilerParams(collective_id=1, has_side_effects=True, vmem_limit_bytes=BIG),
        cost_estimate=cost(0, 1e6), name="end_all",
    )(mid, kept, come, x, norm, g1, w, gain, ff, *small)


ALL = ("tensor", "chip", "core")


def fetch(shard):
    full = lax.all_gather(shard, ALL, axis=0, tiled=True)
    return full.reshape(2, -1, shard.shape[1])


def spread_sum(grad):
    return lax.psum_scatter(grad.reshape(-1, grad.shape[2]), ALL, scatter_dimension=0, tiled=True)


def on_device(tokens, memory, seg_ids, positions, grad_output, attn_in, attn_out, cross_q, cross_kv,
              cross_out, mlp_in, mlp_out, norm_gain, norm_bias, proj_bias, mlp_bias, out_bias):
    width = tokens.shape[1]
    rows_here, _, part = attn_in.shape
    units = mlp_in.shape[1]
    heads = width // HEAD
    frames = memory.shape[1]
    core = lax.axis_index("core")
    tensor = lax.axis_index("tensor")
    core_at = core.astype(jnp.int32).reshape(1)
    swap = [(0, 0), (1, 2), (2, 1), (3, 3)]
    mine = (core == tensor).astype(jnp.int32).reshape(1)
    fix = lambda x: lax.ppermute(x, ("core", "tensor"), swap)
    other = lambda x: lax.ppermute(x, "core", [(0, 1), (1, 0)])

    chips = lax.axis_size("chip")
    mid = jnp.concatenate([attn_out.T, cross_q, cross_kv.reshape(rows_here, 2 * part), cross_out.T], 1)
    first, mid = lax.optimization_barrier((attn_in.transpose(1, 0, 2), mid))
    w_mid = fetch(mid)
    w_qkv, seg_cont, x_come = gather_all(first, seg_ids, tokens, chips)
    late_in, late_out, w_qkv = lax.optimization_barrier((mlp_in, mlp_out, w_qkv))
    w_ff = fetch(jnp.concatenate([late_in, late_out.T], 1))
    bias_halves = proj_bias[:2].reshape(2, 2, part).transpose(1, 0, 2)

    norm_one, sent, moved = qkv_sent(core_at, mine, tokens, x_come, w_qkv, norm_gain, norm_bias, bias_halves)
    come = other(sent)
    kept = qkv_kept(core_at, norm_one, w_qkv, bias_halves)
    grad_come = lax.ppermute(grad_output, ("core", "tensor"), [(1, 2), (2, 1)])
    mem_come = other(memory[0])
    o_kept, o_sent, lse_self = self_fwd(core_at, kept, come, seg_cont[:, None], seg_cont[None, :])
    o_come = other(o_sent)
    kv, mem = memory_project(mine, memory[0], mem_come, w_mid, proj_bias)
    kv, o_come = lax.optimization_barrier((kv, o_come))
    resid_one, norm_two, q_cross = middle(core_at, moved, o_kept, o_come, w_mid, norm_gain, norm_bias, proj_bias)
    attn_cross, lse_cross = cross_fwd(q_cross, kv, frames, heads)
    (out, norm_three, hidden, dpre, g_two, dattn, grad_in, sum_g, sum_dpre, sum_g_two, gain_three, shift_three) = feed(
        mine, attn_cross, resid_one, grad_output, grad_come, w_mid, w_ff, norm_gain, norm_bias, proj_bias, mlp_bias[None], out_bias[None])
    output = fix(out)
    gw_ff = feed_weights(norm_three, grad_in, dpre, hidden)
    dattn, gw_ff = lax.optimization_barrier((dattn, gw_ff))
    g_ff = spread_sum(gw_ff)
    dq, dk, dv = cross_bwd(q_cross, kv, frames, dattn, attn_cross, lse_cross, heads)
    g_one, do_kept, do_sent, sum_dq, sum_g_one, gain_two, shift_two = middle_back(core_at, dq, resid_one, g_two, w_mid, norm_gain)
    do_come = other(do_sent)
    d_kept, d_sent = self_bwd(core_at, kept, come, do_kept, do_come, o_kept, o_sent, lse_self,
                              seg_cont.reshape(-1, 1, BLK), seg_cont[:, None])
    d_kept, d_sent, output = lax.optimization_barrier((d_kept, d_sent, output))
    d_come = other(d_sent)
    dq_late, d_kept = lax.optimization_barrier((dq, d_kept))
    gw_mid, sum_dv = middle_weights(core_at, g_one, o_kept, o_come, norm_two, dq_late, mem, dk, dv, g_two, attn_cross)
    early = [gain_two, gain_three, shift_two, shift_three, sum_g_one, sum_dq, sum_dv, sum_g_two, sum_dpre, sum_g]
    if rows_here % 16 == 0:
        (g_qkv, g_attn_out, g_cross_q, g_cross_k, g_cross_v, g_cross_out, sums, g_mlp_in, g_mlp_out, grad_low) = end_all(
            gw_mid, d_kept, d_come, moved, norm_one, g_one, w_qkv, norm_gain, g_ff, early, chips)
    else:
        grad_low, gain_one, shift_one = qkv_back(core_at, d_kept, d_come, moved, g_one, w_qkv, norm_gain)
        grad_low = fix(grad_low)
        gw_qkv, sum_q, sum_v = qkv_weights(core_at, norm_one, d_kept, d_come)
        g_qkv, g_attn_out, g_cross_q, g_cross_k, g_cross_v, g_cross_out, sums, g_mlp_in, g_mlp_out = sum_all(
            jnp.concatenate([gw_qkv, gw_mid], 2), g_ff,
            [gain_one, *early[:2], shift_one, *early[2:4], sum_q, sum_v, *early[4:]], chips)
    grad_tokens = grad_low.astype(F32)
    g_gain, g_shift, g_proj = sums[:3], sums[3:6], sums[6:12]
    unit_rows = sum_dpre.shape[0]
    g_units, g_out_bias = sums[12:12 + unit_rows].reshape(-1), sums[12 + unit_rows]
    return (output, grad_tokens, g_qkv.transpose(1, 0, 2), g_attn_out.T, g_cross_q,
            jnp.stack([g_cross_k, g_cross_v], 1), g_cross_out.T, g_mlp_in, g_mlp_out.T,
            g_gain, g_shift, g_proj, g_units, g_out_bias)


def solution(mesh):
    grid = Mesh(mesh.devices.reshape(-1, 2, mesh.shape["tensor"]), ("chip", "core", "tensor"))
    rows = ("chip", "core", "tensor")
    dp = ("chip", "core")
    in_specs = (P(rows, None), P(dp, None, None), P(rows), P(rows), P(rows, None), P(dp, None, "tensor"), P("tensor", dp),
                P(dp, "tensor"), P(dp, None, "tensor"), P("tensor", dp), P(dp, "tensor"), P("tensor", dp),
                P(), P(), P(), P(), P())
    out_specs = (P(rows, None), P(rows, None), P(dp, None, "tensor"), P("tensor", dp), P(dp, "tensor"), P(dp, None, "tensor"),
                 P("tensor", dp), P(dp, "tensor"), P("tensor", dp), P(), P(), P(), P(), P())
    return jax.shard_map(on_device, mesh=grid, in_specs=in_specs, out_specs=out_specs, check_vma=False)
```

```python
import functools, jax, jax.numpy as jnp
from jax import lax
from jax.experimental import pallas as pl
from jax.experimental.pallas import tpu as pltpu
from jax.sharding import Mesh
from jax.sharding import PartitionSpec as P
BLK=256
HEAD=64
LANES=128
NEG=-1e30
LOG2E=1.4426950408889634
F32=jnp.float32; BF=jnp.bfloat16

def lane_ids(rows): return lax.broadcasted_iota(jnp.int32,(rows,LANES),1)

def nt(a,b): return lax.dot_general(a,b,(((1,),(1,)),((),())),preferred_element_type=F32)
def nn(a,b): return lax.dot_general(a,b,(((1,),(0,)),((),())),preferred_element_type=F32)
def tn(a,b): return lax.dot_general(a,b,(((0,),(0,)),((),())),preferred_element_type=F32)

def pick(head, lanes): return (lanes<64) if head==0 else (lanes>=64)

def places(core, half):
    return (core * half, (1 - core) * half)


def rows_at(base, offset, count):
    return pl.ds(pl.multiple_of(base + offset, BLK), count)


def self_fwd_kernel(core_ref,kept_ref,come_ref,segq_ref,segk_ref,own_ref,sent_ref,lse_ref,q_ref,k_ref,vx_ref,o_ref):
    half=kept_ref.shape[1]; rows=2*half; n=rows//BLK
    core=core_ref[0]
    for ref,base in zip((kept_ref,come_ref),places(core,half)):
        at=rows_at(base,0,half)
        q_ref[at,:]=ref[0]
        k_ref[at,:]=ref[1]
        vx_ref[at,:LANES]=ref[2]
    vx_ref[:,LANES:]=jnp.ones((rows,LANES),BF)
    lanes=lane_ids(BLK)
    for i in range(n):
        r0=i*BLK; kn=r0+BLK
        q=q_ref[r0:kn,:]
        outs=[];lses=[]
        for h in range(2):
            qm=jnp.where(pick(h,lanes),q,jnp.zeros_like(q))
            s=nt(qm,k_ref[:kn,:])
            cut = half if i>=n//2 else r0
            a=s[:,:cut] if cut>0 else None
            b=s[:,cut:]
            w=kn-cut
            qi=lax.broadcasted_iota(jnp.int32,(BLK,w),0)+(r0-cut)
            kj=lax.broadcasted_iota(jnp.int32,(BLK,w),1)
            ok=kj<=qi
            if i>=n//2:
                ok=ok&(segk_ref[:,:kn-half]==segq_ref[r0-half:kn-half,:])
            b=jnp.where(ok,b,NEG)
            m=jnp.max(b,-1,keepdims=True)
            if a is not None: m=jnp.maximum(m,jnp.max(a,-1,keepdims=True))
            pb=jnp.exp2(b-m).astype(BF)
            ox=nn(pb,vx_ref[cut:kn,:])
            if a is not None:
                pa=jnp.exp2(a-m).astype(BF)
                ox=ox+nn(pa,vx_ref[:cut,:])
            l=ox[:,LANES:]
            outs.append(ox[:,:LANES]/l); lses.append(m+jnp.log2(l))
        sel=lanes<64
        o_ref[r0:kn,:]=jnp.where(sel,outs[0],outs[1]).astype(BF)
        lse_ref[r0:kn,:]=jnp.where(sel,lses[0],lses[1])
    for ref,base in zip((own_ref,sent_ref),places(core,half)):
        ref[...]=o_ref[rows_at(base,0,half),:]


def scalar():
    return pl.BlockSpec(memory_space=pltpu.SMEM)


def pair_cost(pairs,passes,nbytes):
    return pl.CostEstimate(flops=int(pairs*passes*64),bytes_accessed=int(nbytes)//8,transcendentals=int(pairs)//8)


def self_fwd(core,kept,come,segq,segk):
    half,part=kept.shape[1:]; rows=2*half
    three=pl.BlockSpec((3,half,LANES),lambda p:(0,0,p))
    one=pl.BlockSpec((half,LANES),lambda p:(0,p))
    n=rows//BLK
    return pl.pallas_call(self_fwd_kernel,
        grid=(part//LANES,),
        in_specs=[scalar(),three,three,pl.BlockSpec(segq.shape,lambda p:(0,0)),pl.BlockSpec(segk.shape,lambda p:(0,0))],
        out_specs=[one,one,pl.BlockSpec((rows,LANES),lambda p:(0,p))],
        out_shape=[jax.ShapeDtypeStruct((half,part),BF),jax.ShapeDtypeStruct((half,part),BF),jax.ShapeDtypeStruct((rows,part),F32)],
        scratch_shapes=[pltpu.VMEM((rows,LANES),BF),pltpu.VMEM((rows,LANES),BF),pltpu.VMEM((rows,2*LANES),BF),pltpu.VMEM((rows,LANES),BF)],
        compiler_params=pltpu.CompilerParams(vmem_limit_bytes=60*2**20),
        cost_estimate=pair_cost(n*(n+1)//2*BLK*BLK*(part//HEAD),2,12*rows*part),
        name="self_fwd",
    )(core,kept,come,segq,segk)

def cross_fwd_kernel(frames,q_ref,k_ref,v_ref,o_ref,lse_ref,kx_ref,vx_ref):
    rows=q_ref.shape[0]; n=rows//BLK; kp=k_ref.shape[0]
    tail=frames//BLK*BLK
    kx_ref[...]=k_ref[...]
    vx_ref[:,:LANES]=v_ref[...]
    vx_ref[:,LANES:]=jnp.ones((kp,LANES),BF)
    if frames<kp:
        keep=lax.broadcasted_iota(jnp.int32,(kp-tail,LANES),0)+tail<frames
        kx_ref[tail:,:]=jnp.where(keep,k_ref[tail:,:],jnp.zeros((),BF))
        vx_ref[tail:,:LANES]=jnp.where(keep,v_ref[tail:,:],jnp.zeros((),BF))
    lanes=lane_ids(BLK)
    for i in range(n):
        r0=i*BLK
        q=q_ref[r0:r0+BLK,:]
        outs=[];lses=[]
        for h in range(2):
            qm=jnp.where(pick(h,lanes),q,jnp.zeros_like(q))
            s=nt(qm,kx_ref[...])
            if frames<kp:
                kj=lax.broadcasted_iota(jnp.int32,(BLK,kp-tail),1)+tail
                s=jnp.concatenate([s[:,:tail],jnp.where(kj<frames,s[:,tail:],NEG)],axis=1)
            m=jnp.max(s,-1,keepdims=True)
            p=jnp.exp2(s-m).astype(BF)
            ox=nn(p,vx_ref[...])
            l=ox[:,LANES:]
            outs.append(ox[:,:LANES]/l); lses.append(m+jnp.log2(l))
        sel=lanes<64
        o_ref[r0:r0+BLK,:]=jnp.where(sel,outs[0],outs[1]).astype(BF)
        lse_ref[r0:r0+BLK,:]=jnp.where(sel,lses[0],lses[1])

def cross_fwd(q,kv,frames,heads):
    rows=q.shape[0]; npair=heads//2; kp=kv.shape[0]
    return pl.pallas_call(functools.partial(cross_fwd_kernel,frames),
        grid=(npair,),
        in_specs=[pl.BlockSpec((rows,LANES),lambda p:(0,p)),
                  pl.BlockSpec((kp,LANES),lambda p:(0,p)),
                  pl.BlockSpec((kp,LANES),lambda p:(0,npair+p))],
        out_specs=[pl.BlockSpec((rows,LANES),lambda p:(0,p)),pl.BlockSpec((rows,LANES),lambda p:(0,p))],
        out_shape=[jax.ShapeDtypeStruct((rows,heads*64),BF),jax.ShapeDtypeStruct((rows,heads*64),F32)],
        scratch_shapes=[pltpu.VMEM((kp,LANES),BF),pltpu.VMEM((kp,2*LANES),BF)],
        compiler_params=pltpu.CompilerParams(vmem_limit_bytes=60*2**20),
        cost_estimate=pair_cost(rows*kp*heads,2,8*rows*heads*64+4*kp*heads*64),
        name="cross_fwd",
    )(q,kv,kv)

def split3(x):
    hi=x.astype(BF); r=x-hi.astype(F32); mid=r.astype(BF); lo=(r-mid.astype(F32)).astype(BF)
    return hi,mid,lo

def aug(value,head,lanes,one_lane):
    hi,mid,lo=split3(-value)
    z=jnp.zeros(lanes.shape,F32)
    b=64*head
    x=jnp.where(lanes==b,hi.astype(F32),jnp.where(lanes==b+1,mid.astype(F32),jnp.where(lanes==b+2,lo.astype(F32),z)))
    if one_lane: x=jnp.where(lanes==b+3,1.0,x)
    return x.astype(BF)

def build_q(q,do,o,lse,at,qx_ref,dox_ref,masked):
    lanes=lane_ids(BLK)
    prod=do.astype(F32)*o.astype(F32)
    for h in range(2):
        sel=pick(h,lanes)
        delta=jnp.sum(jnp.where(sel,prod,0.0),-1,keepdims=True)
        qx_ref[h,at,:LANES]=jnp.where(sel,q,jnp.zeros((),BF))
        qx_ref[h,at,LANES:]=aug(lse,h,lanes,masked)
        dox_ref[h,at,:LANES]=jnp.where(sel,do,jnp.zeros((),BF))
        dox_ref[h,at,LANES:]=aug(delta,h,lanes,False)

def build_k(k,v,r0,at,kx_ref,km_ref,vx_ref,frames):
    lanes=lane_ids(BLK)
    low=lanes%64
    ones=jnp.where(low<3,1.0,0.0)
    kones=ones
    if frames is not None and r0+BLK>frames:
        bad=lax.broadcasted_iota(jnp.int32,(BLK,LANES),0)+r0>=frames
        k=jnp.where(bad,jnp.zeros((),BF),k); v=jnp.where(bad,jnp.zeros((),BF),v)
        kones=jnp.where(bad&(low==3),NEG,ones)
    kx_ref[at,:LANES]=k; kx_ref[at,LANES:]=kones.astype(BF)
    vx_ref[at,:LANES]=v; vx_ref[at,LANES:]=ones.astype(BF)
    for h in range(2): km_ref[h,at,:]=jnp.where(pick(h,lanes),k,jnp.zeros((),BF))

def block_back(kx,vx,km,qx,dox,mask):
    s=nt(kx,qx)
    if mask is not None:
        cut=s.shape[0]-mask.shape[0]
        low=jnp.where(mask,s[cut:],NEG)
        s=jnp.concatenate([s[:cut],low],0) if cut else low
    p=jnp.exp2(s)
    dp=nt(vx,dox)
    ds=(p*dp).astype(BF)
    pb=p.astype(BF)
    dv=nn(pb,dox[:,:LANES])
    dk=nn(ds,qx[:,:LANES])
    dq=tn(ds,km)
    return dv,dk,dq

def self_bwd_kernel(core_ref,kept_ref,come_ref,do_ref,do_come_ref,o_ref,o_sent_ref,lse_ref,segq_ref,segk_ref,own_ref,sent_ref,
                    qx_ref,dox_ref,kx_ref,km_ref,vx_ref,dqa_ref,dka_ref,dva_ref):
    half=kept_ref.shape[1]; rows=2*half; n=rows//BLK
    core=core_ref[0]
    for ref,d,o,base in zip((kept_ref,come_ref),(do_ref,do_come_ref),(o_ref,o_sent_ref),places(core,half)):
        for r0 in range(0,half,BLK):
            here=slice(r0,r0+BLK); at=rows_at(base,r0,BLK)
            build_q(ref[0,here,:],d[here,:],o[here,:],lse_ref[at,:],at,qx_ref,dox_ref,False)
            build_k(ref[1,here,:],ref[2,here,:],0,at,kx_ref,km_ref,vx_ref,None)
    dka_ref[...]=jnp.zeros_like(dka_ref)
    dva_ref[...]=jnp.zeros_like(dva_ref)
    for i in range(n):
        r0=i*BLK; kn=r0+BLK; at=slice(r0,kn)
        cut=half if i>=n//2 else r0
        w=kn-cut
        mask=lax.broadcasted_iota(jnp.int32,(w,BLK),0)<=lax.broadcasted_iota(jnp.int32,(w,BLK),1)+(r0-cut)
        if i>=n//2: mask=mask&(segk_ref[:kn-half,:]==segq_ref[i-n//2])
        r=[block_back(kx_ref[:kn,:],vx_ref[:kn,:],km_ref[h,:kn,:],qx_ref[h,at,:],dox_ref[h,at,:],mask) for h in range(2)]
        dva_ref[:kn,:]+=r[0][0]+r[1][0]
        dka_ref[:kn,:]+=r[0][1]+r[1][1]
        dqa_ref[at,:]=((r[0][2]+r[1][2])*0.125).astype(BF)
    for ref,base in zip((own_ref,sent_ref),places(core,half)):
        at=rows_at(base,0,half)
        ref[0]=dqa_ref[at,:]
        ref[1]=(dka_ref[at,:]*(1/LOG2E)).astype(BF)
        ref[2]=dva_ref[at,:].astype(BF)

def self_bwd(core,kept,come,do,do_come,o,o_sent,lse,segq,segk):
    half,part=kept.shape[1:]; rows=2*half
    three=pl.BlockSpec((3,half,LANES),lambda p:(0,0,p))
    one=pl.BlockSpec((half,LANES),lambda p:(0,p))
    out=jax.ShapeDtypeStruct((3,half,part),BF)
    n=rows//BLK
    return pl.pallas_call(self_bwd_kernel,
        grid=(part//LANES,),
        in_specs=[scalar(),three,three,one,one,one,one,pl.BlockSpec((rows,LANES),lambda p:(0,p)),
                  pl.BlockSpec(segq.shape,lambda p:(0,0,0)),pl.BlockSpec(segk.shape,lambda p:(0,0))],
        out_specs=[three,three],
        out_shape=[out,out],
        scratch_shapes=[pltpu.VMEM((2,rows,2*LANES),BF),pltpu.VMEM((2,rows,2*LANES),BF),pltpu.VMEM((rows,2*LANES),BF),
                        pltpu.VMEM((2,rows,LANES),BF),pltpu.VMEM((rows,2*LANES),BF),pltpu.VMEM((rows,LANES),BF),
                        pltpu.VMEM((rows,LANES),F32),pltpu.VMEM((rows,LANES),F32)],
        compiler_params=pltpu.CompilerParams(vmem_limit_bytes=60*2**20),
        cost_estimate=pair_cost(n*(n+1)//2*BLK*BLK*(part//HEAD),5,20*rows*part),
        name="self_bwd",
    )(core,kept,come,do,do_come,o,o_sent,lse,segq,segk)

def cross_bwd_kernel(frames,q_ref,k_ref,v_ref,do_ref,o_ref,lse_ref,dq_ref,dk_ref,dv_ref,
                     qx_ref,dox_ref,kx_ref,km_ref,vx_ref,dka_ref,dva_ref):
    rows=q_ref.shape[0]; n=rows//BLK; kp=k_ref.shape[0]; nk=kp//BLK
    for r0 in range(0,rows,BLK):
        at=slice(r0,r0+BLK)
        build_q(q_ref[at,:],do_ref[at,:],o_ref[at,:],lse_ref[at,:],at,qx_ref,dox_ref,True)
    for r0 in range(0,kp,BLK):
        at=slice(r0,r0+BLK)
        build_k(k_ref[at,:],v_ref[at,:],r0,at,kx_ref,km_ref,vx_ref,frames)
    for i in range(rows//BLK):
        at=slice(i*BLK,(i+1)*BLK)
        r=[block_back(kx_ref[...],vx_ref[...],km_ref[h],qx_ref[h,at,:],dox_ref[h,at,:],None) for h in range(2)]
        dv=r[0][0]+r[1][0]; dk=r[0][1]+r[1][1]
        if i==0: dva_ref[...]=dv; dka_ref[...]=dk
        else: dva_ref[...]+=dv; dka_ref[...]+=dk
        dq_ref[at,:]=((r[0][2]+r[1][2])*0.125).astype(BF)
    dk_ref[...]=(dka_ref[...]*(1/LOG2E)).astype(BF)
    dv_ref[...]=dva_ref[...].astype(BF)

def cross_bwd(q,kv,frames,do,o,lse,heads):
    rows=q.shape[0]; npair=heads//2; kp=kv.shape[0]
    big=lambda f:pl.BlockSpec((rows,LANES),f)
    kb=lambda f:pl.BlockSpec((kp,LANES),f)
    return pl.pallas_call(functools.partial(cross_bwd_kernel,frames),
        grid=(npair,),
        in_specs=[big(lambda p:(0,p)),kb(lambda p:(0,p)),kb(lambda p:(0,npair+p)),big(lambda p:(0,p)),big(lambda p:(0,p)),big(lambda p:(0,p))],
        out_specs=[big(lambda p:(0,p)),kb(lambda p:(0,p)),kb(lambda p:(0,p))],
        out_shape=[jax.ShapeDtypeStruct((rows,heads*64),BF),jax.ShapeDtypeStruct((kp,heads*64),BF),jax.ShapeDtypeStruct((kp,heads*64),BF)],
        scratch_shapes=[pltpu.VMEM((2,rows,2*LANES),BF),pltpu.VMEM((2,rows,2*LANES),BF),pltpu.VMEM((kp,2*LANES),BF),
                        pltpu.VMEM((2,kp,LANES),BF),pltpu.VMEM((kp,2*LANES),BF),
                        pltpu.VMEM((kp,LANES),F32),pltpu.VMEM((kp,LANES),F32)],
        compiler_params=pltpu.CompilerParams(vmem_limit_bytes=60*2**20),
        cost_estimate=pair_cost(rows*kp*heads,5,12*rows*heads*64+8*kp*heads*64),
        name="cross_bwd",
    )(q,kv,kv,do,o,lse)


EPSILON = 1e-05
ROWS = 256
BIG = 60 * 2**20


def whole(shape):
    return pl.BlockSpec(shape, lambda *_: (0,) * len(shape), pipeline_mode=pl.Buffered(1))


def by_rows(*lead_and_cols):
    *lead, cols = lead_and_cols
    return pl.BlockSpec((*lead, ROWS, cols), lambda i: (0,) * len(lead) + (i, 0))


def shaped(shape, dtype):
    return jax.ShapeDtypeStruct(shape, dtype)


def cost(flops, nbytes, trans=0):
    return pl.CostEstimate(flops=int(flops), bytes_accessed=int(nbytes), transcendentals=int(trans))


def normalize(values):
    centre = values - jnp.mean(values, -1, keepdims=True)
    scale = lax.rsqrt(jnp.mean(centre * centre, -1, keepdims=True) + EPSILON)
    return centre * scale, scale


def norm_grad(normed, scale, gain, grad):
    weighted = grad * gain
    return scale * (weighted - jnp.mean(weighted, -1, keepdims=True)
                    - normed * jnp.mean(weighted * normed, -1, keepdims=True))


def accumulate(ref, value):
    ref[...] = value + jnp.where(pl.program_id(0) == 0, jnp.zeros_like(value), ref[...])


def column_sum(values):
    return jnp.sum(values, 0, keepdims=True)


def qkv_heads(low, w_ref, bias_ref, at, out_ref):
    part = out_ref.shape[2]
    cols = nn(low, w_ref[at])
    out_ref[0] = ((cols[:, :part] + bias_ref[at, 0:1]) * (HEAD ** -0.5 * LOG2E)).astype(BF)
    out_ref[1] = cols[:, part:2 * part].astype(BF)
    out_ref[2] = (cols[:, 2 * part:] + bias_ref[at, 1:2]).astype(BF)


def qkv_sent_kernel(core_ref, mine_ref, x_own_ref, x_come_ref, w_ref, gain_ref, shift_ref, bias_ref, norm_ref, sent_ref, x_ref):
    x = jnp.where(mine_ref[0] == 1, x_own_ref[...], x_come_ref[...])
    x_ref[...] = x
    normed, _ = normalize(x.astype(F32))
    low = (normed * gain_ref[0:1] + shift_ref[0:1]).astype(BF)
    norm_ref[...] = low
    qkv_heads(low, w_ref, bias_ref, 1 - core_ref[0], sent_ref)


def qkv_kept_kernel(core_ref, norm_ref, w_ref, bias_ref, kept_ref):
    qkv_heads(norm_ref[...], w_ref, bias_ref, core_ref[0], kept_ref)


def qkv_sent(core, mine, x_own, x_come, w, gain, shift, bias):
    rows, width = x_own.shape
    part = width // 2
    return pl.pallas_call(
        qkv_sent_kernel, grid=(rows // ROWS,),
        in_specs=[scalar(), scalar(), by_rows(width), by_rows(width), whole(w.shape), whole(gain.shape), whole(shift.shape), whole(bias.shape)],
        out_specs=[by_rows(width), by_rows(3, part), by_rows(width)],
        out_shape=[shaped((rows, width), BF), shaped((3, rows, part), BF), shaped((rows, width), BF)],
        compiler_params=pltpu.CompilerParams(vmem_limit_bytes=BIG),
        cost_estimate=cost(3 * rows * width * width, 2 * (3 * width * width + 4 * rows * width)), name="qkv_sent",
    )(core, mine, x_own, x_come, w, gain, shift, bias)


def qkv_kept(core, norm, w, bias):
    rows, width = norm.shape
    part = width // 2
    return pl.pallas_call(
        qkv_kept_kernel, grid=(rows // ROWS,),
        in_specs=[scalar(), by_rows(width), whole(w.shape), whole(bias.shape)],
        out_specs=by_rows(3, part), out_shape=shaped((3, rows, part), BF),
        compiler_params=pltpu.CompilerParams(vmem_limit_bytes=BIG),
        cost_estimate=cost(3 * rows * width * width, 2 * (3 * width * width + 3 * rows * width)), name="qkv_kept",
    )(core, norm, w, bias)


def memory_kernel(frames, mine_ref, own_ref, come_ref, w_ref, bias_ref, kv_ref, mem_ref):
    width = own_ref.shape[1]
    part = width // 2
    mem = jnp.where(mine_ref[0] == 1, own_ref[...], come_ref[...])
    row = lax.broadcasted_iota(jnp.int32, mem.shape, 0) + pl.program_id(0) * ROWS
    mem = jnp.where(row < frames, mem, jnp.zeros((), BF))
    mem_ref[...] = mem
    for t in range(2):
        cols = nn(mem, w_ref[t])
        kv_ref[:, t * part:(t + 1) * part] = cols[:, :part].astype(BF)
        kv_ref[:, width + t * part:width + (t + 1) * part] = (cols[:, part:] + bias_ref[4:5, t * part:(t + 1) * part]).astype(BF)


def memory_project(mine, own, come, w_mid, bias):
    frames, width = own.shape
    steps = pl.cdiv(frames, ROWS)
    return pl.pallas_call(
        functools.partial(memory_kernel, frames), grid=(steps,),
        in_specs=[scalar(), by_rows(width), by_rows(width),
                  pl.BlockSpec((2, width, width), lambda i: (0, 0, 1), pipeline_mode=pl.Buffered(1)), whole(bias.shape)],
        out_specs=[by_rows(2 * width), by_rows(width)],
        out_shape=[shaped((steps * ROWS, 2 * width), BF), shaped((steps * ROWS, width), BF)],
        compiler_params=pltpu.CompilerParams(vmem_limit_bytes=BIG),
        cost_estimate=cost(4 * frames * width * width, 2 * (2 * width * width + 5 * frames * width)), name="memory_project",
    )(mine, own, come, w_mid, bias)


def middle_kernel(core_ref, x_ref, own_ref, come_ref, wo_ref, wq_ref, gain_ref, shift_ref, bias_ref,
                  resid_ref, norm_ref, q_ref):
    part = own_ref.shape[1]
    core = core_ref[0]
    resid = x_ref[...].astype(F32) + nt(own_ref[...], wo_ref[core]) + nt(come_ref[...], wo_ref[1 - core]) + bias_ref[2:3]
    resid_ref[...] = resid
    normed, _ = normalize(resid)
    low = (normed * gain_ref[1:2] + shift_ref[1:2]).astype(BF)
    norm_ref[...] = low
    for t in range(2):
        at = slice(t * part, (t + 1) * part)
        q_ref[:, at] = ((nn(low, wq_ref[t]) + bias_ref[3:4, at]) * (HEAD ** -0.5 * LOG2E)).astype(BF)


def middle(core, x, own, come, w_mid, gain, shift, bias):
    rows, width = x.shape
    part = width // 2
    w_at = lambda c: pl.BlockSpec((2, width, part), lambda i: (0, 0, c), pipeline_mode=pl.Buffered(1))
    return pl.pallas_call(
        middle_kernel, grid=(rows // ROWS,),
        in_specs=[scalar(), by_rows(width), by_rows(part), by_rows(part), w_at(0), w_at(1),
                  whole(gain.shape), whole(shift.shape), whole(bias.shape)],
        out_specs=[by_rows(width)] * 3,
        out_shape=[shaped((rows, width), F32), shaped((rows, width), BF), shaped((rows, width), BF)],
        compiler_params=pltpu.CompilerParams(vmem_limit_bytes=BIG),
        cost_estimate=cost(4 * rows * width * width, 4 * width * width + 12 * rows * width), name="middle",
    )(core, x, own, come, w_mid, w_mid, gain, shift, bias)


def gelu_parts(v):
    z = jnp.abs(v) * (0.5 ** 0.5)
    t = 1.0 / (1.0 + 0.3275911 * z)
    bell = jnp.exp2(v * v * (-0.5 * LOG2E))
    poly = ((((1.061405429 * t - 1.453152027) * t + 1.421413741) * t - 0.284496736) * t + 0.254829592) * t
    tail = (0.5 * poly) * bell
    phi = jnp.where(v >= 0, 1.0 - tail, tail)
    return phi, phi + v * bell * 0.3989422804014327


def feed_kernel(mine_ref, attn_ref, resid_ref, g_own_ref, g_come_ref, wo_ref, wi_ref, wm_low_ref, wm_high_ref, gain_ref, shift_ref, bias_ref, unit_bias_ref, out_bias_ref,
                out_ref, norm_ref, hidden_ref, dpre_ref, g2_ref, dattn_ref, g_ref,
                sum_g_ref, sum_dpre_ref, sum_g2_ref, sum_gain_ref, sum_shift_ref):
    part = wo_ref.shape[2]
    units = wi_ref.shape[2]
    resid = resid_ref[...] + bias_ref[5:6]
    for t in range(2):
        resid = resid + nt(attn_ref[:, t * part:(t + 1) * part], wo_ref[t])
    normed, scale = normalize(resid)
    low = (normed * gain_ref[2:3] + shift_ref[2:3]).astype(BF)
    norm_ref[...] = low
    g_low = jnp.where(mine_ref[0] == 1, g_own_ref[...], g_come_ref[...])
    g_ref[...] = g_low
    out = resid + out_bias_ref[...]
    back = jnp.zeros_like(resid)
    sums = []
    chunk = units // 2
    spots = [(t, c) for t in range(2) for c in (0, chunk)]
    wm = {0: wm_low_ref, chunk: wm_high_ref}

    def first(spot):
        t, c = spot
        at = slice(t * units + c, t * units + c + chunk)
        return nn(low, wi_ref[t, :, c:c + chunk]) + unit_bias_ref[:, at], nn(g_low, wm[c][t])

    ahead = first(spots[0])
    for k, (t, c) in enumerate(spots):
        at = slice(t * units + c, t * units + c + chunk)
        pre, back_hidden = ahead
        if k + 1 < len(spots):
            ahead = first(spots[k + 1])
        phi, slope = gelu_parts(pre)
        hidden = (pre * phi).astype(BF)
        hidden_ref[:, at] = hidden
        out = out + nt(hidden, wm[c][t])
        dpre = back_hidden * slope
        sums.append(column_sum(dpre))
        dpre = dpre.astype(BF)
        dpre_ref[:, at] = dpre
        back = back + nt(dpre, wi_ref[t, :, c:c + chunk])
    out_ref[...] = out.astype(BF)
    sums = jnp.concatenate(sums, 1)
    wide = sum_dpre_ref.shape[1]
    accumulate(sum_dpre_ref, jnp.concatenate([sums[:, i * wide:(i + 1) * wide] for i in range(sum_dpre_ref.shape[0])], 0))
    g = g_low.astype(F32)
    accumulate(sum_g_ref, column_sum(g))
    accumulate(sum_gain_ref, column_sum(back * normed))
    accumulate(sum_shift_ref, column_sum(back))
    g2 = g + norm_grad(normed, scale, gain_ref[2:3], back)
    accumulate(sum_g2_ref, column_sum(g2))
    g2_ref[...] = g2
    g2_low = g2.astype(BF)
    for t in range(2):
        dattn_ref[:, t * part:(t + 1) * part] = nn(g2_low, wo_ref[t]).astype(BF)


def feed(mine, attn, resid, g_own, g_come, w_mid, w_ff, w_high, gain, shift, bias, unit_bias, out_bias):
    rows, width = resid.shape
    part = width // 2
    units = 2 * w_high.shape[2]
    w_at = lambda cols, c: pl.BlockSpec((2, width, cols), lambda i: (0, 0, c), pipeline_mode=pl.Buffered(1))
    line = lambda count: (pl.BlockSpec((count, width), lambda i: (0, 0)), shaped((count, width), F32))
    lines = [line(1), line(2 * units // width), line(1), line(1), line(1)]
    return pl.pallas_call(
        feed_kernel, grid=(rows // ROWS,),
        in_specs=[scalar(), by_rows(width), by_rows(width), by_rows(width), by_rows(width), w_at(part, 4), w_at(units, 0), w_at(units // 2, 2), whole(w_high.shape),
                  whole(gain.shape), whole(shift.shape), whole(bias.shape), whole(unit_bias.shape), whole(out_bias.shape)],
        out_specs=[by_rows(width), by_rows(width), by_rows(2 * units), by_rows(2 * units), by_rows(width), by_rows(width), by_rows(width)] + [a for a, _ in lines],
        out_shape=[shaped((rows, width), BF), shaped((rows, width), BF), shaped((rows, 2 * units), BF), shaped((rows, 2 * units), BF),
                   shaped((rows, width), F32), shaped((rows, width), BF), shaped((rows, width), BF)] + [b for _, b in lines],
        compiler_params=pltpu.CompilerParams(vmem_limit_bytes=BIG),
        cost_estimate=cost(2 * rows * width * (2 * width + 8 * units), 2 * width * (width + 4 * units) + 2 * rows * (8 * width + 4 * units), 4 * rows * units),
        name="feed",
    )(mine, attn, resid, g_own, g_come, w_mid, w_ff, w_ff, w_high, gain, shift, bias, unit_bias, out_bias)


def feed_weights_kernel(norm_ref, g_ref, dpre_ref, hidden_ref, out_ref):
    cols = dpre_ref.shape[1]
    out_ref[0, :, :cols] = tn(norm_ref[...], dpre_ref[...]).astype(BF)
    out_ref[0, :, cols:] = tn(g_ref[...], hidden_ref[...]).astype(BF)


def feed_weights(norm, g, dpre, hidden):
    rows, width = norm.shape
    units = dpre.shape[1] // 2
    cols = units // 2
    return pl.pallas_call(
        feed_weights_kernel, grid=(2, 2),
        in_specs=[whole(norm.shape), whole(g.shape), pl.BlockSpec((rows, cols), lambda t, c: (0, 2 * t + c)),
                  pl.BlockSpec((rows, cols), lambda t, c: (0, 2 * t + c))],
        out_specs=pl.BlockSpec((1, width, 2 * cols), lambda t, c: (t, 0, c)),
        out_shape=shaped((2, width, 2 * units), BF),
        compiler_params=pltpu.CompilerParams(vmem_limit_bytes=BIG),
        cost_estimate=cost(8 * rows * width * units, 2 * (4 * width * units + 4 * rows * units)), name="feed_weights",
    )(norm, g, dpre, hidden)


def middle_back_kernel(core_ref, dq_ref, resid_ref, g2_ref, wq_ref, wo_ref, gain_ref,
                       g1_ref, kept_ref, sent_ref, sum_dq_ref, sum_g1_ref, sum_gain_ref, sum_shift_ref):
    part = kept_ref.shape[1]
    core = core_ref[0]
    dq = dq_ref[...]
    back = nt(dq[:, :part], wq_ref[0]) + nt(dq[:, part:], wq_ref[1])
    accumulate(sum_dq_ref, column_sum(dq.astype(F32)))
    normed, scale = normalize(resid_ref[...])
    accumulate(sum_gain_ref, column_sum(back * normed))
    accumulate(sum_shift_ref, column_sum(back))
    g1 = g2_ref[...] + norm_grad(normed, scale, gain_ref[1:2], back)
    g1_ref[...] = g1
    accumulate(sum_g1_ref, column_sum(g1))
    low = g1.astype(BF)
    kept_ref[...] = nn(low, wo_ref[core]).astype(BF)
    sent_ref[...] = nn(low, wo_ref[1 - core]).astype(BF)


def middle_back(core, dq, resid, g2, w_mid, gain):
    rows, width = resid.shape
    part = width // 2
    w_at = lambda c: pl.BlockSpec((2, width, part), lambda i: (0, 0, c), pipeline_mode=pl.Buffered(1))
    line = pl.BlockSpec((1, width), lambda i: (0, 0))
    return pl.pallas_call(
        middle_back_kernel, grid=(rows // ROWS,),
        in_specs=[scalar(), by_rows(width), by_rows(width), by_rows(width), w_at(1), w_at(0), whole(gain.shape)],
        out_specs=[by_rows(width), by_rows(part), by_rows(part)] + [line] * 4,
        out_shape=[shaped((rows, width), F32), shaped((rows, part), BF), shaped((rows, part), BF)] + [shaped((1, width), F32)] * 4,
        compiler_params=pltpu.CompilerParams(vmem_limit_bytes=BIG),
        cost_estimate=cost(4 * rows * width * width, 4 * width * width + 18 * rows * width), name="middle_back",
    )(core, dq, resid, g2, w_mid, w_mid, gain)


def middle_weights_kernel(core_ref, g1_ref, own_ref, come_ref, norm_ref, dq_ref, mem_ref, dk_ref, dv_ref, g2_ref, attn_ref,
                          out_ref, sum_dv_ref):
    part = own_ref.shape[1]
    attn_self = jnp.where(pl.program_id(0) == core_ref[0], own_ref[...], come_ref[...])
    out_ref[0, :, :part] = tn(g1_ref[...].astype(BF), attn_self).astype(BF)
    out_ref[0, :, part:2 * part] = tn(norm_ref[...], dq_ref[...]).astype(BF)
    mem = mem_ref[...]
    out_ref[0, :, 2 * part:3 * part] = tn(mem, dk_ref[...]).astype(BF)
    out_ref[0, :, 3 * part:4 * part] = tn(mem, dv_ref[...]).astype(BF)
    out_ref[0, :, 4 * part:] = tn(g2_ref[...].astype(BF), attn_ref[...]).astype(BF)
    sum_dv_ref[...] = column_sum(dv_ref[...].astype(F32))


def middle_weights(core, g1, own, come, norm, dq, mem, dk, dv, g2, attn):
    rows, width = norm.shape
    frames = mem.shape[0]
    part = width // 2
    half = lambda n: pl.BlockSpec((n, part), lambda t: (0, t))
    return pl.pallas_call(
        middle_weights_kernel, grid=(2,),
        in_specs=[scalar(), whole(g1.shape), whole(own.shape), whole(come.shape), whole(norm.shape), half(rows), whole(mem.shape),
                  half(frames), half(frames), whole(g2.shape), half(rows)],
        out_specs=[pl.BlockSpec((1, width, 5 * part), lambda t: (t, 0, 0)), pl.BlockSpec((1, part), lambda t: (0, t))],
        out_shape=[shaped((2, width, 5 * part), BF), shaped((1, width), F32)],
        compiler_params=pltpu.CompilerParams(vmem_limit_bytes=BIG),
        cost_estimate=cost(2 * width * width * (3 * rows + 2 * frames), 10 * width * width + 2 * width * (10 * rows + 3 * frames)),
        name="middle_weights",
    )(core, g1, own, come, norm, dq, mem, dk, dv, g2, attn)


def qkv_back_kernel(core_ref, own_ref, come_ref, x_ref, g1_ref, w_ref, gain_ref, grad_ref, sum_gain_ref, sum_shift_ref):
    part = own_ref.shape[2]
    core = core_ref[0]
    back = jnp.zeros(x_ref.shape, F32)
    for ref, at in ((own_ref, core), (come_ref, 1 - core)):
        for j in range(3):
            back = back + nt(ref[j], w_ref[at, :, j * part:(j + 1) * part])
    normed, scale = normalize(x_ref[...].astype(F32))
    accumulate(sum_gain_ref, column_sum(back * normed))
    accumulate(sum_shift_ref, column_sum(back))
    grad_ref[...] = (g1_ref[...] + norm_grad(normed, scale, gain_ref[0:1], back)).astype(BF)


def qkv_back(core, own, come, x, g1, w, gain):
    rows, width = x.shape
    part = width // 2
    line = pl.BlockSpec((1, width), lambda i: (0, 0))
    return pl.pallas_call(
        qkv_back_kernel, grid=(rows // ROWS,),
        in_specs=[scalar(), by_rows(3, part), by_rows(3, part), by_rows(width), by_rows(width), whole(w.shape), whole(gain.shape)],
        out_specs=[by_rows(width), line, line],
        out_shape=[shaped((rows, width), BF), shaped((1, width), F32), shaped((1, width), F32)],
        compiler_params=pltpu.CompilerParams(vmem_limit_bytes=BIG),
        cost_estimate=cost(6 * rows * width * width, 2 * (3 * width * width + 7 * rows * width)), name="qkv_back",
    )(core, own, come, x, g1, w, gain)


def qkv_weights_kernel(core_ref, norm_ref, own_ref, come_ref, out_ref, sum_q_ref, sum_v_ref):
    part = own_ref.shape[2]
    mine = pl.program_id(0) == core_ref[0]
    norm = norm_ref[...]
    for j in range(3):
        grad = jnp.where(mine, own_ref[j], come_ref[j])
        out_ref[0, :, j * part:(j + 1) * part] = tn(norm, grad).astype(BF)
        if j != 1:
            (sum_q_ref if j == 0 else sum_v_ref)[...] = column_sum(grad.astype(F32))


def qkv_weights(core, norm, own, come):
    rows, width = norm.shape
    part = width // 2
    return pl.pallas_call(
        qkv_weights_kernel, grid=(2,),
        in_specs=[scalar(), whole(norm.shape), whole(own.shape), whole(come.shape)],
        out_specs=[pl.BlockSpec((1, width, 3 * part), lambda t: (t, 0, 0)), pl.BlockSpec((1, part), lambda t: (0, t)), pl.BlockSpec((1, part), lambda t: (0, t))],
        out_shape=[shaped((2, width, 3 * part), BF), shaped((1, width), F32), shaped((1, width), F32)],
        compiler_params=pltpu.CompilerParams(vmem_limit_bytes=BIG),
        cost_estimate=cost(6 * rows * width * width, 2 * (3 * width * width + 4 * rows * width)), name="qkv_weights",
    )(core, norm, own, come)


def bit_names(chips):
    return ["t"] + ["k%d" % b for b in reversed(range((chips - 1).bit_length()))] + ["core"]


def my_bit(name):
    if name == "t":
        return lax.axis_index("tensor")
    if name == "core":
        return lax.axis_index("core")
    return lax.axis_index("chip") // 2 ** int(name[1:]) % 2


def partner(name):
    bit = my_bit(name)
    if name == "t":
        return {"tensor": 1 - bit}
    if name == "core":
        return {"core": 1 - bit}
    return {"chip": lax.axis_index("chip") + 2 ** int(name[1:]) * (1 - 2 * bit)}


def greet(names, *others):
    barrier = pltpu.get_barrier_semaphore()
    for device in [partner(name) for name in names] + list(others):
        pl.semaphore_signal(barrier, inc=1, device_id=device, device_id_type=pl.DeviceIdType.MESH)
    pl.semaphore_wait(barrier, len(names) + len(others))


def exchange_orders(names):
    low = [n for n in reversed(names) if n[0] == "k"]
    return [["core", "t"] + low, ["core"] + low + ["t"], ["core"] + low[1:] + ["t"] + low[:1]]


def stream_cols(cols, count):
    tiles = cols // LANES
    cuts = [tiles * i // count * LANES for i in range(count + 1)]
    return [slice(a, b) for a, b in zip(cuts, cuts[1:])]


CHUNKS = 8


class Swap:
    def __init__(self, src_ref, dst_ref, send_sem, recv_sem):
        core, tensor = lax.axis_index("core"), lax.axis_index("tensor")
        cut = src_ref.shape[0] // CHUNKS
        self.differ, self.started = core != tensor, 0
        self.copies = [pltpu.make_async_remote_copy(
            src_ref.at[i * cut:(i + 1) * cut], dst_ref.at[i * cut:(i + 1) * cut], send_sem.at[i], recv_sem.at[i],
            device_id={"core": tensor, "tensor": core}, device_id_type=pl.DeviceIdType.MESH) for i in range(CHUNKS)]

    def some(self, count):
        chosen = self.copies[self.started:self.started + count]
        self.started += len(chosen)
        if chosen:
            @pl.when(self.differ)
            def _():
                for copy in chosen:
                    copy.start()

    def wait(self):
        @pl.when(self.differ)
        def _():
            for copy in self.copies:
                copy.wait()


def gather_kernel(names, orders, own_ref, more_ref, seg_ref, x_ref, out_ref, more_out_ref, seg_out_ref, moved_ref, block, segs, local_sem, send_sem, recv_sem,
                  swap_send, swap_recv):
    core, tensor = lax.axis_index("core"), lax.axis_index("tensor")
    greet(names, {"core": 1 - core, "tensor": 1 - tensor})
    spare = 2 * len(orders)
    swap = Swap(x_ref, moved_ref, swap_send, swap_recv)
    pieces, _, part = own_ref.shape
    for i in range(pieces):
        block[:, i * part:(i + 1) * part] = own_ref[i]
    cut = more_ref.shape[1] - more_out_ref.shape[-1]
    more = more_ref.at[:, cut:]
    streams = [(order, block.at[:, lane], out_ref, lane) for order, lane in zip(orders, stream_cols(block.shape[1], len(orders)))]
    streams += [(order, more_ref.at[:, cut + lane.start:cut + lane.stop], more_out_ref, lane)
                for order, lane in zip(orders, stream_cols(more_out_ref.shape[-1], len(orders)))]
    place = tuple(my_bit(n) for n in names)
    known = [[] for _ in streams]
    sent = []
    flying = [None] * len(streams)

    def send(src, dst, st, step, name):
        copy = pltpu.make_async_remote_copy(src, dst, send_sem.at[st, step], recv_sem.at[st, step],
                                            device_id=partner(name), device_id_type=pl.DeviceIdType.MESH)
        copy.start()
        sent.append(copy)
        return copy

    def start(st, step):
        order, own, full, lane = streams[st]
        name = order[step]
        at = tuple(slice(None) if n in known[st] else my_bit(n) for n in names)
        dst = full.at[at + (slice(None), lane)]
        flying[st] = send(dst if step else own, dst, st, step, name)
        known[st].append(name)

    for st in range(len(streams)):
        start(st, 0)
    local = pltpu.make_async_copy(block, out_ref.at[place], local_sem.at[0])
    local.start()
    local_more = pltpu.make_async_copy(more, more_out_ref.at[place], local_sem.at[1])
    local_more.start()
    segs[core, tensor] = seg_ref[...]
    along = send(segs.at[core, tensor], segs.at[core, tensor], spare, 0, "t")
    swap.some(2)
    local.wait()
    local_more.wait()
    for step in range(len(names)):
        for st in range(len(streams)):
            flying[st].wait_recv()
            if step + 1 < len(names):
                start(st, step + 1)
        swap.some(2)
        if step == 0:
            along.wait_recv()
            along = send(segs.at[core], segs.at[core], spare, 1, "core")
    along.wait_recv()
    seg_out_ref[...] = segs[tensor, 1]
    for copy in sent:
        copy.wait_send()
    swap.wait()


def gather_all(shard, more, more_cols, seg, x, chips):
    names = bit_names(chips)
    orders = [list(reversed(o)) for o in exchange_orders(names)]
    pieces, rows, part = shard.shape
    cols = pieces * part
    dma = pltpu.SemaphoreType.DMA
    vmem = pl.BlockSpec(memory_space=pltpu.VMEM)
    seg = seg.reshape(-1, LANES)
    hbm = pl.BlockSpec(memory_space=pl.ANY)
    full, more, seg, moved = pl.pallas_call(
        functools.partial(gather_kernel, names, orders),
        in_specs=[vmem, vmem, vmem, hbm], out_specs=[hbm, hbm, vmem, hbm],
        out_shape=[shaped((2,) * len(names) + (rows, cols), shard.dtype),
                   shaped((2,) * len(names) + (rows, more_cols), shard.dtype), shaped(seg.shape, seg.dtype), shaped(x.shape, x.dtype)],
        scratch_shapes=[pltpu.VMEM((rows, cols), shard.dtype), pltpu.VMEM((2, 2) + seg.shape, seg.dtype),
                        dma((2,)), dma((2 * len(orders) + 1, len(names))), dma((2 * len(orders) + 1, len(names))),
                        dma((CHUNKS,)), dma((CHUNKS,))],
        compiler_params=pltpu.CompilerParams(collective_id=0, has_side_effects=True, vmem_limit_bytes=BIG),
        cost_estimate=cost(0, 1e6), name="gather_all",
    )(shard, more, seg, x)
    return full.reshape(2, -1, cols), more.reshape(2, -1, more_cols), seg.reshape(-1), moved


class Sums:
    def __init__(self, names, send_sem, recv_sem):
        self.names, self.sems, self.streams = names, (send_sem, recv_sem), []

    def add(self, sent_ref, kept_ref, order, recv, held, out):
        self.streams.append(dict(sent=sent_ref, kept=kept_ref, order=order, recv=recv, held=held, out=out, left=list(self.names),
                                 step=0, copies=[]))
        return len(self.streams) - 1

    def start(self, k):
        s = self.streams[k]
        name = s["order"][s["step"]]
        src = s["sent"] if s["kept"] is None else s["sent"].at[tuple(1 - my_bit(n) if n == name else slice(None) for n in s["left"])]
        copy = pltpu.make_async_remote_copy(src, s["recv"][s["step"]], self.sems[0].at[k, s["step"]], self.sems[1].at[k, s["step"]],
                                            device_id=partner(name), device_id_type=pl.DeviceIdType.MESH)
        copy.start()
        s["copies"].append(copy)

    def advance(self, k):
        s = self.streams[k]
        step = s["step"]
        if step == len(self.names):
            return
        s["copies"][-1].wait_recv()
        name = s["order"][step]
        if s["kept"] is None:
            total = s["sent"][...] + s["recv"][step][...]
        else:
            kept = s["kept"].at[tuple(my_bit(n) if n == name else slice(None) for n in s["left"])]
            total = kept[...].astype(F32) + s["recv"][step][...].astype(F32)
            s["left"].remove(name)
        s["step"] += 1
        if s["step"] == len(self.names):
            s["out"](total)
            return
        held = s["held"][step]
        held[...] = total.astype(held.dtype)
        if s["kept"] is not None:
            s["kept"] = held
        s["sent"] = held
        self.start(k)

    def finish(self):
        for _ in self.names:
            for k in range(len(self.streams)):
                self.advance(k)
        for s in self.streams:
            for copy in s["copies"]:
                copy.wait_send()


def part_streams(cols, part, count):
    return [slice(a.start * part, a.stop * part) for a in stream_parts(cols // part, count)]


def stream_parts(parts, count):
    cuts = [parts * i // count for i in range(count + 1)]
    return [slice(a, b) for a, b in zip(cuts, cuts[1:])]


def sum_bufs(steps, rows, lanes):
    recv = [pltpu.VMEM((2,) * (steps - 1 - i) + (rows, lane.stop - lane.start), BF) for lane in lanes for i in range(steps)]
    held = [pltpu.VMEM((2,) * (steps - 1 - i) + (rows, lane.stop - lane.start), BF) for lane in lanes for i in range(steps - 1)]
    return recv + held


def split_bufs(bufs, steps, count):
    recv, held = bufs[:count * steps], bufs[count * steps:]
    return [(recv[st * steps:(st + 1) * steps], held[st * (steps - 1):(st + 1) * (steps - 1)]) for st in range(count)]


def put_pieces(lane, part, place):
    def out(total):
        for at in range(lane.start, lane.stop, part):
            place(at // part, total[:, at - lane.start:at - lane.start + part])
    return out


def unpack_ff(ff_ref, ff_in_ref, ff_out_ref):
    quarter = ff_ref.shape[1] // 4
    for i in range(4):
        ref, at = (ff_out_ref if i % 2 else ff_in_ref), i // 2 * quarter
        ref[:, at:at + quarter] = ff_ref[:, i * quarter:(i + 1) * quarter].astype(F32)


def fill_rows(ref, values):
    row = 0
    for value in values:
        ref[row:row + value.shape[0]] = value
        row += value.shape[0]
    if row < ref.shape[0]:
        ref[row:] = jnp.zeros((ref.shape[0] - row, ref.shape[1]), F32)


def sum_kernel(names, orders, lanes, smalls, pieces, grad_ref, ff_ref, *refs):
    small_refs, refs = refs[:smalls], refs[smalls:]
    qkv_ref, *out_refs = refs[:pieces + 1]
    small_out_ref, ff_in_ref, ff_out_ref, small_first, small_recv, small_held, send_sem, recv_sem, *bufs = refs[pieces + 1:]
    greet(names)
    steps = len(names)

    def place(i, value):
        if i < 3:
            qkv_ref[i] = value
        else:
            out_refs[i - 3][...] = value

    def small_out(total):
        small_out_ref[...] = total

    sums = Sums(names, send_sem, recv_sem)
    part = qkv_ref.shape[2]
    for lane, order, (recv, held) in zip(lanes, orders, split_bufs(bufs, steps, len(lanes))):
        ref = grad_ref.at[(slice(None),) * (steps + 1) + (lane,)]
        sums.start(sums.add(ref, ref, order, recv, held, put_pieces(lane, part, place)))
    fill_rows(small_first, [ref[...] for ref in small_refs])
    sums.start(sums.add(small_first, None, orders[0], [small_recv.at[i] for i in range(steps)],
                        [small_held.at[i] for i in range(steps - 1)], small_out))
    unpack_ff(ff_ref, ff_in_ref, ff_out_ref)
    sums.finish()


def small_bufs(steps, small):
    shape = ((sum(s.shape[0] for s in small) + 7) // 8 * 8, small[-1].shape[1])
    return shape, [pltpu.VMEM(shape, F32), pltpu.VMEM((steps,) + shape, F32), pltpu.VMEM((steps,) + shape, F32)]


def sum_all(grad, ff, small, chips):
    names = bit_names(chips)
    orders = exchange_orders(names)
    cols = grad.shape[2]
    rows = grad.shape[1] // (2 * chips)
    steps = len(names)
    part = small[0].shape[1] // 2
    pieces = cols // part - 3
    lanes = part_streams(cols, part, len(orders))
    shape, extra = small_bufs(steps, small)
    dma = pltpu.SemaphoreType.DMA
    vmem = pl.BlockSpec(memory_space=pltpu.VMEM)
    return pl.pallas_call(
        functools.partial(sum_kernel, names, orders, lanes, len(small), pieces),
        in_specs=[vmem] * (2 + len(small)), out_specs=[vmem] * (pieces + 4),
        out_shape=[shaped((3, rows, part), F32)] + [shaped((rows, part), F32)] * pieces
        + [shaped(shape, F32)] + [shaped((rows, ff.shape[1] // 2), F32)] * 2,
        scratch_shapes=extra + [dma((len(orders) + 1, steps)), dma((len(orders) + 1, steps))] + sum_bufs(steps, rows, lanes),
        compiler_params=pltpu.CompilerParams(collective_id=1, has_side_effects=True, vmem_limit_bytes=BIG),
        cost_estimate=cost(0, 1e6), name="sum_all",
    )(grad.reshape((2,) * steps + (rows, cols)), ff, *small)


def end_kernel(names, orders, mid_lanes, qkv_lanes, smalls, mid_hbm, kept_hbm, come_hbm, x_hbm, norm_hbm, g1_hbm, w_hbm,
               gain_ref, ff_ref, *refs):
    small_refs, refs = refs[:smalls], refs[smalls:]
    qkv_ref, refs = refs[0], refs[1:]
    pieces = len(mid_lanes)
    parts = mid_hbm.shape[-1] // qkv_ref.shape[2]
    mid_refs, refs = refs[:parts], refs[parts:]
    (small_out_ref, ff_in_ref, ff_out_ref, moved_ref, mid, kept, come, x, norm, g1, w, grad_qkv, grad_low, small_first, small_recv,
     small_held, load_sem, send_sem, recv_sem, swap_send, swap_recv, *bufs) = refs
    core, tensor = lax.axis_index("core"), lax.axis_index("tensor")
    steps = len(names)
    part = qkv_ref.shape[2]
    loads = [pltpu.make_async_copy(src, dst, load_sem.at[i]) for i, (src, dst) in enumerate(
        ((mid_hbm, mid), (w_hbm, w), (kept_hbm, kept), (come_hbm, come), (x_hbm, x), (g1_hbm, g1), (norm_hbm, norm)))]
    for load in loads[1:] + loads[:1]:
        load.start()
    greet(names, {"core": 1 - core, "tensor": 1 - tensor})
    sums = Sums(names, send_sem, recv_sem)
    split = len(mid_lanes) * (2 * steps - 1)
    everything = (slice(None),) * (steps + 1)

    def mid_place(i, value):
        mid_refs[i][...] = value

    def qkv_place(i, value):
        qkv_ref[i] = value

    def small_out(total):
        small_out_ref[...] = total

    for lane, order, (recv, held) in zip(mid_lanes, orders, split_bufs(bufs[:split], steps, len(mid_lanes))):
        at = everything + (lane,)
        sums.start(sums.add(mid_hbm.at[at], mid.at[at], order, recv, held, put_pieces(lane, part, mid_place)))

    def step_mid():
        for k in range(pieces):
            sums.advance(k)

    for load in loads[1:6]:
        load.wait()
    rows, width = x.shape
    gains, shifts = 0.0, 0.0
    for b in range(rows // ROWS):
        at = slice(b * ROWS, (b + 1) * ROWS)
        back = jnp.zeros((ROWS, width), F32)
        for ref, t in ((kept, core), (come, 1 - core)):
            for j in range(3):
                back = back + nt(ref[j, at, :], w[t, :, j * part:(j + 1) * part])
        normed, scale = normalize(x[at, :].astype(F32))
        gains = gains + column_sum(back * normed)
        shifts = shifts + column_sum(back)
        grad_low[at, :] = (g1[at, :] + norm_grad(normed, scale, gain_ref[0:1], back)).astype(BF)
        if b == 1:
            loads[0].wait()
            step_mid()
    swap = Swap(grad_low, moved_ref, swap_send, swap_recv)
    stay = pltpu.make_async_copy(grad_low, moved_ref, load_sem.at[7])
    swap.some(CHUNKS)

    @pl.when(core == tensor)
    def _():
        stay.start()

    step_mid()
    loads[6].wait()
    bias = []
    for ref, t in ((kept, core), (come, 1 - core)):
        for j in range(3):
            grad = tn(norm[...], ref[j]).astype(BF)
            grad_qkv[(t,) + everything[1:] + (slice(j * part, (j + 1) * part),)] = grad.reshape(grad_qkv.shape[1:-1] + (part,))
            bias.append(column_sum(ref[j].astype(F32)))
        step_mid()
        swap.some(2)
    for lane, order, (recv, held) in zip(qkv_lanes, orders, split_bufs(bufs[split:], steps, len(qkv_lanes))):
        ref = grad_qkv.at[everything + (lane,)]
        sums.start(sums.add(ref, ref, order, recv, held, put_pieces(lane, part, qkv_place)))

    def line(j):
        return jnp.concatenate([jnp.where(core == 0, bias[j], bias[3 + j]), jnp.where(core == 0, bias[3 + j], bias[j])], 1)

    small = [ref[...] for ref in small_refs]
    fill_rows(small_first, [gains, *small[:2], shifts, *small[2:4], line(0), line(2), *small[4:]])
    sums.start(sums.add(small_first, None, orders[0], [small_recv.at[i] for i in range(steps)],
                        [small_held.at[i] for i in range(steps - 1)], small_out))
    unpack_ff(ff_ref, ff_in_ref, ff_out_ref)
    swap.some(CHUNKS)
    sums.finish()
    swap.wait()

    @pl.when(core == tensor)
    def _():
        stay.wait()


def end_all(mid, kept, come, x, norm, g1, w, gain, ff, small, chips):
    names = bit_names(chips)
    orders = exchange_orders(names)
    steps = len(names)
    rows, width = x.shape
    part = width // 2
    here = width // (2 * chips)
    mid_cols = mid.shape[2]
    mid_lanes = part_streams(mid_cols, part, len(orders))
    qkv_lanes = part_streams(3 * part, part, len(orders))
    pieces = mid_cols // part
    shape, extra = small_bufs(steps, small + [jnp.zeros((4, width), F32)])
    dma = pltpu.SemaphoreType.DMA
    vmem, hbm = pl.BlockSpec(memory_space=pltpu.VMEM), pl.BlockSpec(memory_space=pl.ANY)
    lead = (2,) * steps
    mid = mid.reshape(lead + (here, mid_cols))
    count = len(orders) * 2 + 2
    return pl.pallas_call(
        functools.partial(end_kernel, names, orders, mid_lanes, qkv_lanes, len(small)),
        in_specs=[hbm] * 7 + [vmem] * (2 + len(small)), out_specs=[vmem] * (pieces + 4) + [hbm],
        out_shape=[shaped((3, here, part), F32)] + [shaped((here, part), F32)] * pieces
        + [shaped(shape, F32)] + [shaped((here, ff.shape[1] // 2), F32)] * 2 + [shaped((rows, width), BF)],
        scratch_shapes=[pltpu.VMEM(v.shape, v.dtype) for v in (mid, kept, come, x, norm, g1, w)]
        + [pltpu.VMEM(lead + (here, 3 * part), BF), pltpu.VMEM((rows, width), BF)] + extra
        + [dma((8,)), dma((count, steps)), dma((count, steps)), dma((CHUNKS,)), dma((CHUNKS,))]
        + sum_bufs(steps, here, mid_lanes) + sum_bufs(steps, here, qkv_lanes),
        compiler_params=pltpu.CompilerParams(collective_id=1, has_side_effects=True, vmem_limit_bytes=BIG),
        cost_estimate=cost(0, 1e6), name="end_all",
    )(mid, kept, come, x, norm, g1, w, gain, ff, *small)


ALL = ("tensor", "chip", "core")


def fetch(shard):
    full = lax.all_gather(shard, ALL, axis=0, tiled=True)
    return full.reshape(2, -1, shard.shape[1])


def spread_sum(grad):
    return lax.psum_scatter(grad.reshape(-1, grad.shape[2]), ALL, scatter_dimension=0, tiled=True)


def on_device(tokens, memory, seg_ids, positions, grad_output, attn_in, attn_out, cross_q, cross_kv,
              cross_out, mlp_in, mlp_out, norm_gain, norm_bias, proj_bias, mlp_bias, out_bias):
    width = tokens.shape[1]
    rows_here, _, part = attn_in.shape
    units = mlp_in.shape[1]
    heads = width // HEAD
    frames = memory.shape[1]
    core = lax.axis_index("core")
    tensor = lax.axis_index("tensor")
    core_at = core.astype(jnp.int32).reshape(1)
    swap = [(0, 0), (1, 2), (2, 1), (3, 3)]
    mine = (core == tensor).astype(jnp.int32).reshape(1)
    fix = lambda x: lax.ppermute(x, ("core", "tensor"), swap)
    other = lambda x: lax.ppermute(x, "core", [(0, 1), (1, 0)])

    chips = lax.axis_size("chip")
    mid = jnp.concatenate([attn_out.T, cross_q, cross_kv.reshape(rows_here, 2 * part), cross_out.T], 1)
    first, mid = lax.optimization_barrier((attn_in.transpose(1, 0, 2), mid))
    w_mid = fetch(mid)
    w_qkv, w_high, seg_cont, x_come = gather_all(first, mlp_out.T, units // 2, seg_ids, tokens, chips)
    late_in, late_out, w_qkv = lax.optimization_barrier((mlp_in, mlp_out, w_qkv))
    w_ff = fetch(jnp.concatenate([late_in, late_out.T[:, :units // 2]], 1))
    bias_halves = proj_bias[:2].reshape(2, 2, part).transpose(1, 0, 2)

    norm_one, sent, moved = qkv_sent(core_at, mine, tokens, x_come, w_qkv, norm_gain, norm_bias, bias_halves)
    come = other(sent)
    kept = qkv_kept(core_at, norm_one, w_qkv, bias_halves)
    grad_come = lax.ppermute(grad_output, ("core", "tensor"), [(1, 2), (2, 1)])
    mem_come = other(memory[0])
    o_kept, o_sent, lse_self = self_fwd(core_at, kept, come, seg_cont[:, None], seg_cont[None, :])
    o_come = other(o_sent)
    kv, mem = memory_project(mine, memory[0], mem_come, w_mid, proj_bias)
    kv, o_come = lax.optimization_barrier((kv, o_come))
    resid_one, norm_two, q_cross = middle(core_at, moved, o_kept, o_come, w_mid, norm_gain, norm_bias, proj_bias)
    attn_cross, lse_cross = cross_fwd(q_cross, kv, frames, heads)
    (out, norm_three, hidden, dpre, g_two, dattn, grad_in, sum_g, sum_dpre, sum_g_two, gain_three, shift_three) = feed(
        mine, attn_cross, resid_one, grad_output, grad_come, w_mid, w_ff, w_high, norm_gain, norm_bias, proj_bias, mlp_bias[None], out_bias[None])
    output = fix(out)
    gw_ff = feed_weights(norm_three, grad_in, dpre, hidden)
    dattn, gw_ff = lax.optimization_barrier((dattn, gw_ff))
    g_ff = spread_sum(gw_ff)
    dq, dk, dv = cross_bwd(q_cross, kv, frames, dattn, attn_cross, lse_cross, heads)
    g_one, do_kept, do_sent, sum_dq, sum_g_one, gain_two, shift_two = middle_back(core_at, dq, resid_one, g_two, w_mid, norm_gain)
    do_come = other(do_sent)
    d_kept, d_sent = self_bwd(core_at, kept, come, do_kept, do_come, o_kept, o_sent, lse_self,
                              seg_cont.reshape(-1, 1, BLK), seg_cont[:, None])
    d_kept, d_sent, output = lax.optimization_barrier((d_kept, d_sent, output))
    d_come = other(d_sent)
    dq_late, d_kept = lax.optimization_barrier((dq, d_kept))
    gw_mid, sum_dv = middle_weights(core_at, g_one, o_kept, o_come, norm_two, dq_late, mem, dk, dv, g_two, attn_cross)
    early = [gain_two, gain_three, shift_two, shift_three, sum_g_one, sum_dq, sum_dv, sum_g_two, sum_dpre, sum_g]
    if rows_here % 16 == 0:
        (g_qkv, g_attn_out, g_cross_q, g_cross_k, g_cross_v, g_cross_out, sums, g_mlp_in, g_mlp_out, grad_low) = end_all(
            gw_mid, d_kept, d_come, moved, norm_one, g_one, w_qkv, norm_gain, g_ff, early, chips)
    else:
        grad_low, gain_one, shift_one = qkv_back(core_at, d_kept, d_come, moved, g_one, w_qkv, norm_gain)
        grad_low = fix(grad_low)
        gw_qkv, sum_q, sum_v = qkv_weights(core_at, norm_one, d_kept, d_come)
        g_qkv, g_attn_out, g_cross_q, g_cross_k, g_cross_v, g_cross_out, sums, g_mlp_in, g_mlp_out = sum_all(
            jnp.concatenate([gw_qkv, gw_mid], 2), g_ff,
            [gain_one, *early[:2], shift_one, *early[2:4], sum_q, sum_v, *early[4:]], chips)
    grad_tokens = grad_low.astype(F32)
    g_gain, g_shift, g_proj = sums[:3], sums[3:6], sums[6:12]
    unit_rows = sum_dpre.shape[0]
    g_units, g_out_bias = sums[12:12 + unit_rows].reshape(-1), sums[12 + unit_rows]
    return (output, grad_tokens, g_qkv.transpose(1, 0, 2), g_attn_out.T, g_cross_q,
            jnp.stack([g_cross_k, g_cross_v], 1), g_cross_out.T, g_mlp_in, g_mlp_out.T,
            g_gain, g_shift, g_proj, g_units, g_out_bias)


def solution(mesh):
    grid = Mesh(mesh.devices.reshape(-1, 2, mesh.shape["tensor"]), ("chip", "core", "tensor"))
    rows = ("chip", "core", "tensor")
    dp = ("chip", "core")
    in_specs = (P(rows, None), P(dp, None, None), P(rows), P(rows), P(rows, None), P(dp, None, "tensor"), P("tensor", dp),
                P(dp, "tensor"), P(dp, None, "tensor"), P("tensor", dp), P(dp, "tensor"), P("tensor", dp),
                P(), P(), P(), P(), P())
    out_specs = (P(rows, None), P(rows, None), P(dp, None, "tensor"), P("tensor", dp), P(dp, "tensor"), P(dp, None, "tensor"),
                 P("tensor", dp), P(dp, "tensor"), P("tensor", dp), P(), P(), P(), P(), P())
    return jax.shard_map(on_device, mesh=grid, in_specs=in_specs, out_specs=out_specs, check_vma=False)
```
